32 devices in a mesh: dp: 8 (over z, x), tensor: 4 (over y, core).
Axes of the slice: x: 2, y: 2, z: 4, core: 2. Of those that a mesh axis runs over, the one named last changes fastest.
Arguments:
- tokens: bfloat16 [16, 1024, 768], P('dp', 'tensor'), may hold values from -6 to 6
- clip_lengths: int32 [16, 6], P('dp'), may hold values from 100 to 170, as said below
- cotangent: bfloat16 [16, 1024, 768], P('dp', 'tensor'), may hold values from -6 to 6
- query_key_value_weight: bfloat16 [768, 2304], P(None, 'tensor'), may hold values from -0.21875 to 0.21875
- qv_bias: float32 [1536], P('tensor'), may hold values from -0.6 to 0.6
- output_weight: bfloat16 [768, 768], P('tensor'), may hold values from -3 to 3
- out_bias: float32 [768], replicated, may hold values from -1.5 to 1.5
- gain1: float32 [768], replicated, may hold values from 0.5 to 1.5
- shift1: float32 [768], replicated, may hold values from -1.5 to 1.5
- gain2: float32 [768], replicated, may hold values from 0.5 to 1.5
- shift2: float32 [768], replicated, may hold values from -1.5 to 1.5
- up_weight: bfloat16 [768, 3072], P(None, 'tensor'), may hold values from -0.21875 to 0.21875
- hidden_bias: float32 [3072], P('tensor'), may hold values from -2.5 to 2.5
- down_weight: bfloat16 [3072, 768], P('tensor'), may hold values from -0.109375 to 0.109375
- down_bias: float32 [768], replicated, may hold values from -1.5 to 1.5
Outputs:
- block_out: bfloat16 [16, 1024, 768], P('dp', 'tensor')
- input_grad: bfloat16 [16, 1024, 768], P('dp', 'tensor')
- grad_qkv: float32 [768, 2304], P(None, 'tensor')
- grad_qv_bias: float32 [1536], P('tensor')
- grad_out: float32 [768, 768], P('tensor')
- grad_out_bias: float32 [768], replicated
- grad_gain1: float32 [768], replicated
- grad_shift1: float32 [768], replicated
- grad_gain2: float32 [768], replicated
- grad_shift2: float32 [768], replicated
- grad_up: float32 [768, 3072], P(None, 'tensor')
- grad_up_bias: float32 [3072], P('tensor')
- grad_down: float32 [3072, 768], P('tensor')
- grad_down_bias: float32 [768], replicated
The draws below stay inside these ranges and needn't reach their ends.
Inputs may be any that keep to these rules, and one draw needn't show every extreme that they name: `clip_lengths`: clips stand one after another from the first row of a sequence; the rows after the 6 clips are padding.
All inputs are finite; a program needn't handle non-finite values.
Results may differ from the reference program's by a relative error of at most 0.018.
Values may be sent and summed in bfloat16 or wider, within the bound.
No kernel may reach another device: no remote copies, remote signals or barrier semaphores. Data moves between devices by JAX's collectives and lax.ppermute only.
A program may use at most 128 MiB of HBM per device.

```python
from functools import partial
import jax
import jax.numpy as jnp
from jax import lax

D = 768
HEADS = 12
HEAD_DIM = 64
FF = 3072
L = 1024
CLIPS = 6
SEQS = 16
CLIP_LO = 100
CLIP_HI = 170


def draw_clip_lengths(key, part):
    clip_draw = jax.random.randint(key, (SEQS, CLIPS), CLIP_LO, CLIP_HI + 1)
    clip_draw = clip_draw.at[0, 0].set(CLIP_HI).at[0, 1].set(CLIP_LO)
    return clip_draw.astype(jnp.int32)


def level_of(stream_key, dims, cuts, low, largest):
    factor_of, own = 1.0, jax.random.fold_in(stream_key, 6)
    for axis_at, parts in cuts:
        heights = jnp.exp(jax.random.uniform(jax.random.fold_in(own, axis_at), (parts,), jnp.float32, low / len(cuts), largest / len(cuts)))
        factor_of = factor_of * jnp.repeat(heights, dims[axis_at] // parts).reshape([-1 if axis == axis_at else 1 for axis in range(len(dims))])
    return factor_of


def normal_values(key, dims, scale, reach, cuts=(), kind=jnp.bfloat16):
    loudness = level_of(key, dims, cuts, -0.22, 0.18) if cuts else 1.0
    values = jax.random.normal(key, dims, jnp.float32) * scale * loudness
    return jnp.minimum(jnp.maximum(values, -reach), reach).astype(kind)


def setup_inputs(seed: int = 0) -> dict:
    splits = jax.random.split(jax.random.key(seed), 16)
    return {
        "tokens": normal_values(splits[0], (SEQS, L, D), 1.0, 6.0, ((0, 8), (1, 4))),
        "clip_lengths": draw_clip_lengths(jax.random.fold_in(splits[15], 71), 0),
        "cotangent": normal_values(splits[2], (SEQS, L, D), 1.0, 6.0, ((0, 8), (1, 4))),
        "query_key_value_weight": normal_values(splits[3], (D, HEADS * 3 * HEAD_DIM), D ** -0.5, 0.21875, ((1, 4),)),
        "qv_bias": normal_values(splits[4], (HEADS * 2 * HEAD_DIM,), 0.1, 0.6, ((0, 4),), jnp.float32),
        "output_weight": normal_values(splits[5], (HEADS * HEAD_DIM, D), (max(1, D // 160)) ** -0.5, 3.0, ((0, 4),)),
        "out_bias": normal_values(splits[6], (D,), 0.3, 1.5, (), jnp.float32),
        "gain1": jnp.clip(1.0 + 0.1 * jax.random.normal(splits[7], (D,), jnp.float32), 0.5, 1.5),
        "shift1": normal_values(splits[8], (D,), 0.3, 1.5, (), jnp.float32),
        "gain2": jnp.clip(1.0 + 0.1 * jax.random.normal(splits[9], (D,), jnp.float32), 0.5, 1.5),
        "shift2": normal_values(splits[10], (D,), 0.3, 1.5, (), jnp.float32),
        "up_weight": normal_values(splits[11], (D, FF), D ** -0.5, 0.21875, ((1, 4),)),
        "hidden_bias": normal_values(splits[12], (FF,), 0.5, 2.5, ((0, 4),), jnp.float32),
        "down_weight": normal_values(splits[13], (FF, D), FF ** -0.5, 0.109375, ((0, 4),)),
        "down_bias": normal_values(splits[14], (D,), 0.3, 1.5, (), jnp.float32),
    }


EPS = 1e-06

@jax.custom_vjp
def low(v):
    return lax.optimization_barrier(v.astype(jnp.bfloat16)).astype(jnp.float32)

@jax.custom_vjp
def low_back(v):
    return v

def low_keep(v):
    return (low(v), None)

def low_pass(kept, grad):
    return (grad,)

def back_keep(v):
    return (v, None)

def back_low(kept, grad):
    return (low(grad),)
low.defvjp(low_keep, low_pass)
low_back.defvjp(back_keep, back_low)

def layer_norm(values, gain_vec, shift_vec):
    average = lax.optimization_barrier(jnp.mean(values, axis=-1, keepdims=True))
    centred = values - average
    variance = lax.optimization_barrier(jnp.mean(centred * centred, axis=-1, keepdims=True))
    return centred * lax.rsqrt(variance + EPS) * gain_vec + shift_vec

def matmul(left, right):
    return jnp.dot(left, right, precision=lax.Precision.HIGHEST)

def segment_ids(lengths):
    clip_ends = jnp.cumsum(lengths).astype(jnp.int32)
    places = jnp.arange(L, dtype=jnp.int32)
    return lax.optimization_barrier(jnp.sum((places[:, None] >= clip_ends[None, :]).astype(jnp.int32), axis=1))

def sequence_attention(packed):
    projected, lengths = packed
    split_qkv = projected.reshape(L, HEADS, 3, HEAD_DIM)
    query_rows = split_qkv[:, :, 0]
    key_rows = split_qkv[:, :, 1]
    value_rows = split_qkv[:, :, 2]
    scores = jnp.einsum('qhd,khd->hqk', query_rows, key_rows, precision=lax.Precision.HIGHEST) * HEAD_DIM ** (-0.5)
    scores = low_back(scores)
    segment = segment_ids(lengths)
    allowed = segment[:, None] == segment[None, :]
    scores = jnp.where(allowed[None], scores, -1e+30)
    softmax_rows = low(jax.nn.softmax(scores, axis=-1))
    mixture = jnp.einsum('hqk,khd->qhd', softmax_rows, value_rows, precision=lax.Precision.HIGHEST)
    return mixture.reshape(L, HEADS * HEAD_DIM)

def forward(lengths, tokens, query_key_value_weight, qv_bias, output_weight, out_bias, gain1, shift1, gain2, shift2, up_weight, hidden_bias, down_weight, down_bias):
    token_rows = tokens.reshape(SEQS * L, D)
    normed = low(layer_norm(token_rows, gain1, shift1))
    bias_pairs = qv_bias.reshape(HEADS, 2, HEAD_DIM)
    bias_complete = jnp.stack([bias_pairs[:, 0], jnp.zeros_like(bias_pairs[:, 0]), bias_pairs[:, 1]], axis=1).reshape(HEADS * 3 * HEAD_DIM)
    projected = low_back(low(matmul(normed, query_key_value_weight) + bias_complete))
    attention_result = lax.map(jax.checkpoint(sequence_attention), (projected.reshape(SEQS, L, HEADS * 3 * HEAD_DIM), lengths))
    attention_result = low_back(low(attention_result.reshape(SEQS * L, HEADS * HEAD_DIM)))
    attention_out = low_back(matmul(attention_result, output_weight) + out_bias)
    middle = token_rows + attention_out
    normed2 = low(layer_norm(middle, gain2, shift2))
    upward = low_back(matmul(normed2, up_weight) + hidden_bias)
    active = low(jax.nn.gelu(upward, approximate=False))
    branch = low_back(matmul(active, down_weight) + down_bias)
    return (middle + branch).reshape(SEQS, L, D)

def reference(tokens, clip_lengths, cotangent, query_key_value_weight, qv_bias, output_weight, out_bias, gain1, shift1, gain2, shift2, up_weight, hidden_bias, down_weight, down_bias):
    floats = [item.astype(jnp.float32) for item in (tokens, query_key_value_weight, qv_bias, output_weight, out_bias, gain1, shift1, gain2, shift2, up_weight, hidden_bias, down_weight, down_bias)]
    result, pullback = jax.vjp(partial(forward, clip_lengths), *floats)
    gradients = pullback(cotangent.astype(jnp.float32))
    return (result.astype(jnp.bfloat16), gradients[0].astype(jnp.bfloat16), gradients[1], gradients[2], gradients[3], gradients[4], gradients[5], gradients[6], gradients[7], gradients[8], gradients[9], gradients[10], gradients[11], gradients[12])
```

```python
import functools

import jax
import jax.numpy as jnp
from jax import lax
from jax.experimental import pallas as pl
from jax.experimental.pallas import tpu as pltpu
from jax.sharding import PartitionSpec as P

HEAD_DIM = 64
EPS = 1e-06
SCALE = HEAD_DIM ** (-0.5)
BF = jnp.bfloat16
F32 = jnp.float32
LONGEST = 170
WINDOW = 192
MASKED = -1e30
VEC_ROWS = 16

V_UP, V_DOWN, V_GAIN2, V_SHIFT2, V_OUT, V_GAIN1, V_SHIFT1, V_QKV = range(8)


def dot_nn(a, b):
    return lax.dot_general(a, b, (((1,), (0,)), ((), ())), preferred_element_type=F32)


def dot_nt(a, b):
    return lax.dot_general(a, b, (((1,), (1,)), ((), ())), preferred_element_type=F32)


def dot_tn(a, b):
    return lax.dot_general(a, b, (((0,), (0,)), ((), ())), preferred_element_type=F32)


def call(body, out_shape, scalars, arrays, scratch, limit_mb, flops):
    whole = pl.BlockSpec(memory_space=pltpu.VMEM)
    moved = sum(a.size * a.dtype.itemsize for a in arrays) + sum(
        o.size * o.dtype.itemsize for o in out_shape
    )
    return pl.pallas_call(
        body,
        out_shape=out_shape,
        in_specs=[pl.BlockSpec(memory_space=pltpu.SMEM)] * len(scalars) + [whole] * len(arrays),
        out_specs=[whole] * len(out_shape),
        scratch_shapes=scratch,
        compiler_params=pltpu.CompilerParams(vmem_limit_bytes=limit_mb << 20),
        cost_estimate=pl.CostEstimate(flops=flops, transcendentals=0, bytes_accessed=moved),
    )(*scalars, *arrays)


def block_start(meta, p, rows):
    return pl.multiple_of(lax.bitwise_xor(meta[0], jnp.int32(p)) * rows, rows)


def norm_rows(x):
    mean = jnp.mean(x, axis=-1, keepdims=True)
    centred = x - mean
    var = jnp.mean(centred * centred, axis=-1, keepdims=True)
    inv = lax.rsqrt(var + EPS)
    return centred * inv, inv


def phi_parts(u):
    cdf = 0.5 * (1.0 + lax.erf(u * 0.7071067811865476))
    return cdf, jnp.exp(u * u * -0.5) * 0.3989422804014327


def stage_a(seq, heads, length, rows, meta, lens, *refs):
    x_refs, (g1, b1, w, bias, wo, normed_o, qkv_o, att_o, keep_o, send_o) = refs[:4], refs[4:]
    clips = lens.shape[1]
    for p in range(4):
        r0 = block_start(meta, p, rows)
        xhat, _ = norm_rows(x_refs[p][...].astype(F32))
        nb = (xhat * g1[...] + b1[...]).astype(BF)
        normed_o[pl.ds(r0, rows), :] = nb
        qkv_o[pl.ds(r0, rows), :] = (dot_nn(nb, w[...]) + bias[...]).astype(BF)

    def attend(q0, q_rows, k0, k_rows, first, last):
        outs = []
        key_at = lax.broadcasted_iota(jnp.int32, (1, k_rows), 1) + k0
        allowed = (key_at >= first) & (key_at < last)
        for h in range(heads):
            col = h * 3 * HEAD_DIM
            q = qkv_o[pl.ds(q0, q_rows), col : col + HEAD_DIM] * BF(SCALE)
            k = qkv_o[pl.ds(k0, k_rows), col + HEAD_DIM : col + 2 * HEAD_DIM]
            v = qkv_o[pl.ds(k0, k_rows), col + 2 * HEAD_DIM : col + 3 * HEAD_DIM]
            s = jnp.where(allowed, dot_nt(q, k), MASKED)
            e = jnp.exp(s - jnp.max(s, axis=1, keepdims=True))
            probs = (e * (1.0 / jnp.sum(e, axis=1, keepdims=True))).astype(BF)
            outs.append(dot_nn(probs, v).astype(BF))
        row_at = lax.broadcasted_iota(jnp.int32, (q_rows, 1), 0) + q0
        new = jnp.concatenate(outs, axis=1)
        old = att_o[pl.ds(q0, q_rows), :]
        att_o[pl.ds(q0, q_rows), :] = jnp.where(row_at >= first, new, old)

    def one_clip(c, first):
        last = first + lens[seq, c]
        w0 = pl.multiple_of(jnp.minimum(first // 16 * 16, length - WINDOW), 16)
        attend(w0, WINDOW, w0, WINDOW, first, last)
        return last

    first = lax.fori_loop(0, clips, one_clip, jnp.int32(0))
    for q0, q_rows, k0 in pad_tiles(clips, length):

        @pl.when(first < q0 + q_rows)
        def _():
            attend(q0, q_rows, k0, length - k0, first, length)

    for p in range(4):
        r0 = block_start(meta, p, rows)
        part = dot_nn(att_o[pl.ds(r0, rows), :], wo[...]).astype(BF)
        (keep_o, send_o)[p & 1][(p >> 1) * rows : (p >> 1) * rows + rows, :] = part


def pad_tiles(clips, length):
    k0 = clips * 100 // 64 * 64
    step = 112 if (length - k0) % 112 == 0 else 64
    return [(q0, step, k0) for q0 in range(k0, length, step)]


def stage_b(first_seq, last_seq, rows, blocks, meta, *refs):
    xs, ms, cots, refs = refs[:4], refs[4:6], refs[6:10], refs[10:]
    ob, g2, b2, wu, hb, wd = refs[:6]
    refs = refs[6:]
    if not first_seq:
        old_up, old_down, old_vec = refs[:3]
        refs = refs[3:]
    keep_f, send_f, keep_n, send_n, xhat_o, inv_o = refs[:6]
    refs = refs[6:]
    if last_seq:
        grads_o, vec_o, n2_s, act_s, ug_s, cot_s = refs
    else:
        up_o, down_o, vec_o, n2_s, act_s, ug_s, cot_s = refs
    d = wu.shape[0]
    up_sum = jnp.zeros((1, wu.shape[1]), F32)
    down_sum = jnp.zeros((1, d), F32)
    for p in range(4):
        half = slice((p >> 1) * rows, (p >> 1) * rows + rows)
        here = slice(p * rows, p * rows + rows)
        mid = xs[p][...].astype(F32) + ms[p & 1][half, :].astype(F32) + ob[...]
        xhat, inv = norm_rows(mid)
        xhat_o[here, :] = xhat.astype(BF)
        inv_o[here, :] = inv
        n2 = (xhat * g2[...] + b2[...]).astype(BF)
        n2_s[here, :] = n2
        u = dot_nn(n2, wu[...]) + hb[...]
        cdf, pdf = phi_parts(u)
        act = (u * cdf).astype(BF)
        act_s[here, :] = act
        (keep_f, send_f)[p & 1][half, :] = dot_nn(act, wd[...]).astype(BF)
        cot = cots[p][...]
        cot_s[here, :] = cot
        down_sum = down_sum + jnp.sum(cot.astype(F32), axis=0, keepdims=True)
        ug = (dot_nt(cot, wd[...]) * (cdf + u * pdf)).astype(BF)
        ug_s[here, :] = ug
        up_sum = up_sum + jnp.sum(ug.astype(F32), axis=0, keepdims=True)
        (keep_n, send_n)[p & 1][half, :] = dot_nt(ug, wu[...]).astype(BF)
    grad_up = dot_tn(n2_s[...], ug_s[...])
    grad_down = dot_tn(act_s[...], cot_s[...])
    if not first_seq:
        grad_up = grad_up + old_up[...]
        grad_down = grad_down + old_down[...]
        up_sum = up_sum + old_vec[V_UP : V_UP + 1, :]
        down_sum = down_sum + old_vec[V_DOWN : V_DOWN + 1, :]
    vec_o[V_UP : V_UP + 1, :] = up_sum
    vec_o[V_DOWN : V_DOWN + 1, :] = down_sum
    if not last_seq:
        up_o[...] = grad_up
        down_o[...] = grad_down
        return
    each = d // blocks
    for j in range(blocks):
        at = lax.bitwise_xor(meta[1], jnp.int32(j))
        grads_o[at, :each, :] = grad_up[j * each : j * each + each].astype(BF)
        grads_o[at, each:, :] = grad_down[j * each : j * each + each].astype(BF)


def stage_c(seq, first_seq, last_seq, heads, length, rows, blocks, meta, lens, *refs):
    ns, cots, refs = refs[:2], refs[2:6], refs[6:]
    xhat_i, inv_i, g2, wo, normed, qkv, att, w, g1, b1 = refs[:10]
    refs = refs[10:]
    if not first_seq:
        old_qkv, old_out, old_vec = refs[:3]
        refs = refs[3:]
    if last_seq:
        vec_b, refs = refs[0], refs[1:]
    mg_o, keep_o, send_o = refs[:3]
    refs = refs[3:]
    if last_seq:
        grads_o, ag_s, da_s, dq_s = refs
    else:
        qkv_o, out_o, vec_o, ag_s, da_s, dq_s = refs
    clips = lens.shape[1]
    d = g2.shape[1]
    sums = {k: jnp.zeros((1, d), F32) for k in (V_GAIN2, V_SHIFT2, V_OUT, V_GAIN1, V_SHIFT1)}
    for p in range(4):
        half = slice((p >> 1) * rows, (p >> 1) * rows + rows)
        here = slice(p * rows, p * rows + rows)
        r0 = block_start(meta, p, rows)
        n = ns[p & 1][half, :].astype(F32)
        xhat = xhat_i[here, :].astype(F32)
        e = n * g2[...]
        mean_e = jnp.mean(e, axis=-1, keepdims=True)
        mean_ex = jnp.mean(e * xhat, axis=-1, keepdims=True)
        mg = cots[p][...].astype(F32) + inv_i[here, :] * (e - mean_e - xhat * mean_ex)
        if p == 0:
            mg_o[...] = mg
        ag = mg.astype(BF)
        ag_s[pl.ds(r0, rows), :] = ag
        da_s[pl.ds(r0, rows), :] = dot_nt(ag, wo[...]).astype(BF)
        sums[V_GAIN2] += jnp.sum(n * xhat, axis=0, keepdims=True)
        sums[V_SHIFT2] += jnp.sum(n, axis=0, keepdims=True)
        sums[V_OUT] += jnp.sum(ag.astype(F32), axis=0, keepdims=True)

    def attend_back(q0, q_rows, k0, k_rows, first, last, add_keys):
        q_at = lax.broadcasted_iota(jnp.int32, (k_rows, q_rows), 1) + q0
        k_at = lax.broadcasted_iota(jnp.int32, (k_rows, q_rows), 0) + k0
        allowed = (k_at >= first) & (k_at < last) & (q_at >= first) & (q_at < last)
        dq_parts, dk_parts, dv_parts = [], [], []
        for h in range(heads):
            col = h * 3 * HEAD_DIM
            q = qkv[pl.ds(q0, q_rows), col : col + HEAD_DIM] * BF(SCALE)
            k = qkv[pl.ds(k0, k_rows), col + HEAD_DIM : col + 2 * HEAD_DIM]
            v = qkv[pl.ds(k0, k_rows), col + 2 * HEAD_DIM : col + 3 * HEAD_DIM]
            do = da_s[pl.ds(q0, q_rows), h * HEAD_DIM : h * HEAD_DIM + HEAD_DIM]
            s = jnp.where(allowed, dot_nt(k, q), MASKED)
            e = jnp.exp(s - jnp.max(s, axis=0, keepdims=True))
            sm = jnp.where(allowed, e * (1.0 / jnp.sum(e, axis=0, keepdims=True)), 0.0)
            dp = dot_nt(v, do)
            t = sm * dp
            ds = (t - sm * jnp.sum(t, axis=0, keepdims=True)).astype(BF)
            dv_parts.append(dot_nn(sm.astype(BF), do))
            dk_parts.append(dot_nn(ds, q))
            dq_parts.append(dot_tn(ds, k) * SCALE)
        return dq_parts, dk_parts, dv_parts

    def one_clip(c, first):
        last = first + lens[seq, c]
        w0 = pl.multiple_of(jnp.minimum(first // 16 * 16, length - WINDOW), 16)
        dq, dk, dv = attend_back(w0, WINDOW, w0, WINDOW, first, last, False)
        new = jnp.concatenate(
            [part[h].astype(BF) for h in range(heads) for part in (dq, dk, dv)], axis=1
        )
        row_at = lax.broadcasted_iota(jnp.int32, (WINDOW, 1), 0) + w0
        old = dq_s[pl.ds(w0, WINDOW), :]
        dq_s[pl.ds(w0, WINDOW), :] = jnp.where(row_at >= first, new, old)
        return last

    first = lax.fori_loop(0, clips, one_clip, jnp.int32(0))
    tiles = pad_tiles(clips, length)
    k0 = tiles[0][2]
    k_rows = length - k0
    q_step = tiles[0][1]

    def pad_scope(kv_acc, dq_acc):
        kv_acc[...] = jnp.zeros_like(kv_acc)
        for q0, q_rows, _ in tiles:

            @pl.when(first < q0 + q_rows)
            def _():
                dq, dk, dv = attend_back(q0, q_rows, k0, k_rows, first, length, True)
                for h in range(heads):
                    kv_acc[2 * h] += dk[h]
                    kv_acc[2 * h + 1] += dv[h]
                    dq_acc[h, q0 - k0 : q0 - k0 + q_rows, :] = dq[h]

        new = jnp.concatenate(
            [
                part.astype(BF)
                for h in range(heads)
                for part in (dq_acc[h], kv_acc[2 * h], kv_acc[2 * h + 1])
            ],
            axis=1,
        )
        row_at = lax.broadcasted_iota(jnp.int32, (k_rows, 1), 0) + k0
        dq_s[k0:, :] = jnp.where(row_at >= first, new, dq_s[k0:, :])

    pl.run_scoped(
        pad_scope,
        pltpu.VMEM((2 * heads, k_rows, HEAD_DIM), F32),
        pltpu.VMEM((heads, k_rows, HEAD_DIM), F32),
    )
    grad_out = dot_tn(ag_s[...], att[...])
    grad_qkv = dot_tn(normed[...], dq_s[...])
    qkv_sum = jnp.sum(dq_s[...].astype(F32), axis=0, keepdims=True)
    for p in range(4):
        r0 = block_start(meta, p, rows)
        ng = dot_nt(dq_s[pl.ds(r0, rows), :], w[...])
        sums[V_SHIFT1] += jnp.sum(ng, axis=0, keepdims=True)
        sums[V_GAIN1] += jnp.sum(ng * normed[pl.ds(r0, rows), :].astype(F32), axis=0, keepdims=True)
        (keep_o, send_o)[p & 1][(p >> 1) * rows : (p >> 1) * rows + rows, :] = ng.astype(BF)
    sums[V_GAIN1] = (sums[V_GAIN1] - b1[...] * sums[V_SHIFT1]) / g1[...]
    sums[V_QKV] = jnp.concatenate([qkv_sum, jnp.zeros((1, d - qkv_sum.shape[1]), F32)], axis=1)
    if not first_seq:
        grad_qkv = grad_qkv + old_qkv[...]
        grad_out = grad_out + old_out[...]
        for k in sums:
            sums[k] += old_vec[k : k + 1, :]
    if not last_seq:
        qkv_o[...] = grad_qkv
        out_o[...] = grad_out
        for k in sums:
            vec_o[k : k + 1, :] = sums[k]
        return
    for k in (V_UP, V_DOWN):
        sums[k] = vec_b[k : k + 1, :]
    each = d // blocks
    wide = grad_qkv.shape[1]
    for j in range(blocks):
        at = lax.bitwise_xor(meta[1], jnp.int32(j))
        grads_o[at, :each, :wide] = grad_qkv[j * each : j * each + each].astype(BF)
        grads_o[at, :each, wide:] = grad_out[j * each : j * each + each].astype(BF)
        grads_o[at, each:, :] = jnp.broadcast_to(sums[j], (VEC_ROWS, d)).astype(BF)


def stage_d(x, mg, keep, got, far, g1, out):
    rows = x.shape[0]
    xhat, inv = norm_rows(x[...].astype(F32))
    n = keep[:rows, :].astype(F32) + got[:rows, :].astype(F32) + far[...].astype(F32)
    e = n * g1[...]
    mean_e = jnp.mean(e, axis=-1, keepdims=True)
    mean_ex = jnp.mean(e * xhat, axis=-1, keepdims=True)
    out[...] = (mg[...] + inv * (e - mean_e - xhat * mean_ex)).astype(BF)


def unpack_ff(each, d, near, far, meta, up_o, down_o):
    for j in range(8):
        at = lax.bitwise_xor(meta[1], jnp.int32(j))
        rows = slice(j * each, j * each + each)

        @pl.when(at < 4)
        def _():
            block = near[jnp.minimum(at, 3)].astype(F32)
            up_o[rows, :] = block[:each]
            down_o[rows, :] = block[each:]

        @pl.when(at >= 4)
        def _():
            block = far[jnp.maximum(at - 4, 0)].astype(F32)
            up_o[rows, :] = block[:each]
            down_o[rows, :] = block[each:]


def unpack_attn(each, wide, near, far, meta, qkv_o, out_o, vec_o):
    for j in range(8):
        at = lax.bitwise_xor(meta[1], jnp.int32(j))
        rows = slice(j * each, j * each + each)

        def put(block):
            qkv_o[rows, :] = block[:each, :wide]
            out_o[rows, :] = block[:each, wide:]
            vec_o[j : j + 1, :] = block[each : each + 1, :]

        @pl.when(at < 4)
        def _():
            put(near[jnp.minimum(at, 3)].astype(F32))

        @pl.when(at >= 4)
        def _():
            put(far[jnp.maximum(at - 4, 0)].astype(F32))


def on_device(
    tokens,
    clip_lengths,
    cotangent,
    query_key_value_weight,
    qv_bias,
    output_weight,
    out_bias,
    gain1,
    shift1,
    gain2,
    shift2,
    up_weight,
    hidden_bias,
    down_weight,
    down_bias,
):
    n_dp = lax.axis_size("dp")
    n_tensor = lax.axis_size("tensor")
    seqs, rows, d = tokens.shape
    length = rows * n_tensor
    heads = output_weight.shape[0] // HEAD_DIM
    wide = 3 * HEAD_DIM * heads
    hidden = up_weight.shape[1]
    blocks = 8
    each = d // blocks

    def core_swap(v):
        return lax.ppermute(v, "tensor", [(t, t ^ 1) for t in range(n_tensor)])

    def chip_swap(v):
        return lax.ppermute(v, "tensor", [(t, t ^ 2) for t in range(n_tensor)])

    t = lax.axis_index("tensor")
    dp_at = lax.axis_index("dp")
    orders = ((0, 1, 2), (1, 2, 0))
    if n_dp == 8:

        def place(order):
            return sum(((dp_at >> order[k]) & 1) << (2 - k) for k in range(3))

        label = jnp.where(t % 2 == 0, place(orders[0]), place(orders[1]))
    else:
        label = jnp.zeros_like(dp_at)
    meta = jnp.stack([t, label]).astype(jnp.int32)

    def add(a, b):
        return (a.astype(F32) + b.astype(F32)).astype(BF)

    def step_perm(k):
        pairs = []
        for dev in range(n_dp):
            for s in range(n_tensor):
                other = dev ^ (1 << orders[s % 2][k])
                pairs.append((dev * n_tensor + s, other * n_tensor + s))
        return pairs

    def all_reduce(buf):
        if n_dp != 8:
            full = lax.psum(buf, "dp")
            return full[:4], full[4:]
        held = buf
        for k in range(3):
            half = held.shape[0] // 2
            got = lax.ppermute(held[half:], ("dp", "tensor"), step_perm(k))
            held = add(held[:half], got)
        for k in (2, 1):
            got = lax.ppermute(held, ("dp", "tensor"), step_perm(k))
            held = jnp.concatenate([held, got], axis=0)
        return held, lax.ppermute(held, ("dp", "tensor"), step_perm(0))

    def row(v):
        return v.reshape(1, -1)

    pairs = qv_bias.reshape(heads, 2, HEAD_DIM)
    bias = row(jnp.stack([pairs[:, 0], jnp.zeros_like(pairs[:, 0]), pairs[:, 1]], axis=1))
    g1, b1, g2, b2 = row(gain1), row(shift1), row(gain2), row(shift2)
    ob, hb = row(out_bias), row(hidden_bias)

    def spread(v):
        near = core_swap(v)
        across = chip_swap(v)
        return [v, near, across, core_swap(across)]

    xs = [spread(tokens[s]) for s in range(seqs)]
    cots = [spread(cotangent[s]) for s in range(seqs)]
    half_shape = jax.ShapeDtypeStruct((2 * rows, d), BF)

    kept = []
    mids = []
    for s in range(seqs):
        normed, qkv, att, keep, send = call(
            functools.partial(stage_a, s, heads, length, rows),
            [
                jax.ShapeDtypeStruct((length, d), BF),
                jax.ShapeDtypeStruct((length, wide), BF),
                jax.ShapeDtypeStruct((length, heads * HEAD_DIM), BF),
                half_shape,
                half_shape,
            ],
            [meta, clip_lengths],
            [*xs[s], g1, b1, query_key_value_weight, bias, output_weight],
            [],
            40,
            2 * length * d * (wide + heads * HEAD_DIM) * 2,
        )
        kept.append((normed, qkv, att))
        chip = add(keep, core_swap(send))
        far = chip_swap(chip)
        own = add(chip, jnp.concatenate([far[rows:], far[:rows]], axis=0))
        mids.append((own, core_swap(own)))

    ffs, n2gs, stats = [], [], []
    carry = []
    for s in range(seqs):
        last = s == seqs - 1
        outs = call(
            functools.partial(stage_b, s == 0, last, rows, blocks),
            [half_shape] * 4
            + [jax.ShapeDtypeStruct((length, d), BF), jax.ShapeDtypeStruct((length, 1), F32)]
            + (
                [jax.ShapeDtypeStruct((blocks, 2 * each, d), BF)]
                if last
                else [jax.ShapeDtypeStruct((d, hidden), F32), jax.ShapeDtypeStruct((hidden, d), F32)]
            )
            + [jax.ShapeDtypeStruct((8, d), F32)],
            [meta],
            [*xs[s], *mids[s], *cots[s], ob, g2, b2, up_weight, hb, down_weight, *carry],
            [pltpu.VMEM((length, d), BF), pltpu.VMEM((length, hidden), BF)]
            + [pltpu.VMEM((length, hidden), BF), pltpu.VMEM((length, d), BF)],
            56,
            12 * length * d * hidden,
        )
        keep_f, send_f, keep_n, send_n, xhat, inv = outs[:6]
        carry = outs[6:]
        chip = add(keep_n, core_swap(send_n))
        far = chip_swap(chip)
        own = add(chip, jnp.concatenate([far[rows:], far[:rows]], axis=0))
        n2gs.append((own, core_swap(own)))
        stats.append((xhat, inv))
        got_f = core_swap(send_f)
        far_f = chip_swap(add(keep_f[rows:], got_f[rows:]))
        ff = keep_f[:rows].astype(F32) + got_f[:rows].astype(F32) + far_f.astype(F32)
        middle = tokens[s].astype(F32) + mids[s][0][:rows].astype(F32) + out_bias
        ffs.append((middle + (ff + down_bias)).astype(BF))
    ff_grads, vec_b = carry
    ff_near, ff_far = all_reduce(ff_grads)

    backs = []
    carry = []
    for s in range(seqs):
        last = s == seqs - 1
        outs = call(
            functools.partial(stage_c, s, s == 0, last, heads, length, rows, blocks),
            [jax.ShapeDtypeStruct((rows, d), F32), half_shape, half_shape]
            + (
                [jax.ShapeDtypeStruct((blocks, each + VEC_ROWS, d), BF)]
                if last
                else [
                    jax.ShapeDtypeStruct((d, wide), F32),
                    jax.ShapeDtypeStruct((d, heads * HEAD_DIM), F32),
                    jax.ShapeDtypeStruct((8, d), F32),
                ]
            ),
            [meta, clip_lengths],
            [*n2gs[s], *cots[s], *stats[s], g2, output_weight, *kept[s]]
            + [query_key_value_weight, g1, b1, *carry]
            + ([vec_b] if last else []),
            [pltpu.VMEM((length, d), BF), pltpu.VMEM((length, heads * HEAD_DIM), BF)]
            + [pltpu.VMEM((length, wide), BF)],
            56,
            4 * length * d * (wide + heads * HEAD_DIM) * 2,
        )
        mg, keep, send = outs[:3]
        carry = outs[3:]
        got = core_swap(send)
        far = chip_swap(add(keep[rows:], got[rows:]))
        backs.append((mg, keep, got, far))
    at_near, at_far = all_reduce(carry[0])

    input_grads = [
        call(stage_d, [jax.ShapeDtypeStruct((rows, d), BF)], [], [tokens[s], *backs[s], g1], [], 24, 0)[0]
        for s in range(seqs)
    ]

    def unpack(body, near, far, out_shape):
        whole = pl.BlockSpec(memory_space=pltpu.VMEM)
        return pl.pallas_call(
            body,
            out_shape=out_shape,
            in_specs=[whole, whole, pl.BlockSpec(memory_space=pltpu.SMEM)],
            out_specs=[whole] * len(out_shape),
            compiler_params=pltpu.CompilerParams(vmem_limit_bytes=24 << 20),
        )(near, far, meta)

    grad_up, grad_down = unpack(
        functools.partial(unpack_ff, each, d),
        ff_near,
        ff_far,
        [jax.ShapeDtypeStruct((d, hidden), F32), jax.ShapeDtypeStruct((hidden, d), F32)],
    )
    grad_qkv, grad_out_t, vec = unpack(
        functools.partial(unpack_attn, each, wide),
        at_near,
        at_far,
        [
            jax.ShapeDtypeStruct((d, wide), F32),
            jax.ShapeDtypeStruct((d, heads * HEAD_DIM), F32),
            jax.ShapeDtypeStruct((8, d), F32),
        ],
    )
    norm1 = vec[V_GAIN1 : V_SHIFT1 + 1]
    norm1 = norm1 + core_swap(norm1)
    norm1 = norm1 + chip_swap(norm1)
    qkv_sum = vec[V_QKV, :wide].reshape(heads, 3, HEAD_DIM)
    return (
        jnp.stack(ffs),
        jnp.stack(input_grads),
        grad_qkv,
        qkv_sum[:, ::2].reshape(-1),
        grad_out_t.T,
        vec[V_OUT],
        norm1[0],
        norm1[1],
        vec[V_GAIN2],
        vec[V_SHIFT2],
        grad_up,
        vec[V_UP],
        grad_down,
        vec[V_DOWN],
    )


def solution(mesh):
    placed = (
        P("dp", "tensor", None),
        P("dp", None),
        P("dp", "tensor", None),
        P(None, "tensor"),
        P("tensor"),
        P("tensor", None),
        P(),
        P(),
        P(),
        P(),
        P(),
        P(None, "tensor"),
        P("tensor"),
        P("tensor", None),
        P(),
    )
    return jax.shard_map(
        on_device,
        mesh=mesh,
        in_specs=placed,
        out_specs=(
            P("dp", "tensor", None),
            P("dp", "tensor", None),
            P(None, "tensor"),
            P("tensor"),
            P("tensor", None),
            P(),
            P(),
            P(),
            P(),
            P(),
            P(None, "tensor"),
            P("tensor"),
            P("tensor", None),
            P(),
        ),
        check_vma=False,
    )
```

```python
import functools

import jax
import jax.numpy as jnp
from jax import lax
from jax.experimental import pallas as pl
from jax.experimental.pallas import tpu as pltpu
from jax.sharding import PartitionSpec as P

HEAD_DIM = 64
EPS = 1e-06
SCALE = HEAD_DIM ** (-0.5)
BF = jnp.bfloat16
F32 = jnp.float32
LONGEST = 170
WINDOW = 192
MASKED = -1e30
VEC_ROWS = 16
COST_SCALE = 1
LIMIT_A, LIMIT_B, LIMIT_C = 12, 24, 24

V_UP, V_DOWN, V_GAIN2, V_SHIFT2, V_OUT, V_GAIN1, V_SHIFT1, V_QKV = range(8)


def dot_nn(a, b):
    return lax.dot_general(a, b, (((1,), (0,)), ((), ())), preferred_element_type=F32)


def dot_nt(a, b):
    return lax.dot_general(a, b, (((1,), (1,)), ((), ())), preferred_element_type=F32)


def dot_tn(a, b):
    return lax.dot_general(a, b, (((0,), (0,)), ((), ())), preferred_element_type=F32)


def call(body, out_shape, scalars, arrays, scratch, limit_mb, flops):
    whole = pl.BlockSpec(memory_space=pltpu.VMEM)
    moved = sum(a.size * a.dtype.itemsize for a in arrays) + sum(
        o.size * o.dtype.itemsize for o in out_shape
    )
    return pl.pallas_call(
        body,
        out_shape=out_shape,
        in_specs=[pl.BlockSpec(memory_space=pltpu.SMEM)] * len(scalars) + [whole] * len(arrays),
        out_specs=[whole] * len(out_shape),
        scratch_shapes=scratch,
        compiler_params=pltpu.CompilerParams(vmem_limit_bytes=limit_mb << 20),
        cost_estimate=pl.CostEstimate(flops=flops * COST_SCALE, transcendentals=0, bytes_accessed=moved),
    )(*scalars, *arrays)


def block_start(meta, p, rows):
    return pl.multiple_of(lax.bitwise_xor(meta[0], jnp.int32(p)) * rows, rows)


def chip_slot(meta, p):
    return lax.bitwise_xor(meta[0] >> 1, jnp.int32(p >> 1))


def norm_rows(x):
    mean = jnp.mean(x, axis=-1, keepdims=True)
    centred = x - mean
    var = jnp.mean(centred * centred, axis=-1, keepdims=True)
    inv = lax.rsqrt(var + EPS)
    return centred * inv, inv


def phi_parts(u):
    cdf = 0.5 * (1.0 + lax.erf(u * 0.7071067811865476))
    return cdf, jnp.exp(u * u * -0.5) * 0.3989422804014327


def pad_range(clips, length):
    k0 = clips * 100 // 64 * 64
    step = 112 if (length - k0) % 112 == 0 else 64
    return k0, step, (length - k0) // step


def clip_start(first, length):
    return pl.multiple_of(jnp.minimum(first // 16 * 16, length - WINDOW), 16)


def stage_a(seq, heads, length, rows, meta, lens, *refs):
    x_refs, (g1, b1, w, bias, wo, normed_o, qkv_o, att_o, keep_o, send_o) = refs[:4], refs[4:]
    clips = lens.shape[1]
    for p in range(4):
        r0 = block_start(meta, p, rows)
        xhat, _ = norm_rows(x_refs[p][seq].astype(F32))
        nb = (xhat * g1[...] + b1[...]).astype(BF)
        normed_o[pl.ds(r0, rows), :] = nb
        qkv_o[pl.ds(r0, rows), :] = (dot_nt(nb, w[...]) + bias[...]).astype(BF)

    def attend(q0, q_rows, k0, k_rows, first, last):
        key_at = lax.broadcasted_iota(jnp.int32, (1, k_rows), 1) + k0
        allowed = (key_at >= first) & (key_at < last)
        row_at = lax.broadcasted_iota(jnp.int32, (q_rows, 1), 0) + q0
        scores, outs = [], []
        for h in range(heads):
            col = h * 3 * HEAD_DIM
            q = qkv_o[pl.ds(q0, q_rows), col : col + HEAD_DIM] * BF(SCALE)
            k = qkv_o[pl.ds(k0, k_rows), col + HEAD_DIM : col + 2 * HEAD_DIM]
            scores.append(dot_nt(q, k))
        for h in range(heads):
            v = qkv_o[pl.ds(k0, k_rows), (h * 3 + 2) * HEAD_DIM : (h * 3 + 3) * HEAD_DIM]
            s = jnp.where(allowed, scores[h], MASKED)
            e = jnp.exp(s - jnp.max(s, axis=1, keepdims=True))
            probs = (e * (1.0 / jnp.sum(e, axis=1, keepdims=True))).astype(BF)
            outs.append(dot_nn(probs, v).astype(BF))
        new = jnp.concatenate(outs, axis=1)
        old = att_o[pl.ds(q0, q_rows), :]
        att_o[pl.ds(q0, q_rows), :] = jnp.where(row_at >= first, new, old)

    def one_clip(c, first):
        last = first + lens[seq, c]
        w0 = clip_start(first, length)
        attend(w0, WINDOW, w0, WINDOW, first, last)
        return last

    first = lax.fori_loop(0, clips, one_clip, jnp.int32(0), unroll=2)
    k0, step, tiles = pad_range(clips, length)

    def pad_tile(i, carry):
        attend(pl.multiple_of(k0 + i * step, 16), step, k0, length - k0, first, length)
        return carry

    lax.fori_loop((first - k0) // step, tiles, pad_tile, jnp.int32(0))

    for p in range(4):
        r0 = block_start(meta, p, rows)
        part = dot_nn(att_o[pl.ds(r0, rows), :], wo[...]).astype(BF)
        (keep_o, send_o)[p & 1][chip_slot(meta, p)] = part


def stage_b(seq, first_seq, last_seq, rows, blocks, meta, *refs):
    xs, ms, cots, refs = refs[:4], refs[4:6], refs[6:10], refs[10:]
    ob, g2, b2, wu, hb, wd = refs[:6]
    refs = refs[6:]
    if not first_seq:
        old_up, old_down, old_vec = refs[:3]
        refs = refs[3:]
    keep_f, send_f, keep_n, send_n, xhat_o, inv_o = refs[:6]
    refs = refs[6:]
    if last_seq:
        grads_o, vec_o, n2_s, act_s, ug_s, cot_s = refs
    else:
        up_o, down_o, vec_o, n2_s, act_s, ug_s, cot_s = refs
    d = wu.shape[0]
    up_sum = jnp.zeros((1, wu.shape[1]), F32)
    down_sum = jnp.zeros((1, d), F32)
    for p in range(4):
        slot = chip_slot(meta, p)
        here = slice(p * rows, p * rows + rows)
        mid = xs[p][seq].astype(F32) + ms[p & 1][slot].astype(F32) + ob[...]
        xhat, inv = norm_rows(mid)
        xhat_o[here, :] = xhat.astype(BF)
        inv_o[here, :] = inv
        n2 = (xhat * g2[...] + b2[...]).astype(BF)
        n2_s[here, :] = n2
        u = dot_nn(n2, wu[...]) + hb[...]
        cdf, pdf = phi_parts(u)
        act = (u * cdf).astype(BF)
        act_s[here, :] = act
        (keep_f, send_f)[p & 1][slot] = dot_nn(act, wd[...]).astype(BF)
        cot = cots[p][seq]
        cot_s[here, :] = cot
        down_sum = down_sum + jnp.sum(cot.astype(F32), axis=0, keepdims=True)
        ug = (dot_nt(cot, wd[...]) * (cdf + u * pdf)).astype(BF)
        ug_s[here, :] = ug
        up_sum = up_sum + jnp.sum(ug.astype(F32), axis=0, keepdims=True)
        (keep_n, send_n)[p & 1][slot] = dot_nt(ug, wu[...]).astype(BF)
    grad_up = dot_tn(n2_s[...], ug_s[...])
    grad_down = dot_tn(act_s[...], cot_s[...])
    if not first_seq:
        grad_up = grad_up + old_up[...]
        grad_down = grad_down + old_down[...]
        up_sum = up_sum + old_vec[V_UP : V_UP + 1, :]
        down_sum = down_sum + old_vec[V_DOWN : V_DOWN + 1, :]
    vec_o[V_UP : V_UP + 1, :] = up_sum
    vec_o[V_DOWN : V_DOWN + 1, :] = down_sum
    if not last_seq:
        up_o[...] = grad_up
        down_o[...] = grad_down
        return
    each = d // blocks
    for j in range(blocks):
        at = lax.bitwise_xor(meta[1], jnp.int32(j))
        grads_o[at, :each, :] = grad_up[j * each : j * each + each].astype(BF)
        grads_o[at, each:, :] = grad_down[j * each : j * each + each].astype(BF)


def stage_c(seq, first_seq, last_seq, heads, length, rows, blocks, meta, lens, *refs):
    ns, cots, refs = refs[:2], refs[2:6], refs[6:]
    xhat_i, inv_i, g2, wo, normed, qkv, att, w, g1, b1 = refs[:10]
    refs = refs[10:]
    if not first_seq:
        old_qkv, old_out, old_vec = refs[:3]
        refs = refs[3:]
    if last_seq:
        vec_b, refs = refs[0], refs[1:]
    mg_o, keep_o, send_o = refs[:3]
    refs = refs[3:]
    if last_seq:
        grads_o, ag_s, da_s, dq_s, kv_acc, q_acc = refs
    else:
        qkv_o, out_o, vec_o, ag_s, da_s, dq_s, kv_acc, q_acc = refs
    clips = lens.shape[1]
    d = g2.shape[1]
    sums = {k: jnp.zeros((1, d), F32) for k in (V_GAIN2, V_SHIFT2, V_OUT, V_GAIN1, V_SHIFT1)}
    for p in range(4):
        slot = chip_slot(meta, p)
        here = slice(p * rows, p * rows + rows)
        r0 = block_start(meta, p, rows)
        n = ns[p & 1][slot].astype(F32)
        xhat = xhat_i[here, :].astype(F32)
        e = n * g2[...]
        mean_e = jnp.mean(e, axis=-1, keepdims=True)
        mean_ex = jnp.mean(e * xhat, axis=-1, keepdims=True)
        mg = cots[p][seq].astype(F32) + inv_i[here, :] * (e - mean_e - xhat * mean_ex)
        if p == 0:
            mg_o[...] = mg
        ag = mg.astype(BF)
        ag_s[pl.ds(r0, rows), :] = ag
        da_s[pl.ds(r0, rows), :] = dot_nt(ag, wo[...]).astype(BF)
        sums[V_GAIN2] += jnp.sum(n * xhat, axis=0, keepdims=True)
        sums[V_SHIFT2] += jnp.sum(n, axis=0, keepdims=True)
        sums[V_OUT] += jnp.sum(ag.astype(F32), axis=0, keepdims=True)

    def attend_back(q0, q_rows, k0, k_rows, first, last):
        q_at = lax.broadcasted_iota(jnp.int32, (k_rows, q_rows), 1) + q0
        k_at = lax.broadcasted_iota(jnp.int32, (k_rows, q_rows), 0) + k0
        allowed = (k_at >= first) & (k_at < last) & (q_at >= first) & (q_at < last)
        qs, ks, dos, scores, prob_grads, sms, dss = [], [], [], [], [], [], []
        for h in range(heads):
            col = h * 3 * HEAD_DIM
            qs.append(qkv[pl.ds(q0, q_rows), col : col + HEAD_DIM] * BF(SCALE))
            ks.append(qkv[pl.ds(k0, k_rows), col + HEAD_DIM : col + 2 * HEAD_DIM])
            v = qkv[pl.ds(k0, k_rows), col + 2 * HEAD_DIM : col + 3 * HEAD_DIM]
            dos.append(da_s[pl.ds(q0, q_rows), h * HEAD_DIM : h * HEAD_DIM + HEAD_DIM])
            scores.append(dot_nt(ks[h], qs[h]))
            prob_grads.append(dot_nt(v, dos[h]))
        for h in range(heads):
            s = jnp.where(allowed, scores[h], MASKED)
            e = jnp.exp(s - jnp.max(s, axis=0, keepdims=True))
            sm = jnp.where(allowed, e * (1.0 / jnp.sum(e, axis=0, keepdims=True)), 0.0)
            t = sm * prob_grads[h]
            dss.append((t - sm * jnp.sum(t, axis=0, keepdims=True)).astype(BF))
            sms.append(sm.astype(BF))
        dv = [dot_nn(sms[h], dos[h]) for h in range(heads)]
        dk = [dot_nn(dss[h], qs[h]) for h in range(heads)]
        dq = [dot_tn(dss[h], ks[h]) * SCALE for h in range(heads)]
        return dq, dk, dv

    def one_clip(c, first):
        last = first + lens[seq, c]
        w0 = clip_start(first, length)
        dq, dk, dv = attend_back(w0, WINDOW, w0, WINDOW, first, last)
        new = jnp.concatenate(
            [part[h].astype(BF) for h in range(heads) for part in (dq, dk, dv)], axis=1
        )
        row_at = lax.broadcasted_iota(jnp.int32, (WINDOW, 1), 0) + w0
        old = dq_s[pl.ds(w0, WINDOW), :]
        dq_s[pl.ds(w0, WINDOW), :] = jnp.where(row_at >= first, new, old)
        return last

    first = lax.fori_loop(0, clips, one_clip, jnp.int32(0), unroll=2)
    k0, step, tiles = pad_range(clips, length)
    k_rows = length - k0
    kv_acc[...] = jnp.zeros_like(kv_acc)

    def pad_tile(i, carry):
        at = pl.multiple_of(i * step, 16)
        dq, dk, dv = attend_back(k0 + at, step, k0, k_rows, first, length)
        for h in range(heads):
            kv_acc[2 * h] += dk[h]
            kv_acc[2 * h + 1] += dv[h]
            q_acc[h, pl.ds(at, step), :] = dq[h].astype(BF)
        return carry

    lax.fori_loop((first - k0) // step, tiles, pad_tile, jnp.int32(0))
    new = jnp.concatenate(
        [
            part.astype(BF)
            for h in range(heads)
            for part in (q_acc[h], kv_acc[2 * h], kv_acc[2 * h + 1])
        ],
        axis=1,
    )
    row_at = lax.broadcasted_iota(jnp.int32, (k_rows, 1), 0) + k0
    dq_s[k0:, :] = jnp.where(row_at >= first, new, dq_s[k0:, :])
    grad_out = dot_tn(att[...], ag_s[...])
    grad_qkv = dot_tn(dq_s[...], normed[...])
    qkv_sum = jnp.sum(dq_s[...].astype(F32), axis=0, keepdims=True)
    for p in range(4):
        r0 = block_start(meta, p, rows)
        ng = dot_nn(dq_s[pl.ds(r0, rows), :], w[...])
        sums[V_SHIFT1] += jnp.sum(ng, axis=0, keepdims=True)
        sums[V_GAIN1] += jnp.sum(ng * normed[pl.ds(r0, rows), :].astype(F32), axis=0, keepdims=True)
        (keep_o, send_o)[p & 1][chip_slot(meta, p)] = ng.astype(BF)
    sums[V_GAIN1] = (sums[V_GAIN1] - b1[...] * sums[V_SHIFT1]) / g1[...]
    sums[V_QKV] = jnp.concatenate([qkv_sum, jnp.zeros((1, d - qkv_sum.shape[1]), F32)], axis=1)
    if not first_seq:
        grad_qkv = grad_qkv + old_qkv[...]
        grad_out = grad_out + old_out[...]
        for k in sums:
            sums[k] += old_vec[k : k + 1, :]
    if not last_seq:
        qkv_o[...] = grad_qkv
        out_o[...] = grad_out
        for k in sums:
            vec_o[k : k + 1, :] = sums[k]
        return
    for k in (V_UP, V_DOWN):
        sums[k] = vec_b[k : k + 1, :]
    each = d // blocks
    wide = grad_qkv.shape[0]
    for j in range(blocks):
        at = lax.bitwise_xor(meta[1], jnp.int32(j))
        r = j * each
        part = grad_qkv[r : r + each] if r < wide else grad_out[r - wide : r - wide + each]
        grads_o[at, :each, :] = part.astype(BF)
        grads_o[at, each:, :] = jnp.broadcast_to(sums[j], (VEC_ROWS, d)).astype(BF)


def run_a(seq, heads, length, rows, d, meta, lens, xs, g1, b1, w, bias, wo):
    wide, attn = 3 * heads * HEAD_DIM, heads * HEAD_DIM
    sd = jax.ShapeDtypeStruct
    return call(
        functools.partial(stage_a, seq, heads, length, rows),
        [sd((length, d), BF), sd((length, wide), BF), sd((length, attn), BF)]
        + [sd((2, rows, d), BF)] * 2,
        [meta, lens],
        [*xs, g1, b1, w, bias, wo],
        [],
        LIMIT_A,
        2 * length * d * (wide + attn) * 2,
    )


def run_b(seq, first_seq, last_seq, rows, d, hidden, blocks, meta, xs, ms, cots, ob, g2, b2, wu, hb, wd, carry):
    sd = jax.ShapeDtypeStruct
    length = 4 * rows
    each = d // blocks
    return call(
        functools.partial(stage_b, seq, first_seq, last_seq, rows, blocks),
        [sd((2, rows, d), BF)] * 4
        + [sd((length, d), BF), sd((length, 1), F32)]
        + (
            [sd((blocks, 2 * each, d), BF)]
            if last_seq
            else [sd((d, hidden), F32), sd((hidden, d), F32)]
        )
        + [sd((8, d), F32)],
        [meta],
        [*xs, *ms, *cots, ob, g2, b2, wu, hb, wd, *carry],
        [pltpu.VMEM((length, d), BF), pltpu.VMEM((length, hidden), BF)]
        + [pltpu.VMEM((length, hidden), BF), pltpu.VMEM((length, d), BF)],
        LIMIT_B,
        12 * length * d * hidden,
    )


def run_c(seq, first_seq, last_seq, heads, length, rows, d, blocks, clips, meta, lens, arrays):
    sd = jax.ShapeDtypeStruct
    wide, attn = 3 * heads * HEAD_DIM, heads * HEAD_DIM
    each = d // blocks
    k_rows = length - pad_range(clips, length)[0]
    return call(
        functools.partial(stage_c, seq, first_seq, last_seq, heads, length, rows, blocks),
        [sd((rows, d), F32), sd((2, rows, d), BF), sd((2, rows, d), BF)]
        + (
            [sd((blocks, each + VEC_ROWS, d), BF)]
            if last_seq
            else [sd((wide, d), F32), sd((attn, d), F32), sd((8, d), F32)]
        ),
        [meta, lens],
        arrays,
        [pltpu.VMEM((length, d), BF), pltpu.VMEM((length, attn), BF), pltpu.VMEM((length, wide), BF)]
        + [pltpu.VMEM((2 * heads, k_rows, HEAD_DIM), F32), pltpu.VMEM((heads, k_rows, HEAD_DIM), BF)],
        LIMIT_C,
        4 * length * d * (wide + attn) * 2,
    )


def stage_d(seq, meta, x, mg, keep, got, far, g1, out):
    xhat, inv = norm_rows(x[seq].astype(F32))
    slot = meta[0] >> 1
    n = keep[slot].astype(F32) + got[slot].astype(F32) + far[...].astype(F32)
    e = n * g1[...]
    mean_e = jnp.mean(e, axis=-1, keepdims=True)
    mean_ex = jnp.mean(e * xhat, axis=-1, keepdims=True)
    out[...] = (mg[...] + inv * (e - mean_e - xhat * mean_ex)).astype(BF)


def unpack_ff(each, d, near, far, meta, up_o, down_o):
    for j in range(8):
        at = lax.bitwise_xor(meta[1], jnp.int32(j))
        rows = slice(j * each, j * each + each)

        @pl.when(at < 4)
        def _():
            block = near[jnp.minimum(at, 3)].astype(F32)
            up_o[rows, :] = block[:each]
            down_o[rows, :] = block[each:]

        @pl.when(at >= 4)
        def _():
            block = far[jnp.maximum(at - 4, 0)].astype(F32)
            up_o[rows, :] = block[:each]
            down_o[rows, :] = block[each:]


def unpack_attn(each, wide, near, far, meta, qkv_o, out_o, vec_o):
    for j in range(8):
        at = lax.bitwise_xor(meta[1], jnp.int32(j))
        r = j * each

        def put(block):
            if r < wide:
                qkv_o[r : r + each, :] = block[:each]
            else:
                out_o[r - wide : r - wide + each, :] = block[:each]
            vec_o[j : j + 1, :] = block[each : each + 1, :]

        @pl.when(at < 4)
        def _():
            put(near[jnp.minimum(at, 3)].astype(F32))

        @pl.when(at >= 4)
        def _():
            put(far[jnp.maximum(at - 4, 0)].astype(F32))


def on_device(
    tokens,
    clip_lengths,
    cotangent,
    query_key_value_weight,
    qv_bias,
    output_weight,
    out_bias,
    gain1,
    shift1,
    gain2,
    shift2,
    up_weight,
    hidden_bias,
    down_weight,
    down_bias,
):
    n_dp = lax.axis_size("dp")
    n_tensor = lax.axis_size("tensor")
    seqs, rows, d = tokens.shape
    length = rows * n_tensor
    heads = output_weight.shape[0] // HEAD_DIM
    wide = 3 * HEAD_DIM * heads
    hidden = up_weight.shape[1]
    blocks = 8
    each = d // blocks

    def core_swap(v):
        return lax.ppermute(v, "tensor", [(t, t ^ 1) for t in range(n_tensor)])

    def chip_swap(v):
        return lax.ppermute(v, "tensor", [(t, t ^ 2) for t in range(n_tensor)])

    t = lax.axis_index("tensor")
    dp_at = lax.axis_index("dp")
    orders = ((0, 1, 2), (1, 2, 0))
    if n_dp == 8:

        def place(order):
            return sum(((dp_at >> order[k]) & 1) << (2 - k) for k in range(3))

        label = jnp.where(t % 2 == 0, place(orders[0]), place(orders[1]))
    else:
        label = jnp.zeros_like(dp_at)
    meta = jnp.stack([t, label]).astype(jnp.int32)

    def add(a, b):
        return (a.astype(F32) + b.astype(F32)).astype(BF)

    def after(value, *others):
        return lax.optimization_barrier((value, others))[0]

    def step_perm(k):
        pairs = []
        for dev in range(n_dp):
            for s in range(n_tensor):
                other = dev ^ (1 << orders[s % 2][k])
                pairs.append((dev * n_tensor + s, other * n_tensor + s))
        return pairs

    def reduce_get(held, k):
        return lax.ppermute(held[held.shape[0] // 2 :], ("dp", "tensor"), step_perm(k))

    def reduce_step(held, k):
        return add(held[: held.shape[0] // 2], reduce_get(held, k))

    def gather_step(held, k):
        return lax.ppermute(held, ("dp", "tensor"), step_perm(k))

    def gather_all(held):
        for k in (2, 1):
            held = jnp.concatenate([held, gather_step(held, k)], axis=0)
        return held, gather_step(held, 0)

    def after(value, *others):
        return lax.optimization_barrier((value, others))[0]

    def step_perm(k):
        pairs = []
        for dev in range(n_dp):
            for s in range(n_tensor):
                other = dev ^ (1 << orders[s % 2][k])
                pairs.append((dev * n_tensor + s, other * n_tensor + s))
        return pairs

    def all_reduce(buf):
        if n_dp != 8:
            full = lax.psum(buf, "dp")
            return full[:4], full[4:]
        held = buf
        for k in range(3):
            half = held.shape[0] // 2
            got = lax.ppermute(held[half:], ("dp", "tensor"), step_perm(k))
            held = add(held[:half], got)
        for k in (2, 1):
            got = lax.ppermute(held, ("dp", "tensor"), step_perm(k))
            held = jnp.concatenate([held, got], axis=0)
        return held, lax.ppermute(held, ("dp", "tensor"), step_perm(0))

    def row(v):
        return v.reshape(1, -1)

    pairs = qv_bias.reshape(heads, 2, HEAD_DIM)
    bias = row(jnp.stack([pairs[:, 0], jnp.zeros_like(pairs[:, 0]), pairs[:, 1]], axis=1))
    g1, b1, g2, b2 = row(gain1), row(shift1), row(gain2), row(shift2)
    ob, hb = row(out_bias), row(hidden_bias)
    chip_at = t >> 1

    w_t = query_key_value_weight.T

    def spread(v):
        near = core_swap(v)
        across = chip_swap(v)
        return [v, near, across, core_swap(across)]

    def chip_sum(keep, send):
        return add(keep, core_swap(send))

    def all_rows(chip, far):
        own = add(chip, far)
        return [own, core_swap(own)]

    def peer_rows(keep, got):
        return add(keep[1 - chip_at], got[1 - chip_at])

    xs = spread(tokens)
    cots = spread(cotangent)
    beside = cots[2]

    kept, chips, fars = [], [], []
    for s in range(seqs):
        outs = run_a(
            s, heads, length, rows, d, meta, clip_lengths, after(xs, *chips[-1:]), g1, b1,
            w_t, bias, output_weight,
        )
        kept.append(outs[:3])
        chips.append(chip_sum(outs[3], after(outs[4], beside)))
        beside = chip_swap(chips[s])
        fars.append(beside)

    mids, stats, ff_keep, ff_send, n_chips, n_fars = [], [], [], [], [], []
    carry = []
    for s in range(seqs):
        mids.append(all_rows(chips[s], fars[s]))
        outs = run_b(
            s, s == 0, s == seqs - 1, rows, d, hidden, blocks, meta, xs,
            after(mids[s], *(chips[-1:] + n_chips[-1:])), cots,
            ob, g2, b2, up_weight, hb, down_weight, carry,
        )
        n_chips.append(chip_sum(outs[2], after(outs[3], beside)))
        beside = chip_swap(n_chips[s])
        n_fars.append(beside)
        ff_keep.append(outs[0])
        ff_send.append(outs[1])
        stats.append(outs[4:6])
        carry = outs[6:]
    ff_grads, vec_b = carry

    backs, peers, far_rows = [], [], []
    carry = []
    held = ff_grads
    steps = 0
    for s in range(seqs):
        n_now = after(all_rows(n_chips[s], n_fars[s]), *(n_chips[-1:] + peers[-1:]), held)
        outs = run_c(
            s, s == 0, s == seqs - 1, heads, length, rows, d, blocks, clip_lengths.shape[1],
            meta, clip_lengths,
            [*n_now, *cots, *stats[s], g2, output_weight, *kept[s], w_t]
            + [g1, b1, *carry] + ([vec_b] if s == seqs - 1 else []),
        )
        mg, keep, send = outs[:3]
        carry = outs[3:]
        waits = [beside]
        if n_dp == 8 and steps < 3:
            part = reduce_get(held, steps)
            waits.append(part)
        got = core_swap(after(send, *waits))
        if n_dp == 8 and steps < 3:
            held = add(held[: held.shape[0] // 2], part)
            steps += 1
        peers.append(peer_rows(keep, got))
        beside = chip_swap(peers[s])
        far_rows.append(beside)
        backs.append((mg, keep, got))
    at_grads = carry[0]
    ff_got = [core_swap(after(send, peers[-1])) for send in ff_send]
    ff_far_rows = [chip_swap(peer_rows(keep, got)) for keep, got in zip(ff_keep, ff_got)]
    if n_dp == 8:
        for k in range(steps, 3):
            held = reduce_step(held, k)
        ff_near, ff_far = gather_all(held)
        held = at_grads
        for k in range(3):
            held = reduce_step(held, k)
        at_near, at_far = gather_all(held)
    else:
        ff_sum, at_sum = lax.psum((ff_grads, at_grads), "dp")
        ff_near, ff_far, at_near, at_far = ff_sum[:4], ff_sum[4:], at_sum[:4], at_sum[4:]

    ffs = []
    for s in range(seqs):
        ff = ff_keep[s][chip_at].astype(F32) + ff_got[s][chip_at].astype(F32)
        middle = tokens[s].astype(F32) + mids[s][0][chip_at].astype(F32) + out_bias
        ffs.append((middle + (ff + ff_far_rows[s].astype(F32) + down_bias)).astype(BF))

    whole = pl.BlockSpec(memory_space=pltpu.VMEM)
    input_grads = [
        pl.pallas_call(
            functools.partial(stage_d, s),
            out_shape=jax.ShapeDtypeStruct((rows, d), BF),
            in_specs=[pl.BlockSpec(memory_space=pltpu.SMEM)] + [whole] * 6,
            out_specs=whole,
            compiler_params=pltpu.CompilerParams(vmem_limit_bytes=16 << 20),
        )(meta, tokens, *backs[s], far_rows[s], g1)
        for s in range(seqs)
    ]

    def unpack(body, near, far, out_shape):
        whole = pl.BlockSpec(memory_space=pltpu.VMEM)
        return pl.pallas_call(
            body,
            out_shape=out_shape,
            in_specs=[whole, whole, pl.BlockSpec(memory_space=pltpu.SMEM)],
            out_specs=[whole] * len(out_shape),
            compiler_params=pltpu.CompilerParams(vmem_limit_bytes=24 << 20),
        )(near, far, meta)

    grad_up, grad_down = unpack(
        functools.partial(unpack_ff, each, d),
        ff_near,
        ff_far,
        [jax.ShapeDtypeStruct((d, hidden), F32), jax.ShapeDtypeStruct((hidden, d), F32)],
    )
    grad_qkv, grad_out, vec = unpack(
        functools.partial(unpack_attn, each, wide),
        at_near,
        at_far,
        [
            jax.ShapeDtypeStruct((wide, d), F32),
            jax.ShapeDtypeStruct((d - wide, d), F32),
            jax.ShapeDtypeStruct((8, d), F32),
        ],
    )
    norm1 = vec[V_GAIN1 : V_SHIFT1 + 1]
    norm1 = norm1 + core_swap(norm1)
    norm1 = norm1 + chip_swap(norm1)
    qkv_sum = vec[V_QKV, :wide].reshape(heads, 3, HEAD_DIM)
    return (
        jnp.stack(ffs),
        jnp.stack(input_grads),
        grad_qkv.T,
        qkv_sum[:, ::2].reshape(-1),
        grad_out,
        vec[V_OUT],
        norm1[0],
        norm1[1],
        vec[V_GAIN2],
        vec[V_SHIFT2],
        grad_up,
        vec[V_UP],
        grad_down,
        vec[V_DOWN],
    )


def solution(mesh):
    placed = (
        P("dp", "tensor", None),
        P("dp", None),
        P("dp", "tensor", None),
        P(None, "tensor"),
        P("tensor"),
        P("tensor", None),
        P(),
        P(),
        P(),
        P(),
        P(),
        P(None, "tensor"),
        P("tensor"),
        P("tensor", None),
        P(),
    )
    return jax.shard_map(
        on_device,
        mesh=mesh,
        in_specs=placed,
        out_specs=(
            P("dp", "tensor", None),
            P("dp", "tensor", None),
            P(None, "tensor"),
            P("tensor"),
            P("tensor", None),
            P(),
            P(),
            P(),
            P(),
            P(),
            P(None, "tensor"),
            P("tensor"),
            P("tensor", None),
            P(),
        ),
        check_vma=False,
    )
```

```python
import functools

import jax
import jax.numpy as jnp
from jax import lax
from jax.experimental import pallas as pl
from jax.experimental.pallas import tpu as pltpu
from jax.sharding import PartitionSpec as P

HEAD_DIM = 64
EPS = 1e-06
SCALE = HEAD_DIM ** (-0.5)
BF = jnp.bfloat16
F32 = jnp.float32
LONGEST = 170
WINDOW = 192
MASKED = -1e30
VEC_ROWS = 16
COST_SCALE = 1
LIMIT_A, LIMIT_B, LIMIT_C = 20, 36, 32

V_UP, V_DOWN, V_GAIN2, V_SHIFT2, V_OUT, V_GAIN1, V_SHIFT1, V_QKV = range(8)


def dot_nn(a, b):
    return lax.dot_general(a, b, (((1,), (0,)), ((), ())), preferred_element_type=F32)


def dot_nt(a, b):
    return lax.dot_general(a, b, (((1,), (1,)), ((), ())), preferred_element_type=F32)


def dot_tn(a, b):
    return lax.dot_general(a, b, (((0,), (0,)), ((), ())), preferred_element_type=F32)


def call(body, out_shape, scalars, arrays, scratch, limit_mb, flops, far_in, far_out):
    whole = pl.BlockSpec(memory_space=pltpu.VMEM)
    far = pl.BlockSpec(memory_space=pltpu.HBM)
    moved = sum(a.size * a.dtype.itemsize for a in arrays) + sum(
        o.size * o.dtype.itemsize for o in out_shape
    )
    return pl.pallas_call(
        body,
        out_shape=[pltpu.HBM(o.shape, o.dtype) if i in far_out else o for i, o in enumerate(out_shape)],
        in_specs=[pl.BlockSpec(memory_space=pltpu.SMEM)] * len(scalars)
        + [far if i in far_in else whole for i in range(len(arrays))],
        out_specs=[far if i in far_out else whole for i in range(len(out_shape))],
        scratch_shapes=scratch,
        compiler_params=pltpu.CompilerParams(vmem_limit_bytes=limit_mb << 20),
        cost_estimate=pl.CostEstimate(flops=flops * COST_SCALE, transcendentals=0, bytes_accessed=moved),
    )(
        *scalars,
        *[
            pltpu.with_memory_space_constraint(a, pltpu.HBM) if i in far_in else a
            for i, a in enumerate(arrays)
        ],
    )


def sem(n):
    return pltpu.SemaphoreType.DMA((n,))


def vm(*shape, dtype=BF):
    return pltpu.VMEM(shape, dtype)


def copies(done, *pairs):
    made = [pltpu.make_async_copy(src, dst, done.at[i]) for i, (src, dst) in enumerate(pairs)]
    for c in made:
        c.start()
    return made


def block_start(meta, p, rows):
    return pl.multiple_of(lax.bitwise_xor(meta[0], jnp.int32(p)) * rows, rows)


def chip_slot(meta, p):
    return lax.bitwise_xor(meta[0] >> 1, jnp.int32(p >> 1))


def norm_rows(x):
    mean = jnp.mean(x, axis=-1, keepdims=True)
    centred = x - mean
    var = jnp.mean(centred * centred, axis=-1, keepdims=True)
    inv = lax.rsqrt(var + EPS)
    return centred * inv, inv


def phi_parts(u):
    cdf = 0.5 * (1.0 + lax.erf(u * 0.7071067811865476))
    return cdf, jnp.exp(u * u * -0.5) * 0.3989422804014327


def pad_range(clips, length):
    k0 = clips * 100 // 64 * 64
    step = 112 if (length - k0) % 112 == 0 else 64
    return k0, step, (length - k0) // step


def clip_start(first, length):
    return pl.multiple_of(jnp.minimum(first // 16 * 16, length - WINDOW), 16)


def stage_a(seq, heads, length, rows, meta, lens, *refs):
    x_refs, (g1, b1, w_h, bias, wo_h), refs = refs[:4], refs[4:9], refs[9:]
    normed_h, qkv_h, att_h, keep_o, send_o, x_s, w, wo, normed_o, qkv_o, att_o, in_sem, out_sem = refs
    clips = lens.shape[1]
    get = copies(
        in_sem,
        (x_refs[0].at[seq], x_s.at[0]),
        (w_h, w),
        *[(x_refs[p].at[seq], x_s.at[p]) for p in range(1, 4)],
        (wo_h, wo),
    )
    get[1].wait()
    for p in range(4):
        r0 = block_start(meta, p, rows)
        get[p + (p > 0)].wait()
        xhat, _ = norm_rows(x_s[p].astype(F32))
        nb = (xhat * g1[...] + b1[...]).astype(BF)
        normed_o[pl.ds(r0, rows), :] = nb
        qkv_o[pl.ds(r0, rows), :] = (dot_nt(nb, w[...]) + bias[...]).astype(BF)

    put = copies(out_sem, (normed_o, normed_h), (qkv_o, qkv_h))

    def attend(q0, q_rows, k0, k_rows, first, last):
        key_at = lax.broadcasted_iota(jnp.int32, (1, k_rows), 1) + k0
        allowed = (key_at >= first) & (key_at < last)
        row_at = lax.broadcasted_iota(jnp.int32, (q_rows, 1), 0) + q0
        scores, outs = [], []
        for h in range(heads):
            col = h * 3 * HEAD_DIM
            q = qkv_o[pl.ds(q0, q_rows), col : col + HEAD_DIM] * BF(SCALE)
            k = qkv_o[pl.ds(k0, k_rows), col + HEAD_DIM : col + 2 * HEAD_DIM]
            scores.append(dot_nt(q, k))
        for h in range(heads):
            v = qkv_o[pl.ds(k0, k_rows), (h * 3 + 2) * HEAD_DIM : (h * 3 + 3) * HEAD_DIM]
            s = jnp.where(allowed, scores[h], MASKED)
            e = jnp.exp(s - jnp.max(s, axis=1, keepdims=True))
            probs = (e * (1.0 / jnp.sum(e, axis=1, keepdims=True))).astype(BF)
            outs.append(dot_nn(probs, v).astype(BF))
        new = jnp.concatenate(outs, axis=1)
        old = att_o[pl.ds(q0, q_rows), :]
        att_o[pl.ds(q0, q_rows), :] = jnp.where(row_at >= first, new, old)

    def one_clip(c, first):
        last = first + lens[seq, c]
        w0 = clip_start(first, length)
        attend(w0, WINDOW, w0, WINDOW, first, last)
        return last

    first = lax.fori_loop(0, clips, one_clip, jnp.int32(0), unroll=2)
    k0, step, tiles = pad_range(clips, length)

    def pad_tile(i, carry):
        attend(pl.multiple_of(k0 + i * step, 16), step, k0, length - k0, first, length)
        return carry

    lax.fori_loop((first - k0) // step, tiles, pad_tile, jnp.int32(0))

    att_put = pltpu.make_async_copy(att_o, att_h, out_sem.at[2])
    att_put.start()
    get[5].wait()
    for p in range(4):
        r0 = block_start(meta, p, rows)
        part = dot_nn(att_o[pl.ds(r0, rows), :], wo[...]).astype(BF)
        (keep_o, send_o)[p & 1][chip_slot(meta, p)] = part
    for c in [*put, att_put]:
        c.wait()


def stage_b(seq, first_seq, last_seq, rows, blocks, meta, *refs):
    xs, ms, cots, refs = refs[:4], refs[4:6], refs[6:10], refs[10:]
    ob, g2, b2, wu_h, hb, wd_h = refs[:6]
    refs = refs[6:]
    if not first_seq:
        old_up, old_down, old_vec = refs[:3]
        refs = refs[3:]
    keep_fh, send_fh, keep_n, send_n, xhat_h, inv_h = refs[:6]
    refs = refs[6:]
    if last_seq:
        grads_o, vec_o = refs[:2]
        refs = refs[2:]
    else:
        up_o, down_o, vec_o = refs[:3]
        refs = refs[3:]
    n2_s, act_s, ug_s, cot_s, x_s, wu, wd, keep_f, send_f, xhat_o, inv_o, in_sem, out_sem = refs
    pieces = []
    for p in range(4):
        here = pl.ds(p * rows, rows)
        pieces += [(xs[p].at[seq], x_s.at[p]), (cots[p].at[seq], cot_s.at[here, :])]
        if p == 0:
            pieces += [(wu_h, wu), (wd_h, wd)]
    get = copies(in_sem, *pieces)
    get[2].wait()
    get[3].wait()
    d = wu.shape[0]
    up_sum = jnp.zeros((1, wu.shape[1]), F32)
    down_sum = jnp.zeros((1, d), F32)
    for p in range(4):
        slot = chip_slot(meta, p)
        here = slice(p * rows, p * rows + rows)
        for c in get[2 * p + 2 * (p > 0) : 2 * p + 2 * (p > 0) + 2]:
            c.wait()
        mid = x_s[p].astype(F32) + ms[p & 1][slot].astype(F32) + ob[...]
        xhat, inv = norm_rows(mid)
        xhat_o[here, :] = xhat.astype(BF)
        inv_o[here, :] = inv
        n2 = (xhat * g2[...] + b2[...]).astype(BF)
        n2_s[here, :] = n2
        u = dot_nn(n2, wu[...]) + hb[...]
        cdf, pdf = phi_parts(u)
        act = (u * cdf).astype(BF)
        act_s[here, :] = act
        (keep_f, send_f)[p & 1][slot] = dot_nn(act, wd[...]).astype(BF)
        cot = cot_s[here, :]
        down_sum = down_sum + jnp.sum(cot.astype(F32), axis=0, keepdims=True)
        ug = (dot_nt(cot, wd[...]) * (cdf + u * pdf)).astype(BF)
        ug_s[here, :] = ug
        up_sum = up_sum + jnp.sum(ug.astype(F32), axis=0, keepdims=True)
        (keep_n, send_n)[p & 1][slot] = dot_nt(ug, wu[...]).astype(BF)
    put = copies(
        out_sem, (keep_f, keep_fh), (send_f, send_fh), (xhat_o, xhat_h), (inv_o, inv_h)
    )
    grad_up = dot_tn(n2_s[...], ug_s[...])
    grad_down = dot_tn(act_s[...], cot_s[...])
    if not first_seq:
        grad_up = grad_up + old_up[...]
        grad_down = grad_down + old_down[...]
        up_sum = up_sum + old_vec[V_UP : V_UP + 1, :]
        down_sum = down_sum + old_vec[V_DOWN : V_DOWN + 1, :]
    vec_o[V_UP : V_UP + 1, :] = up_sum
    vec_o[V_DOWN : V_DOWN + 1, :] = down_sum
    if not last_seq:
        up_o[...] = grad_up
        down_o[...] = grad_down
    else:
        each = d // blocks
        for j in range(blocks):
            at = lax.bitwise_xor(meta[1], jnp.int32(j))
            grads_o[at, :each, :] = grad_up[j * each : j * each + each].astype(BF)
            grads_o[at, each:, :] = grad_down[j * each : j * each + each].astype(BF)
    for c in put:
        c.wait()


def stage_c(seq, first_seq, last_seq, heads, length, rows, blocks, meta, lens, *refs):
    ns, cots, refs = refs[:2], refs[2:6], refs[6:]
    xhat_h, inv_h, g2, wo_h, normed_h, qkv_h, att_h, w_h, g1, b1 = refs[:10]
    refs = refs[10:]
    if not first_seq:
        old_qkv, old_out, old_vec = refs[:3]
        refs = refs[3:]
    if last_seq:
        vec_b, refs = refs[0], refs[1:]
    mg_h, keep_o, send_o = refs[:3]
    refs = refs[3:]
    if last_seq:
        grads_o, refs = refs[0], refs[1:]
    else:
        qkv_o, out_o, vec_o = refs[:3]
        refs = refs[3:]
    ag_s, da_s, dq_s, kv_acc, q_acc, cot_s, xhat_i, inv_i = refs[:8]
    wo, normed, qkv, att, w, mg_o, in_sem, out_sem = refs[8:]
    pieces = []
    for p in range(4):
        here = pl.ds(p * rows, rows)
        pieces += [(cots[p].at[seq], cot_s.at[p])]
        pieces += [(ref.at[here, :], dst.at[here, :]) for ref, dst in ((xhat_h, xhat_i), (inv_h, inv_i))]
        if p == 0:
            pieces += [(wo_h, wo)]
    get = copies(in_sem, *pieces, (qkv_h, qkv), (att_h, att), (w_h, w), (normed_h, normed))
    get[3].wait()
    clips = lens.shape[1]
    d = g2.shape[1]
    sums = {k: jnp.zeros((1, d), F32) for k in (V_GAIN2, V_SHIFT2, V_OUT, V_GAIN1, V_SHIFT1)}
    for p in range(4):
        slot = chip_slot(meta, p)
        here = slice(p * rows, p * rows + rows)
        r0 = block_start(meta, p, rows)
        for c in get[3 * p + (p > 0) : 3 * p + (p > 0) + 3]:
            c.wait()
        n = ns[p & 1][slot].astype(F32)
        xhat = xhat_i[here, :].astype(F32)
        e = n * g2[...]
        mean_e = jnp.mean(e, axis=-1, keepdims=True)
        mean_ex = jnp.mean(e * xhat, axis=-1, keepdims=True)
        mg = cot_s[p].astype(F32) + inv_i[here, :] * (e - mean_e - xhat * mean_ex)
        if p == 0:
            mg_o[...] = mg
        ag = mg.astype(BF)
        ag_s[pl.ds(r0, rows), :] = ag
        da_s[pl.ds(r0, rows), :] = dot_nt(ag, wo[...]).astype(BF)
        sums[V_GAIN2] += jnp.sum(n * xhat, axis=0, keepdims=True)
        sums[V_SHIFT2] += jnp.sum(n, axis=0, keepdims=True)
        sums[V_OUT] += jnp.sum(ag.astype(F32), axis=0, keepdims=True)

    put = pltpu.make_async_copy(mg_o, mg_h, out_sem.at[0])
    put.start()
    get[13].wait()

    def attend_back(q0, q_rows, k0, k_rows, first, last):
        q_at = lax.broadcasted_iota(jnp.int32, (k_rows, q_rows), 1) + q0
        k_at = lax.broadcasted_iota(jnp.int32, (k_rows, q_rows), 0) + k0
        allowed = (k_at >= first) & (k_at < last) & (q_at >= first) & (q_at < last)
        qs, ks, dos, scores, prob_grads, sms, dss = [], [], [], [], [], [], []
        for h in range(heads):
            col = h * 3 * HEAD_DIM
            qs.append(qkv[pl.ds(q0, q_rows), col : col + HEAD_DIM] * BF(SCALE))
            ks.append(qkv[pl.ds(k0, k_rows), col + HEAD_DIM : col + 2 * HEAD_DIM])
            v = qkv[pl.ds(k0, k_rows), col + 2 * HEAD_DIM : col + 3 * HEAD_DIM]
            dos.append(da_s[pl.ds(q0, q_rows), h * HEAD_DIM : h * HEAD_DIM + HEAD_DIM])
            scores.append(dot_nt(ks[h], qs[h]))
            prob_grads.append(dot_nt(v, dos[h]))
        for h in range(heads):
            s = jnp.where(allowed, scores[h], MASKED)
            e = jnp.exp(s - jnp.max(s, axis=0, keepdims=True))
            sm = jnp.where(allowed, e * (1.0 / jnp.sum(e, axis=0, keepdims=True)), 0.0)
            t = sm * prob_grads[h]
            dss.append((t - sm * jnp.sum(t, axis=0, keepdims=True)).astype(BF))
            sms.append(sm.astype(BF))
        dv = [dot_nn(sms[h], dos[h]) for h in range(heads)]
        dk = [dot_nn(dss[h], qs[h]) for h in range(heads)]
        dq = [dot_tn(dss[h], ks[h]) * SCALE for h in range(heads)]
        return dq, dk, dv

    def one_clip(c, first):
        last = first + lens[seq, c]
        w0 = clip_start(first, length)
        dq, dk, dv = attend_back(w0, WINDOW, w0, WINDOW, first, last)
        new = jnp.concatenate(
            [part[h].astype(BF) for h in range(heads) for part in (dq, dk, dv)], axis=1
        )
        row_at = lax.broadcasted_iota(jnp.int32, (WINDOW, 1), 0) + w0
        old = dq_s[pl.ds(w0, WINDOW), :]
        dq_s[pl.ds(w0, WINDOW), :] = jnp.where(row_at >= first, new, old)
        return last

    first = lax.fori_loop(0, clips, one_clip, jnp.int32(0), unroll=2)
    k0, step, tiles = pad_range(clips, length)
    k_rows = length - k0
    kv_acc[...] = jnp.zeros_like(kv_acc)

    def pad_tile(i, carry):
        at = pl.multiple_of(i * step, 16)
        dq, dk, dv = attend_back(k0 + at, step, k0, k_rows, first, length)
        for h in range(heads):
            kv_acc[2 * h] += dk[h]
            kv_acc[2 * h + 1] += dv[h]
            q_acc[h, pl.ds(at, step), :] = dq[h].astype(BF)
        return carry

    lax.fori_loop((first - k0) // step, tiles, pad_tile, jnp.int32(0))
    new = jnp.concatenate(
        [
            part.astype(BF)
            for h in range(heads)
            for part in (q_acc[h], kv_acc[2 * h], kv_acc[2 * h + 1])
        ],
        axis=1,
    )
    row_at = lax.broadcasted_iota(jnp.int32, (k_rows, 1), 0) + k0
    dq_s[k0:, :] = jnp.where(row_at >= first, new, dq_s[k0:, :])
    for c in get[14:]:
        c.wait()
    grad_out = dot_tn(att[...], ag_s[...])
    grad_qkv = dot_tn(dq_s[...], normed[...])
    qkv_sum = jnp.sum(dq_s[...].astype(F32), axis=0, keepdims=True)
    for p in range(4):
        r0 = block_start(meta, p, rows)
        ng = dot_nn(dq_s[pl.ds(r0, rows), :], w[...])
        sums[V_SHIFT1] += jnp.sum(ng, axis=0, keepdims=True)
        sums[V_GAIN1] += jnp.sum(ng * normed[pl.ds(r0, rows), :].astype(F32), axis=0, keepdims=True)
        (keep_o, send_o)[p & 1][chip_slot(meta, p)] = ng.astype(BF)
    sums[V_GAIN1] = (sums[V_GAIN1] - b1[...] * sums[V_SHIFT1]) / g1[...]
    sums[V_QKV] = jnp.concatenate([qkv_sum, jnp.zeros((1, d - qkv_sum.shape[1]), F32)], axis=1)
    if not first_seq:
        grad_qkv = grad_qkv + old_qkv[...]
        grad_out = grad_out + old_out[...]
        for k in sums:
            sums[k] += old_vec[k : k + 1, :]
    if not last_seq:
        qkv_o[...] = grad_qkv
        out_o[...] = grad_out
        for k in sums:
            vec_o[k : k + 1, :] = sums[k]
        put.wait()
        return
    for k in (V_UP, V_DOWN):
        sums[k] = vec_b[k : k + 1, :]
    each = d // blocks
    wide = grad_qkv.shape[0]
    for j in range(blocks):
        at = lax.bitwise_xor(meta[1], jnp.int32(j))
        r = j * each
        part = grad_qkv[r : r + each] if r < wide else grad_out[r - wide : r - wide + each]
        grads_o[at, :each, :] = part.astype(BF)
        grads_o[at, each:, :] = jnp.broadcast_to(sums[j], (VEC_ROWS, d)).astype(BF)
    put.wait()


def run_a(seq, heads, length, rows, d, meta, lens, xs, g1, b1, w, bias, wo):
    wide, attn = 3 * heads * HEAD_DIM, heads * HEAD_DIM
    sd = jax.ShapeDtypeStruct
    return call(
        functools.partial(stage_a, seq, heads, length, rows),
        [sd((length, d), BF), sd((length, wide), BF), sd((length, attn), BF)]
        + [sd((2, rows, d), BF)] * 2,
        [meta, lens],
        [*xs, g1, b1, w, bias, wo],
        [vm(4, rows, d), vm(wide, d), vm(attn, d), vm(length, d), vm(length, wide)]
        + [vm(length, attn), sem(6), sem(3)],
        LIMIT_A,
        2 * length * d * (wide + attn) * 2,
        (0, 1, 2, 3, 6, 8),
        (0, 1, 2),
    )


def run_b(seq, first_seq, last_seq, rows, d, hidden, blocks, meta, xs, ms, cots, ob, g2, b2, wu, hb, wd, carry):
    sd = jax.ShapeDtypeStruct
    length = 4 * rows
    each = d // blocks
    return call(
        functools.partial(stage_b, seq, first_seq, last_seq, rows, blocks),
        [sd((2, rows, d), BF)] * 4
        + [sd((length, d), BF), sd((length, 1), F32)]
        + (
            [sd((blocks, 2 * each, d), BF)]
            if last_seq
            else [sd((d, hidden), F32), sd((hidden, d), F32)]
        )
        + [sd((8, d), F32)],
        [meta],
        [*xs, *ms, *cots, ob, g2, b2, wu, hb, wd, *carry],
        [pltpu.VMEM((length, d), BF), pltpu.VMEM((length, hidden), BF)]
        + [pltpu.VMEM((length, hidden), BF), pltpu.VMEM((length, d), BF)]
        + [vm(4, rows, d), vm(d, hidden), vm(hidden, d), vm(2, rows, d), vm(2, rows, d)]
        + [vm(length, d), vm(length, 1, dtype=F32), sem(10), sem(4)],
        LIMIT_B,
        12 * length * d * hidden,
        (0, 1, 2, 3, 6, 7, 8, 9, 13, 15),
        (0, 1, 4, 5),
    )


def run_c(seq, first_seq, last_seq, heads, length, rows, d, blocks, clips, meta, lens, arrays):
    sd = jax.ShapeDtypeStruct
    wide, attn = 3 * heads * HEAD_DIM, heads * HEAD_DIM
    each = d // blocks
    k_rows = length - pad_range(clips, length)[0]
    return call(
        functools.partial(stage_c, seq, first_seq, last_seq, heads, length, rows, blocks),
        [sd((rows, d), F32), sd((2, rows, d), BF), sd((2, rows, d), BF)]
        + (
            [sd((blocks, each + VEC_ROWS, d), BF)]
            if last_seq
            else [sd((wide, d), F32), sd((attn, d), F32), sd((8, d), F32)]
        ),
        [meta, lens],
        arrays,
        [pltpu.VMEM((length, d), BF), pltpu.VMEM((length, attn), BF), pltpu.VMEM((length, wide), BF)]
        + [pltpu.VMEM((2 * heads, k_rows, HEAD_DIM), F32), pltpu.VMEM((heads, k_rows, HEAD_DIM), BF)]
        + [vm(4, rows, d), vm(length, d), vm(length, 1, dtype=F32), vm(attn, d), vm(length, d)]
        + [vm(length, wide), vm(length, attn), vm(wide, d), vm(rows, d, dtype=F32), sem(17), sem(1)],
        LIMIT_C,
        4 * length * d * (wide + attn) * 2,
        (2, 3, 4, 5, 6, 7, 9, 10, 11, 12, 13),
        (0,),
    )


def stage_d(seq, meta, x, mg, keep, got, far, g1, out):
    xhat, inv = norm_rows(x[seq].astype(F32))
    slot = meta[0] >> 1
    n = keep[slot].astype(F32) + got[slot].astype(F32) + far[...].astype(F32)
    e = n * g1[...]
    mean_e = jnp.mean(e, axis=-1, keepdims=True)
    mean_ex = jnp.mean(e * xhat, axis=-1, keepdims=True)
    out[...] = (mg[...] + inv * (e - mean_e - xhat * mean_ex)).astype(BF)


def unpack_ff(each, d, near, far, meta, up_o, down_o):
    for j in range(8):
        at = lax.bitwise_xor(meta[1], jnp.int32(j))
        rows = slice(j * each, j * each + each)

        @pl.when(at < 4)
        def _():
            block = near[jnp.minimum(at, 3)].astype(F32)
            up_o[rows, :] = block[:each]
            down_o[rows, :] = block[each:]

        @pl.when(at >= 4)
        def _():
            block = far[jnp.maximum(at - 4, 0)].astype(F32)
            up_o[rows, :] = block[:each]
            down_o[rows, :] = block[each:]


def unpack_attn(each, wide, near, far, meta, qkv_o, out_o, vec_o):
    for j in range(8):
        at = lax.bitwise_xor(meta[1], jnp.int32(j))
        r = j * each

        def put(block):
            if r < wide:
                qkv_o[r : r + each, :] = block[:each]
            else:
                out_o[r - wide : r - wide + each, :] = block[:each]
            vec_o[j : j + 1, :] = block[each : each + 1, :]

        @pl.when(at < 4)
        def _():
            put(near[jnp.minimum(at, 3)].astype(F32))

        @pl.when(at >= 4)
        def _():
            put(far[jnp.maximum(at - 4, 0)].astype(F32))


def on_device(
    tokens,
    clip_lengths,
    cotangent,
    query_key_value_weight,
    qv_bias,
    output_weight,
    out_bias,
    gain1,
    shift1,
    gain2,
    shift2,
    up_weight,
    hidden_bias,
    down_weight,
    down_bias,
):
    n_dp = lax.axis_size("dp")
    n_tensor = lax.axis_size("tensor")
    seqs, rows, d = tokens.shape
    length = rows * n_tensor
    heads = output_weight.shape[0] // HEAD_DIM
    wide = 3 * HEAD_DIM * heads
    hidden = up_weight.shape[1]
    blocks = 8
    each = d // blocks

    def core_swap(v):
        return lax.ppermute(v, "tensor", [(t, t ^ 1) for t in range(n_tensor)])

    def chip_swap(v):
        return lax.ppermute(v, "tensor", [(t, t ^ 2) for t in range(n_tensor)])

    t = lax.axis_index("tensor")
    dp_at = lax.axis_index("dp")
    orders = ((0, 1, 2), (1, 0, 2))
    if n_dp == 8:

        def place(order):
            return sum(((dp_at >> order[k]) & 1) << (2 - k) for k in range(3))

        label = jnp.where(t % 2 == 0, place(orders[0]), place(orders[1]))
    else:
        label = jnp.zeros_like(dp_at)
    meta = jnp.stack([t, label]).astype(jnp.int32)

    def add(a, b):
        return (a.astype(F32) + b.astype(F32)).astype(BF)

    def after(value, *others):
        return lax.optimization_barrier((value, others))[0]

    def step_perm(k):
        pairs = []
        for dev in range(n_dp):
            for s in range(n_tensor):
                other = dev ^ (1 << orders[s % 2][k])
                pairs.append((dev * n_tensor + s, other * n_tensor + s))
        return pairs

    def reduce_get(held, k):
        return lax.ppermute(held[held.shape[0] // 2 :], ("dp", "tensor"), step_perm(k))

    def reduce_step(held, k):
        return add(held[: held.shape[0] // 2], reduce_get(held, k))

    def gather_step(held, k):
        return lax.ppermute(held, ("dp", "tensor"), step_perm(k))

    def gather_all(held):
        for k in (2, 1):
            held = jnp.concatenate([held, gather_step(held, k)], axis=0)
        return held, gather_step(held, 0)

    def after(value, *others):
        return lax.optimization_barrier((value, others))[0]

    def step_perm(k):
        pairs = []
        for dev in range(n_dp):
            for s in range(n_tensor):
                other = dev ^ (1 << orders[s % 2][k])
                pairs.append((dev * n_tensor + s, other * n_tensor + s))
        return pairs

    def all_reduce(buf):
        if n_dp != 8:
            full = lax.psum(buf, "dp")
            return full[:4], full[4:]
        held = buf
        for k in range(3):
            half = held.shape[0] // 2
            got = lax.ppermute(held[half:], ("dp", "tensor"), step_perm(k))
            held = add(held[:half], got)
        for k in (2, 1):
            got = lax.ppermute(held, ("dp", "tensor"), step_perm(k))
            held = jnp.concatenate([held, got], axis=0)
        return held, lax.ppermute(held, ("dp", "tensor"), step_perm(0))

    def row(v):
        return v.reshape(1, -1)

    pairs = qv_bias.reshape(heads, 2, HEAD_DIM)
    bias = row(jnp.stack([pairs[:, 0], jnp.zeros_like(pairs[:, 0]), pairs[:, 1]], axis=1))
    g1, b1, g2, b2 = row(gain1), row(shift1), row(gain2), row(shift2)
    ob, hb = row(out_bias), row(hidden_bias)
    chip_at = t >> 1

    w_t = query_key_value_weight.T

    def spread(v, *first):
        near = core_swap(v)
        across = after(chip_swap(v), *first)
        return [v, near, across, core_swap(across)]

    def chip_sum(keep, send):
        return add(keep, core_swap(send))

    def all_rows(chip, far):
        own = add(chip, far)
        return [own, core_swap(own)]

    def peer_rows(keep, got):
        return add(keep[1 - chip_at], got[1 - chip_at])

    xs = spread(tokens, g1, b1, g2, b2, ob, hb, bias, meta)
    cot_near = core_swap(cotangent)
    beside = chip_swap(cotangent)

    kept, chips, fars = [], [], []
    for s in range(seqs):
        outs = run_a(
            s, heads, length, rows, d, meta, clip_lengths, after(xs, *chips[-1:]), g1, b1,
            w_t, bias, output_weight,
        )
        kept.append(outs[:3])
        if s == 0:
            beside = after(beside, outs[3])
            cots = [cotangent, cot_near, beside, core_swap(beside)]
        chips.append(chip_sum(outs[3], after(outs[4], beside)))
        beside = chip_swap(chips[s])
        fars.append(beside)

    mids, stats, ff_keep, ff_send, n_chips, n_fars = [], [], [], [], [], []
    carry = []
    for s in range(seqs):
        mids.append(all_rows(chips[s], fars[s]))
        outs = run_b(
            s, s == 0, s == seqs - 1, rows, d, hidden, blocks, meta, xs,
            after(mids[s], *(chips[-1:] + n_chips[-1:])), cots,
            ob, g2, b2, up_weight, hb, down_weight, carry,
        )
        n_chips.append(chip_sum(outs[2], after(outs[3], beside)))
        beside = chip_swap(n_chips[s])
        n_fars.append(beside)
        ff_keep.append(outs[0])
        ff_send.append(outs[1])
        stats.append(outs[4:6])
        carry = outs[6:]
    ff_grads, vec_b = carry

    backs, peers, far_rows = [], [], []
    carry = []
    held = ff_grads
    steps = 0
    for s in range(seqs):
        n_now = after(all_rows(n_chips[s], n_fars[s]), *(n_chips[-1:] + peers[-1:]), held)
        outs = run_c(
            s, s == 0, s == seqs - 1, heads, length, rows, d, blocks, clip_lengths.shape[1],
            meta, clip_lengths,
            [*n_now, *cots, *stats[s], g2, output_weight, *kept[s], w_t]
            + [g1, b1, *carry] + ([vec_b] if s == seqs - 1 else []),
        )
        mg, keep, send = outs[:3]
        carry = outs[3:]
        waits = [beside]
        if n_dp == 8 and steps < 3:
            part = reduce_get(held, steps)
            waits.append(part)
        got = core_swap(after(send, *waits))
        if n_dp == 8 and steps < 3:
            held = add(held[: held.shape[0] // 2], part)
            steps += 1
        peers.append(peer_rows(keep, got))
        beside = chip_swap(peers[s])
        far_rows.append(beside)
        backs.append((mg, keep, got))
    at_grads = carry[0]
    ff_got = [core_swap(after(send, peers[-1])) for send in ff_send]
    ff_peers = [peer_rows(keep, got) for keep, got in zip(ff_keep, ff_got)]
    ff_far_rows = [chip_swap(v) for v in ff_peers]
    whole = pl.BlockSpec(memory_space=pltpu.VMEM)

    def input_rows(s):
        return pl.pallas_call(
            functools.partial(stage_d, s),
            out_shape=jax.ShapeDtypeStruct((rows, d), BF),
            in_specs=[pl.BlockSpec(memory_space=pltpu.SMEM)] + [whole] * 6,
            out_specs=whole,
            compiler_params=pltpu.CompilerParams(vmem_limit_bytes=16 << 20),
        )(meta, tokens, *backs[s], far_rows[s], g1)

    def output_rows(s):
        ff = ff_keep[s][chip_at].astype(F32) + ff_got[s][chip_at].astype(F32)
        middle = tokens[s].astype(F32) + mids[s][0][chip_at].astype(F32) + out_bias
        return (middle + (ff + ff_far_rows[s].astype(F32) + down_bias)).astype(BF)

    input_grad = jnp.stack([input_rows(s) for s in range(seqs)])
    block_out = jnp.stack([output_rows(s) for s in range(seqs)])
    if n_dp == 8:
        for k in range(steps, 3):
            part = after(reduce_get(held, k), *(ff_peers if k == 2 else []))
            held = add(held[: held.shape[0] // 2], part)
        part = gather_step(held, 2)
        held = jnp.concatenate([held, part], axis=0)
        part = after(gather_step(held, 1), input_grad, block_out)
        ff_near = jnp.concatenate([held, part], axis=0)
        ff_far = gather_step(ff_near, 0)
        held = at_grads
        for k in range(3):
            held = reduce_step(held, k)
        at_near, at_far = gather_all(held)
    else:
        ff_sum, at_sum = lax.psum((ff_grads, at_grads), "dp")
        ff_near, ff_far, at_near, at_far = ff_sum[:4], ff_sum[4:], at_sum[:4], at_sum[4:]

    def unpack(body, near, far, out_shape):
        whole = pl.BlockSpec(memory_space=pltpu.VMEM)
        return pl.pallas_call(
            body,
            out_shape=out_shape,
            in_specs=[whole, whole, pl.BlockSpec(memory_space=pltpu.SMEM)],
            out_specs=[whole] * len(out_shape),
            compiler_params=pltpu.CompilerParams(vmem_limit_bytes=24 << 20),
        )(near, far, meta)

    grad_up, grad_down = unpack(
        functools.partial(unpack_ff, each, d),
        ff_near,
        ff_far,
        [jax.ShapeDtypeStruct((d, hidden), F32), jax.ShapeDtypeStruct((hidden, d), F32)],
    )
    at_far = after(at_far, block_out, input_grad, grad_up, grad_down)

    def vec_row(j):
        at = label ^ j
        return jnp.where(at < 4, at_near[at & 3, each], at_far[at & 3, each]).astype(F32)

    norm1 = jnp.stack([vec_row(V_GAIN1), vec_row(V_SHIFT1)])
    norm1 = norm1 + core_swap(norm1)
    norm1 = norm1 + chip_swap(norm1)
    grad_qkv, grad_out, vec = unpack(
        functools.partial(unpack_attn, each, wide),
        at_near,
        at_far,
        [
            jax.ShapeDtypeStruct((wide, d), F32),
            jax.ShapeDtypeStruct((d - wide, d), F32),
            jax.ShapeDtypeStruct((8, d), F32),
        ],
    )
    qkv_sum = vec[V_QKV, :wide].reshape(heads, 3, HEAD_DIM)
    return (
        block_out,
        input_grad,
        grad_qkv.T,
        qkv_sum[:, ::2].reshape(-1),
        grad_out,
        vec[V_OUT],
        norm1[0],
        norm1[1],
        vec[V_GAIN2],
        vec[V_SHIFT2],
        grad_up,
        vec[V_UP],
        grad_down,
        vec[V_DOWN],
    )


def solution(mesh):
    placed = (
        P("dp", "tensor", None),
        P("dp", None),
        P("dp", "tensor", None),
        P(None, "tensor"),
        P("tensor"),
        P("tensor", None),
        P(),
        P(),
        P(),
        P(),
        P(),
        P(None, "tensor"),
        P("tensor"),
        P("tensor", None),
        P(),
    )
    return jax.shard_map(
        on_device,
        mesh=mesh,
        in_specs=placed,
        out_specs=(
            P("dp", "tensor", None),
            P("dp", "tensor", None),
            P(None, "tensor"),
            P("tensor"),
            P("tensor", None),
            P(),
            P(),
            P(),
            P(),
            P(),
            P(None, "tensor"),
            P("tensor"),
            P("tensor", None),
            P(),
        ),
        check_vma=False,
    )
```

```python
import functools

import jax
import jax.numpy as jnp
from jax import lax
from jax.experimental import pallas as pl
from jax.experimental.pallas import tpu as pltpu
from jax.sharding import PartitionSpec as P

HEAD_DIM = 64
EPS = 1e-06
SCALE = HEAD_DIM ** (-0.5)
BF = jnp.bfloat16
F32 = jnp.float32
LONGEST = 170
WINDOW = 192
MASKED = -1e30
VEC_ROWS = 16
COST_SCALE = 1
LIMIT_A, LIMIT_B, LIMIT_C = 20, 36, 32

V_UP, V_DOWN, V_GAIN2, V_SHIFT2, V_OUT, V_GAIN1, V_SHIFT1, V_QKV = range(8)


def dot_nn(a, b):
    return lax.dot_general(a, b, (((1,), (0,)), ((), ())), preferred_element_type=F32)


def dot_nt(a, b):
    return lax.dot_general(a, b, (((1,), (1,)), ((), ())), preferred_element_type=F32)


def dot_tn(a, b):
    return lax.dot_general(a, b, (((0,), (0,)), ((), ())), preferred_element_type=F32)


def call(body, out_shape, scalars, arrays, scratch, limit_mb, flops, far_in, far_out):
    whole = pl.BlockSpec(memory_space=pltpu.VMEM)
    far = pl.BlockSpec(memory_space=pltpu.HBM)
    moved = sum(a.size * a.dtype.itemsize for a in arrays) + sum(
        o.size * o.dtype.itemsize for o in out_shape
    )
    return pl.pallas_call(
        body,
        out_shape=[pltpu.HBM(o.shape, o.dtype) if i in far_out else o for i, o in enumerate(out_shape)],
        in_specs=[pl.BlockSpec(memory_space=pltpu.SMEM)] * len(scalars)
        + [far if i in far_in else whole for i in range(len(arrays))],
        out_specs=[far if i in far_out else whole for i in range(len(out_shape))],
        scratch_shapes=scratch,
        compiler_params=pltpu.CompilerParams(vmem_limit_bytes=limit_mb << 20),
        cost_estimate=pl.CostEstimate(flops=flops * COST_SCALE, transcendentals=0, bytes_accessed=moved),
    )(
        *scalars,
        *[
            pltpu.with_memory_space_constraint(a, pltpu.HBM) if i in far_in else a
            for i, a in enumerate(arrays)
        ],
    )


def sem(n):
    return pltpu.SemaphoreType.DMA((n,))


def vm(*shape, dtype=BF):
    return pltpu.VMEM(shape, dtype)


def copies(done, *pairs):
    made = [pltpu.make_async_copy(src, dst, done.at[i]) for i, (src, dst) in enumerate(pairs)]
    for c in made:
        c.start()
    return made


def block_start(meta, p, rows):
    return pl.multiple_of(lax.bitwise_xor(meta[0], jnp.int32(p)) * rows, rows)


def chip_slot(meta, p):
    return lax.bitwise_xor(meta[0] >> 1, jnp.int32(p >> 1))


def norm_rows(x):
    mean = jnp.mean(x, axis=-1, keepdims=True)
    centred = x - mean
    var = jnp.mean(centred * centred, axis=-1, keepdims=True)
    inv = lax.rsqrt(var + EPS)
    return centred * inv, inv


def phi_parts(u):
    cdf = 0.5 * (1.0 + lax.erf(u * 0.7071067811865476))
    return cdf, jnp.exp(u * u * -0.5) * 0.3989422804014327


def pad_range(clips, length):
    k0 = clips * 100 // 64 * 64
    step = 112 if (length - k0) % 112 == 0 else 64
    return k0, step, (length - k0) // step


def clip_start(first, length):
    return pl.multiple_of(jnp.minimum(first // 16 * 16, length - WINDOW), 16)


def stage_a(seq, heads, length, rows, meta, lens, *refs):
    x_refs, (g1, b1, w_h, bias, wo_h), refs = refs[:4], refs[4:9], refs[9:]
    normed_h, qkv_h, att_h, keep_o, send_o, x_s, w, wo, normed_o, qkv_o, att_o, in_sem, out_sem = refs
    clips = lens.shape[1]
    get = copies(
        in_sem,
        (x_refs[0].at[seq], x_s.at[0]),
        (w_h, w),
        *[(x_refs[p].at[seq], x_s.at[p]) for p in range(1, 4)],
        (wo_h, wo),
    )
    get[1].wait()
    for p in range(4):
        r0 = block_start(meta, p, rows)
        get[p + (p > 0)].wait()
        xhat, _ = norm_rows(x_s[p].astype(F32))
        nb = (xhat * g1[...] + b1[...]).astype(BF)
        normed_o[pl.ds(r0, rows), :] = nb
        qkv_o[pl.ds(r0, rows), :] = (dot_nt(nb, w[...]) + bias[...]).astype(BF)

    put = copies(out_sem, (normed_o, normed_h), (qkv_o, qkv_h))

    def attend(q0, q_rows, k0, k_rows, first, last):
        key_at = lax.broadcasted_iota(jnp.int32, (1, k_rows), 1) + k0
        allowed = (key_at >= first) & (key_at < last)
        row_at = lax.broadcasted_iota(jnp.int32, (q_rows, 1), 0) + q0
        scores, outs = [], []
        for h in range(heads):
            col = h * 3 * HEAD_DIM
            q = qkv_o[pl.ds(q0, q_rows), col : col + HEAD_DIM] * BF(SCALE)
            k = qkv_o[pl.ds(k0, k_rows), col + HEAD_DIM : col + 2 * HEAD_DIM]
            scores.append(dot_nt(q, k))
        for h in range(heads):
            v = qkv_o[pl.ds(k0, k_rows), (h * 3 + 2) * HEAD_DIM : (h * 3 + 3) * HEAD_DIM]
            s = jnp.where(allowed, scores[h], MASKED)
            e = jnp.exp(s - jnp.max(s, axis=1, keepdims=True))
            probs = (e * (1.0 / jnp.sum(e, axis=1, keepdims=True))).astype(BF)
            outs.append(dot_nn(probs, v).astype(BF))
        new = jnp.concatenate(outs, axis=1)
        old = att_o[pl.ds(q0, q_rows), :]
        att_o[pl.ds(q0, q_rows), :] = jnp.where(row_at >= first, new, old)

    def one_clip(c, first):
        last = first + lens[seq, c]
        w0 = clip_start(first, length)
        attend(w0, WINDOW, w0, WINDOW, first, last)
        return last

    first = lax.fori_loop(0, clips, one_clip, jnp.int32(0), unroll=2)
    k0, step, tiles = pad_range(clips, length)

    def pad_tile(i, carry):
        attend(pl.multiple_of(k0 + i * step, 16), step, k0, length - k0, first, length)
        return carry

    lax.fori_loop((first - k0) // step, tiles, pad_tile, jnp.int32(0))

    att_put = pltpu.make_async_copy(att_o, att_h, out_sem.at[2])
    att_put.start()
    get[5].wait()
    for p in range(4):
        r0 = block_start(meta, p, rows)
        part = dot_nn(att_o[pl.ds(r0, rows), :], wo[...]).astype(BF)
        (keep_o, send_o)[p & 1][chip_slot(meta, p)] = part
    for c in [*put, att_put]:
        c.wait()


def stage_b(seq, first_seq, last_seq, rows, blocks, meta, *refs):
    xs, ms, cots, refs = refs[:4], refs[4:6], refs[6:10], refs[10:]
    ob, g2, b2, wu_h, hb, wd_h = refs[:6]
    refs = refs[6:]
    if not first_seq:
        old_up, old_down, old_vec = refs[:3]
        refs = refs[3:]
    keep_fh, send_fh, keep_n, send_n, xhat_h, inv_h = refs[:6]
    refs = refs[6:]
    if last_seq:
        grads_o, vec_o = refs[:2]
        refs = refs[2:]
    else:
        up_o, down_o, vec_o = refs[:3]
        refs = refs[3:]
    n2_s, act_s, ug_s, cot_s, x_s, wu, wd, keep_f, send_f, xhat_o, inv_o, in_sem, out_sem = refs
    pieces = []
    for p in range(4):
        here = pl.ds(p * rows, rows)
        pieces += [(xs[p].at[seq], x_s.at[p]), (cots[p].at[seq], cot_s.at[here, :])]
        if p == 0:
            pieces += [(wu_h, wu), (wd_h, wd)]
    get = copies(in_sem, *pieces)
    get[2].wait()
    get[3].wait()
    d = wu.shape[0]
    up_sum = jnp.zeros((1, wu.shape[1]), F32)
    down_sum = jnp.zeros((1, d), F32)
    for p in range(4):
        slot = chip_slot(meta, p)
        here = slice(p * rows, p * rows + rows)
        for c in get[2 * p + 2 * (p > 0) : 2 * p + 2 * (p > 0) + 2]:
            c.wait()
        mid = x_s[p].astype(F32) + ms[p & 1][slot].astype(F32) + ob[...]
        xhat, inv = norm_rows(mid)
        xhat_o[here, :] = xhat.astype(BF)
        inv_o[here, :] = inv
        n2 = (xhat * g2[...] + b2[...]).astype(BF)
        n2_s[here, :] = n2
        u = dot_nn(n2, wu[...]) + hb[...]
        cdf, pdf = phi_parts(u)
        act = (u * cdf).astype(BF)
        act_s[here, :] = act
        (keep_f, send_f)[p & 1][slot] = dot_nn(act, wd[...]).astype(BF)
        cot = cot_s[here, :]
        down_sum = down_sum + jnp.sum(cot.astype(F32), axis=0, keepdims=True)
        ug = (dot_nt(cot, wd[...]) * (cdf + u * pdf)).astype(BF)
        ug_s[here, :] = ug
        up_sum = up_sum + jnp.sum(ug.astype(F32), axis=0, keepdims=True)
        (keep_n, send_n)[p & 1][slot] = dot_nt(ug, wu[...]).astype(BF)
    put = copies(
        out_sem, (keep_f, keep_fh), (send_f, send_fh), (xhat_o, xhat_h), (inv_o, inv_h)
    )
    grad_up = dot_tn(n2_s[...], ug_s[...])
    grad_down = dot_tn(act_s[...], cot_s[...])
    if not first_seq:
        grad_up = grad_up + old_up[...]
        grad_down = grad_down + old_down[...]
        up_sum = up_sum + old_vec[V_UP : V_UP + 1, :]
        down_sum = down_sum + old_vec[V_DOWN : V_DOWN + 1, :]
    vec_o[V_UP : V_UP + 1, :] = up_sum
    vec_o[V_DOWN : V_DOWN + 1, :] = down_sum
    if not last_seq:
        up_o[...] = grad_up
        down_o[...] = grad_down
    else:
        each = d // blocks
        for j in range(blocks):
            at = lax.bitwise_xor(meta[1], jnp.int32(j))
            grads_o[at, :each, :] = grad_up[j * each : j * each + each].astype(BF)
            grads_o[at, each:, :] = grad_down[j * each : j * each + each].astype(BF)
    for c in put:
        c.wait()


def stage_c(seq, heads, length, rows, meta, lens, *refs):
    ns, cots, refs = refs[:2], refs[2:6], refs[6:]
    xhat_h, inv_h, g2, wo_h, qkv_h, mg_h, ag_s, dq_s, vec_o = refs[:9]
    da_s, kv_acc, q_acc, cot_s, xhat_i, inv_i, wo, qkv, mg_o, in_sem, out_sem = refs[9:]
    pieces = []
    for p in range(4):
        here = pl.ds(p * rows, rows)
        pieces += [(cots[p].at[seq], cot_s.at[p])]
        pieces += [(ref.at[here, :], dst.at[here, :]) for ref, dst in ((xhat_h, xhat_i), (inv_h, inv_i))]
        if p == 0:
            pieces += [(wo_h, wo)]
    get = copies(in_sem, *pieces, (qkv_h, qkv))
    get[3].wait()
    clips = lens.shape[1]
    d = g2.shape[1]
    sums = {k: jnp.zeros((1, d), F32) for k in (V_GAIN2, V_SHIFT2, V_OUT)}
    for p in range(4):
        slot = chip_slot(meta, p)
        here = slice(p * rows, p * rows + rows)
        r0 = block_start(meta, p, rows)
        for c in get[3 * p + (p > 0) : 3 * p + (p > 0) + 3]:
            c.wait()
        n = ns[p & 1][slot].astype(F32)
        xhat = xhat_i[here, :].astype(F32)
        e = n * g2[...]
        mean_e = jnp.mean(e, axis=-1, keepdims=True)
        mean_ex = jnp.mean(e * xhat, axis=-1, keepdims=True)
        mg = cot_s[p].astype(F32) + inv_i[here, :] * (e - mean_e - xhat * mean_ex)
        if p == 0:
            mg_o[...] = mg
        ag = mg.astype(BF)
        ag_s[pl.ds(r0, rows), :] = ag
        da_s[pl.ds(r0, rows), :] = dot_nt(ag, wo[...]).astype(BF)
        sums[V_GAIN2] += jnp.sum(n * xhat, axis=0, keepdims=True)
        sums[V_SHIFT2] += jnp.sum(n, axis=0, keepdims=True)
        sums[V_OUT] += jnp.sum(ag.astype(F32), axis=0, keepdims=True)

    put = pltpu.make_async_copy(mg_o, mg_h, out_sem.at[0])
    put.start()
    get[13].wait()

    def attend_back(q0, q_rows, k0, k_rows, first, last):
        q_at = lax.broadcasted_iota(jnp.int32, (k_rows, q_rows), 1) + q0
        k_at = lax.broadcasted_iota(jnp.int32, (k_rows, q_rows), 0) + k0
        allowed = (k_at >= first) & (k_at < last) & (q_at >= first) & (q_at < last)
        qs, ks, dos, scores, prob_grads, sms, dss = [], [], [], [], [], [], []
        for h in range(heads):
            col = h * 3 * HEAD_DIM
            qs.append(qkv[pl.ds(q0, q_rows), col : col + HEAD_DIM] * BF(SCALE))
            ks.append(qkv[pl.ds(k0, k_rows), col + HEAD_DIM : col + 2 * HEAD_DIM])
            v = qkv[pl.ds(k0, k_rows), col + 2 * HEAD_DIM : col + 3 * HEAD_DIM]
            dos.append(da_s[pl.ds(q0, q_rows), h * HEAD_DIM : h * HEAD_DIM + HEAD_DIM])
            scores.append(dot_nt(ks[h], qs[h]))
            prob_grads.append(dot_nt(v, dos[h]))
        for h in range(heads):
            s = jnp.where(allowed, scores[h], MASKED)
            e = jnp.exp(s - jnp.max(s, axis=0, keepdims=True))
            sm = jnp.where(allowed, e * (1.0 / jnp.sum(e, axis=0, keepdims=True)), 0.0)
            t = sm * prob_grads[h]
            dss.append((t - sm * jnp.sum(t, axis=0, keepdims=True)).astype(BF))
            sms.append(sm.astype(BF))
        dv = [dot_nn(sms[h], dos[h]) for h in range(heads)]
        dk = [dot_nn(dss[h], qs[h]) for h in range(heads)]
        dq = [dot_tn(dss[h], ks[h]) * SCALE for h in range(heads)]
        return dq, dk, dv

    def one_clip(c, first):
        last = first + lens[seq, c]
        w0 = clip_start(first, length)
        dq, dk, dv = attend_back(w0, WINDOW, w0, WINDOW, first, last)
        new = jnp.concatenate(
            [part[h].astype(BF) for h in range(heads) for part in (dq, dk, dv)], axis=1
        )
        row_at = lax.broadcasted_iota(jnp.int32, (WINDOW, 1), 0) + w0
        old = dq_s[pl.ds(w0, WINDOW), :]
        dq_s[pl.ds(w0, WINDOW), :] = jnp.where(row_at >= first, new, old)
        return last

    first = lax.fori_loop(0, clips, one_clip, jnp.int32(0), unroll=2)
    k0, step, tiles = pad_range(clips, length)
    k_rows = length - k0
    kv_acc[...] = jnp.zeros_like(kv_acc)

    def pad_tile(i, carry):
        at = pl.multiple_of(i * step, 16)
        dq, dk, dv = attend_back(k0 + at, step, k0, k_rows, first, length)
        for h in range(heads):
            kv_acc[2 * h] += dk[h]
            kv_acc[2 * h + 1] += dv[h]
            q_acc[h, pl.ds(at, step), :] = dq[h].astype(BF)
        return carry

    lax.fori_loop((first - k0) // step, tiles, pad_tile, jnp.int32(0))
    new = jnp.concatenate(
        [
            part.astype(BF)
            for h in range(heads)
            for part in (q_acc[h], kv_acc[2 * h], kv_acc[2 * h + 1])
        ],
        axis=1,
    )
    row_at = lax.broadcasted_iota(jnp.int32, (k_rows, 1), 0) + k0
    dq_s[k0:, :] = jnp.where(row_at >= first, new, dq_s[k0:, :])
    for k in sums:
        vec_o[k : k + 1, :] = sums[k]
    put.wait()


def stage_grads(first_seq, last_seq, rows, blocks, meta, *refs):
    ag_s, dq_s, vec_a, normed_h, att_h, w_h, g1, b1 = refs[:8]
    refs = refs[8:]
    if not first_seq:
        old_qkv, old_out, old_vec = refs[:3]
        refs = refs[3:]
    if last_seq:
        vec_b, refs = refs[0], refs[1:]
    keep_o, send_o = refs[:2]
    refs = refs[2:]
    if last_seq:
        grads_o, refs = refs[0], refs[1:]
    else:
        qkv_o, out_o, vec_o = refs[:3]
        refs = refs[3:]
    normed, att, w, in_sem = refs
    get = copies(in_sem, (w_h, w), (normed_h, normed), (att_h, att))
    d = g1.shape[1]
    sums = {k: vec_a[k : k + 1, :] for k in (V_GAIN2, V_SHIFT2, V_OUT)}
    sums[V_GAIN1] = jnp.zeros((1, d), F32)
    sums[V_SHIFT1] = jnp.zeros((1, d), F32)
    for c in get:
        c.wait()
    grad_out = dot_tn(att[...], ag_s[...])
    grad_qkv = dot_tn(dq_s[...], normed[...])
    qkv_sum = jnp.sum(dq_s[...].astype(F32), axis=0, keepdims=True)
    for p in range(4):
        r0 = block_start(meta, p, rows)
        ng = dot_nn(dq_s[pl.ds(r0, rows), :], w[...])
        sums[V_SHIFT1] += jnp.sum(ng, axis=0, keepdims=True)
        sums[V_GAIN1] += jnp.sum(ng * normed[pl.ds(r0, rows), :].astype(F32), axis=0, keepdims=True)
        (keep_o, send_o)[p & 1][chip_slot(meta, p)] = ng.astype(BF)
    sums[V_GAIN1] = (sums[V_GAIN1] - b1[...] * sums[V_SHIFT1]) / g1[...]
    sums[V_QKV] = jnp.concatenate([qkv_sum, jnp.zeros((1, d - qkv_sum.shape[1]), F32)], axis=1)
    if not first_seq:
        grad_qkv = grad_qkv + old_qkv[...]
        grad_out = grad_out + old_out[...]
        for k in sums:
            sums[k] += old_vec[k : k + 1, :]
    if not last_seq:
        qkv_o[...] = grad_qkv
        out_o[...] = grad_out
        for k in sums:
            vec_o[k : k + 1, :] = sums[k]
        return
    for k in (V_UP, V_DOWN):
        sums[k] = vec_b[k : k + 1, :]
    each = d // blocks
    wide = grad_qkv.shape[0]
    for j in range(blocks):
        at = lax.bitwise_xor(meta[1], jnp.int32(j))
        r = j * each
        part = grad_qkv[r : r + each] if r < wide else grad_out[r - wide : r - wide + each]
        grads_o[at, :each, :] = part.astype(BF)
        grads_o[at, each:, :] = jnp.broadcast_to(sums[j], (VEC_ROWS, d)).astype(BF)


def run_a(seq, heads, length, rows, d, meta, lens, xs, g1, b1, w, bias, wo):
    wide, attn = 3 * heads * HEAD_DIM, heads * HEAD_DIM
    sd = jax.ShapeDtypeStruct
    return call(
        functools.partial(stage_a, seq, heads, length, rows),
        [sd((length, d), BF), sd((length, wide), BF), sd((length, attn), BF)]
        + [sd((2, rows, d), BF)] * 2,
        [meta, lens],
        [*xs, g1, b1, w, bias, wo],
        [vm(4, rows, d), vm(wide, d), vm(attn, d), vm(length, d), vm(length, wide)]
        + [vm(length, attn), sem(6), sem(3)],
        LIMIT_A,
        2 * length * d * (wide + attn) * 2,
        (0, 1, 2, 3, 6, 8),
        (0, 1, 2),
    )


def run_b(seq, first_seq, last_seq, rows, d, hidden, blocks, meta, xs, ms, cots, ob, g2, b2, wu, hb, wd, carry):
    sd = jax.ShapeDtypeStruct
    length = 4 * rows
    each = d // blocks
    return call(
        functools.partial(stage_b, seq, first_seq, last_seq, rows, blocks),
        [sd((2, rows, d), BF)] * 4
        + [sd((length, d), BF), sd((length, 1), F32)]
        + (
            [sd((blocks, 2 * each, d), BF)]
            if last_seq
            else [sd((d, hidden), F32), sd((hidden, d), F32)]
        )
        + [sd((8, d), F32)],
        [meta],
        [*xs, *ms, *cots, ob, g2, b2, wu, hb, wd, *carry],
        [pltpu.VMEM((length, d), BF), pltpu.VMEM((length, hidden), BF)]
        + [pltpu.VMEM((length, hidden), BF), pltpu.VMEM((length, d), BF)]
        + [vm(4, rows, d), vm(d, hidden), vm(hidden, d), vm(2, rows, d), vm(2, rows, d)]
        + [vm(length, d), vm(length, 1, dtype=F32), sem(10), sem(4)],
        LIMIT_B,
        12 * length * d * hidden,
        (0, 1, 2, 3, 6, 7, 8, 9, 13, 15),
        (0, 1, 4, 5),
    )


def run_c(seq, heads, length, rows, d, clips, meta, lens, arrays):
    sd = jax.ShapeDtypeStruct
    wide, attn = 3 * heads * HEAD_DIM, heads * HEAD_DIM
    k_rows = length - pad_range(clips, length)[0]
    return call(
        functools.partial(stage_c, seq, heads, length, rows),
        [sd((rows, d), F32), sd((length, d), BF), sd((length, wide), BF), sd((8, d), F32)],
        [meta, lens],
        arrays,
        [vm(length, attn), vm(2 * heads, k_rows, HEAD_DIM, dtype=F32), vm(heads, k_rows, HEAD_DIM)]
        + [vm(4, rows, d), vm(length, d), vm(length, 1, dtype=F32), vm(attn, d)]
        + [vm(length, wide), vm(rows, d, dtype=F32), sem(14), sem(1)],
        LIMIT_C,
        4 * length * d * attn * 2,
        (2, 3, 4, 5, 6, 7, 9, 10),
        (0,),
    )


def run_grads(first_seq, last_seq, rows, blocks, wide, meta, arrays):
    sd = jax.ShapeDtypeStruct
    length, d = arrays[0].shape
    attn = d - wide
    each = d // blocks
    return call(
        functools.partial(stage_grads, first_seq, last_seq, rows, blocks),
        [sd((2, rows, d), BF), sd((2, rows, d), BF)]
        + (
            [sd((blocks, each + VEC_ROWS, d), BF)]
            if last_seq
            else [sd((wide, d), F32), sd((attn, d), F32), sd((8, d), F32)]
        ),
        [meta],
        arrays,
        [vm(length, d), vm(length, attn), vm(wide, d), sem(3)],
        LIMIT_A,
        4 * length * d * d,
        (3, 4, 5),
        (),
    )


def stage_d(seq, meta, x, mg, keep, got, far, g1, out):
    xhat, inv = norm_rows(x[seq].astype(F32))
    slot = meta[0] >> 1
    n = keep[slot].astype(F32) + got[slot].astype(F32) + far[...].astype(F32)
    e = n * g1[...]
    mean_e = jnp.mean(e, axis=-1, keepdims=True)
    mean_ex = jnp.mean(e * xhat, axis=-1, keepdims=True)
    out[...] = (mg[...] + inv * (e - mean_e - xhat * mean_ex)).astype(BF)


def unpack_ff(each, d, near, far, meta, up_o, down_o):
    for j in range(8):
        at = lax.bitwise_xor(meta[1], jnp.int32(j))
        rows = slice(j * each, j * each + each)

        @pl.when(at < 4)
        def _():
            block = near[jnp.minimum(at, 3)].astype(F32)
            up_o[rows, :] = block[:each]
            down_o[rows, :] = block[each:]

        @pl.when(at >= 4)
        def _():
            block = far[jnp.maximum(at - 4, 0)].astype(F32)
            up_o[rows, :] = block[:each]
            down_o[rows, :] = block[each:]


def unpack_attn(each, wide, near, far, meta, qkv_o, out_o, vec_o):
    for j in range(8):
        at = lax.bitwise_xor(meta[1], jnp.int32(j))
        r = j * each

        def put(block):
            if r < wide:
                qkv_o[r : r + each, :] = block[:each]
            else:
                out_o[r - wide : r - wide + each, :] = block[:each]
            vec_o[j : j + 1, :] = block[each : each + 1, :]

        @pl.when(at < 4)
        def _():
            put(near[jnp.minimum(at, 3)].astype(F32))

        @pl.when(at >= 4)
        def _():
            put(far[jnp.maximum(at - 4, 0)].astype(F32))


def on_device(
    tokens,
    clip_lengths,
    cotangent,
    query_key_value_weight,
    qv_bias,
    output_weight,
    out_bias,
    gain1,
    shift1,
    gain2,
    shift2,
    up_weight,
    hidden_bias,
    down_weight,
    down_bias,
):
    n_dp = lax.axis_size("dp")
    n_tensor = lax.axis_size("tensor")
    seqs, rows, d = tokens.shape
    length = rows * n_tensor
    heads = output_weight.shape[0] // HEAD_DIM
    wide = 3 * HEAD_DIM * heads
    hidden = up_weight.shape[1]
    blocks = 8
    each = d // blocks

    def core_swap(v):
        return lax.ppermute(v, "tensor", [(t, t ^ 1) for t in range(n_tensor)])

    def chip_swap(v):
        return lax.ppermute(v, "tensor", [(t, t ^ 2) for t in range(n_tensor)])

    t = lax.axis_index("tensor")
    dp_at = lax.axis_index("dp")
    orders = ((0, 1, 2), (1, 0, 2))
    if n_dp == 8:

        def place(order):
            return sum(((dp_at >> order[k]) & 1) << (2 - k) for k in range(3))

        label = jnp.where(t % 2 == 0, place(orders[0]), place(orders[1]))
    else:
        label = jnp.zeros_like(dp_at)
    meta = jnp.stack([t, label]).astype(jnp.int32)

    def add(a, b):
        return (a.astype(F32) + b.astype(F32)).astype(BF)

    def after(value, *others):
        return lax.optimization_barrier((value, others))[0]

    def step_perm(k):
        pairs = []
        for dev in range(n_dp):
            for s in range(n_tensor):
                other = dev ^ (1 << orders[s % 2][k])
                pairs.append((dev * n_tensor + s, other * n_tensor + s))
        return pairs

    def reduce_get(held, k):
        return lax.ppermute(held[held.shape[0] // 2 :], ("dp", "tensor"), step_perm(k))

    def gather_step(held, k):
        return lax.ppermute(held, ("dp", "tensor"), step_perm(k))

    def after(value, *others):
        return lax.optimization_barrier((value, others))[0]

    def step_perm(k):
        pairs = []
        for dev in range(n_dp):
            for s in range(n_tensor):
                other = dev ^ (1 << orders[s % 2][k])
                pairs.append((dev * n_tensor + s, other * n_tensor + s))
        return pairs

    def reduce_get(held, k):
        return lax.ppermute(held[held.shape[0] // 2 :], ("dp", "tensor"), step_perm(k))

    def reduce_step(held, k):
        return add(held[: held.shape[0] // 2], reduce_get(held, k))

    def gather_step(held, k):
        return lax.ppermute(held, ("dp", "tensor"), step_perm(k))

    def gather_all(held):
        for k in (2, 1):
            held = jnp.concatenate([held, gather_step(held, k)], axis=0)
        return held, gather_step(held, 0)

    def after(value, *others):
        return lax.optimization_barrier((value, others))[0]

    def step_perm(k):
        pairs = []
        for dev in range(n_dp):
            for s in range(n_tensor):
                other = dev ^ (1 << orders[s % 2][k])
                pairs.append((dev * n_tensor + s, other * n_tensor + s))
        return pairs

    def all_reduce(buf):
        if n_dp != 8:
            full = lax.psum(buf, "dp")
            return full[:4], full[4:]
        held = buf
        for k in range(3):
            half = held.shape[0] // 2
            got = lax.ppermute(held[half:], ("dp", "tensor"), step_perm(k))
            held = add(held[:half], got)
        for k in (2, 1):
            got = lax.ppermute(held, ("dp", "tensor"), step_perm(k))
            held = jnp.concatenate([held, got], axis=0)
        return held, lax.ppermute(held, ("dp", "tensor"), step_perm(0))

    def row(v):
        return v.reshape(1, -1)

    pairs = qv_bias.reshape(heads, 2, HEAD_DIM)
    bias = row(jnp.stack([pairs[:, 0], jnp.zeros_like(pairs[:, 0]), pairs[:, 1]], axis=1))
    g1, b1, g2, b2 = row(gain1), row(shift1), row(gain2), row(shift2)
    ob, hb = row(out_bias), row(hidden_bias)
    chip_at = t >> 1

    w_t = query_key_value_weight.T

    def spread(v, *first):
        near = core_swap(v)
        across = after(chip_swap(v), *first)
        return [v, near, across, core_swap(across)]

    def chip_sum(keep, send):
        return add(keep, core_swap(send))

    def all_rows(chip, far):
        own = add(chip, far)
        return [own, core_swap(own)]

    def peer_rows(keep, got):
        return add(keep[1 - chip_at], got[1 - chip_at])

    xs = spread(tokens, g1, b1, g2, b2, ob, hb, bias, meta)
    cot_near = core_swap(cotangent)
    beside = chip_swap(cotangent)

    kept, chips, fars = [], [], []
    for s in range(seqs):
        outs = run_a(
            s, heads, length, rows, d, meta, clip_lengths, after(xs, *chips[-1:]), g1, b1,
            w_t, bias, output_weight,
        )
        kept.append(outs[:3])
        if s == 0:
            beside = after(beside, outs[3])
            cots = [cotangent, cot_near, beside, core_swap(beside)]
        chips.append(chip_sum(outs[3], after(outs[4], beside)))
        beside = chip_swap(chips[s])
        fars.append(beside)

    mids, stats, ff_keep, ff_send, n_chips, n_fars = [], [], [], [], [], []
    carry = []
    for s in range(seqs):
        mids.append(all_rows(chips[s], fars[s]))
        outs = run_b(
            s, s == 0, s == seqs - 1, rows, d, hidden, blocks, meta, xs,
            after(mids[s], *(chips[-1:] + n_chips[-1:])), cots,
            ob, g2, b2, up_weight, hb, down_weight, carry,
        )
        n_chips.append(chip_sum(outs[2], after(outs[3], beside)))
        beside = chip_swap(n_chips[s])
        n_fars.append(beside)
        ff_keep.append(outs[0])
        ff_send.append(outs[1])
        stats.append(outs[4:6])
        carry = outs[6:]
    ff_grads, vec_b = carry

    moves = [("halve", 0), ("halve", 1), ("halve", 2), ("double", 2), ("double", 1)]

    def send_move(held):
        kind, k = moves[0]
        return reduce_get(held, k) if kind == "halve" else gather_step(held, k)

    def take_move(held, part):
        if moves.pop(0)[0] == "halve":
            return add(held[: held.shape[0] // 2], part)
        return jnp.concatenate([held, part], axis=0)

    by_hand = n_dp == 8 and seqs == 2
    backs, peers, far_rows = [], [], []
    carry = []
    held = ff_grads
    for s in range(seqs):
        last = s == seqs - 1
        n_now = after(all_rows(n_chips[s], n_fars[s]), *n_chips[-1:], held)
        mg, ag, dq, vec_a = run_c(
            s, heads, length, rows, d, clip_lengths.shape[1], meta, clip_lengths,
            [*n_now, *cots, *stats[s], g2, output_weight, kept[s][1]],
        )
        if by_hand:
            held = take_move(held, after(send_move(held), dq))
            dq = after(dq, held)
        outs = run_grads(
            s == 0, last, rows, blocks, wide, meta,
            [ag, dq, vec_a, kept[s][0], kept[s][2], w_t, g1, b1, *carry] + ([vec_b] if last else []),
        )
        keep, send = outs[:2]
        carry = outs[2:]
        waits = [] if last else [beside]
        if by_hand and last:
            part = send_move(held)
        elif by_hand:
            held = take_move(held, after(send_move(held), send))
        got = core_swap(after(send, *waits))
        peers.append(peer_rows(keep, got))
        beside = chip_swap(peers[s])
        far_rows.append(beside)
        backs.append((mg, keep, got))
    at_grads = carry[0]
    ff_got = [core_swap(after(send, peers[-1])) for send in ff_send]
    ff_peers = [peer_rows(keep, got) for keep, got in zip(ff_keep, ff_got)]
    ff_far_rows = [chip_swap(v) for v in ff_peers]
    whole = pl.BlockSpec(memory_space=pltpu.VMEM)

    def input_rows(s):
        return pl.pallas_call(
            functools.partial(stage_d, s),
            out_shape=jax.ShapeDtypeStruct((rows, d), BF),
            in_specs=[pl.BlockSpec(memory_space=pltpu.SMEM)] + [whole] * 6,
            out_specs=whole,
            compiler_params=pltpu.CompilerParams(vmem_limit_bytes=16 << 20),
        )(meta, tokens, *backs[s], far_rows[s], g1)

    def output_rows(s):
        ff = ff_keep[s][chip_at].astype(F32) + ff_got[s][chip_at].astype(F32)
        middle = tokens[s].astype(F32) + mids[s][0][chip_at].astype(F32) + out_bias
        return (middle + (ff + ff_far_rows[s].astype(F32) + down_bias)).astype(BF)

    input_grad = jnp.stack([input_rows(s) for s in range(seqs)])
    block_out = jnp.stack([output_rows(s) for s in range(seqs)])
    if by_hand:
        at_held = add(at_grads[:4], after(reduce_get(at_grads, 0), *ff_peers))
        held = take_move(held, after(part, at_held))
        part = send_move(held)
        at_held = add(at_held[:2], reduce_get(at_held, 1))
        at_held = add(at_held[:1], reduce_get(at_held, 2))
        ff_near = take_move(held, after(part, at_held, input_grad))
        ff_far = gather_step(ff_near, 0)
        at_held = jnp.concatenate([at_held, gather_step(at_held, 2)], axis=0)
        part = after(gather_step(at_held, 1), block_out)
        at_near = jnp.concatenate([at_held, part], axis=0)
        at_far = gather_step(at_near, 0)
    else:
        ff_sum, at_sum = lax.psum((ff_grads, at_grads), "dp")
        ff_near, ff_far, at_near, at_far = ff_sum[:4], ff_sum[4:], at_sum[:4], at_sum[4:]

    def unpack(body, near, far, out_shape):
        whole = pl.BlockSpec(memory_space=pltpu.VMEM)
        return pl.pallas_call(
            body,
            out_shape=out_shape,
            in_specs=[whole, whole, pl.BlockSpec(memory_space=pltpu.SMEM)],
            out_specs=[whole] * len(out_shape),
            compiler_params=pltpu.CompilerParams(vmem_limit_bytes=24 << 20),
        )(near, far, meta)

    grad_up, grad_down = unpack(
        functools.partial(unpack_ff, each, d),
        ff_near,
        ff_far,
        [jax.ShapeDtypeStruct((d, hidden), F32), jax.ShapeDtypeStruct((hidden, d), F32)],
    )
    at_far = after(at_far, block_out, input_grad, grad_up, grad_down)

    def vec_row(j):
        at = label ^ j
        return jnp.where(at < 4, at_near[at & 3, each], at_far[at & 3, each]).astype(F32)

    norm1 = jnp.stack([vec_row(V_GAIN1), vec_row(V_SHIFT1)])
    across = lax.ppermute(norm1, "tensor", [(t, t ^ 3) for t in range(n_tensor)])
    norm1 = (norm1 + core_swap(norm1)) + (chip_swap(norm1) + across)
    grad_qkv, grad_out, vec = unpack(
        functools.partial(unpack_attn, each, wide),
        at_near,
        at_far,
        [
            jax.ShapeDtypeStruct((wide, d), F32),
            jax.ShapeDtypeStruct((d - wide, d), F32),
            jax.ShapeDtypeStruct((8, d), F32),
        ],
    )
    qkv_sum = vec[V_QKV, :wide].reshape(heads, 3, HEAD_DIM)
    return (
        block_out,
        input_grad,
        grad_qkv.T,
        qkv_sum[:, ::2].reshape(-1),
        grad_out,
        vec[V_OUT],
        norm1[0],
        norm1[1],
        vec[V_GAIN2],
        vec[V_SHIFT2],
        grad_up,
        vec[V_UP],
        grad_down,
        vec[V_DOWN],
    )


def solution(mesh):
    placed = (
        P("dp", "tensor", None),
        P("dp", None),
        P("dp", "tensor", None),
        P(None, "tensor"),
        P("tensor"),
        P("tensor", None),
        P(),
        P(),
        P(),
        P(),
        P(),
        P(None, "tensor"),
        P("tensor"),
        P("tensor", None),
        P(),
    )
    return jax.shard_map(
        on_device,
        mesh=mesh,
        in_specs=placed,
        out_specs=(
            P("dp", "tensor", None),
            P("dp", "tensor", None),
            P(None, "tensor"),
            P("tensor"),
            P("tensor", None),
            P(),
            P(),
            P(),
            P(),
            P(),
            P(None, "tensor"),
            P("tensor"),
            P("tensor", None),
            P(),
        ),
        check_vma=False,
    )
```

```python
import functools

import jax
import jax.numpy as jnp
from jax import lax
from jax.experimental import pallas as pl
from jax.experimental.pallas import tpu as pltpu
from jax.sharding import PartitionSpec as P

HEAD_DIM = 64
EPS = 1e-06
SCALE = HEAD_DIM ** (-0.5)
BF = jnp.bfloat16
F32 = jnp.float32
LONGEST = 170
WINDOW = 192
MASKED = -1e30
VEC_ROWS = 16
COST_SCALE = 1
LIMIT_A, LIMIT_B, LIMIT_C = 20, 36, 32

V_UP, V_DOWN, V_GAIN2, V_SHIFT2, V_OUT, V_GAIN1, V_SHIFT1, V_QKV = range(8)


def dot_nn(a, b):
    return lax.dot_general(a, b, (((1,), (0,)), ((), ())), preferred_element_type=F32)


def dot_nt(a, b):
    return lax.dot_general(a, b, (((1,), (1,)), ((), ())), preferred_element_type=F32)


def dot_tn(a, b):
    return lax.dot_general(a, b, (((0,), (0,)), ((), ())), preferred_element_type=F32)


def call(body, out_shape, scalars, arrays, scratch, limit_mb, flops, far_in, far_out):
    whole = pl.BlockSpec(memory_space=pltpu.VMEM)
    far = pl.BlockSpec(memory_space=pltpu.HBM)
    moved = sum(a.size * a.dtype.itemsize for a in arrays) + sum(
        o.size * o.dtype.itemsize for o in out_shape
    )
    return pl.pallas_call(
        body,
        out_shape=[pltpu.HBM(o.shape, o.dtype) if i in far_out else o for i, o in enumerate(out_shape)],
        in_specs=[pl.BlockSpec(memory_space=pltpu.SMEM)] * len(scalars)
        + [far if i in far_in else whole for i in range(len(arrays))],
        out_specs=[far if i in far_out else whole for i in range(len(out_shape))],
        scratch_shapes=scratch,
        compiler_params=pltpu.CompilerParams(vmem_limit_bytes=limit_mb << 20),
        cost_estimate=pl.CostEstimate(flops=flops * COST_SCALE, transcendentals=0, bytes_accessed=moved),
    )(
        *scalars,
        *[
            pltpu.with_memory_space_constraint(a, pltpu.HBM) if i in far_in else a
            for i, a in enumerate(arrays)
        ],
    )


def sem(n):
    return pltpu.SemaphoreType.DMA((n,))


def vm(*shape, dtype=BF):
    return pltpu.VMEM(shape, dtype)


def copies(done, *pairs):
    made = [pltpu.make_async_copy(src, dst, done.at[i]) for i, (src, dst) in enumerate(pairs)]
    for c in made:
        c.start()
    return made


def block_start(meta, p, rows):
    return pl.multiple_of(lax.bitwise_xor(meta[0], jnp.int32(p)) * rows, rows)


def chip_slot(meta, p):
    return lax.bitwise_xor(meta[0] >> 1, jnp.int32(p >> 1))


def norm_rows(x):
    mean = jnp.mean(x, axis=-1, keepdims=True)
    centred = x - mean
    var = jnp.mean(centred * centred, axis=-1, keepdims=True)
    inv = lax.rsqrt(var + EPS)
    return centred * inv, inv


def phi_parts(u):
    cdf = 0.5 * (1.0 + lax.erf(u * 0.7071067811865476))
    return cdf, jnp.exp(u * u * -0.5) * 0.3989422804014327


def pad_range(clips, length):
    k0 = clips * 100 // 64 * 64
    step = 112 if (length - k0) % 112 == 0 else 64
    return k0, step, (length - k0) // step


def clip_start(first, length):
    return pl.multiple_of(jnp.minimum(first // 16 * 16, length - WINDOW), 16)


def stage_a(seq, heads, length, rows, meta, lens, *refs):
    x_refs, (g1, b1, w_h, bias, wo_h), refs = refs[:4], refs[4:9], refs[9:]
    normed_h, qkv_h, att_h, keep_o, send_o, x_s, w, wo, normed_o, qkv_o, att_o, in_sem, out_sem = refs
    clips = lens.shape[1]
    get = copies(
        in_sem,
        (x_refs[0].at[seq], x_s.at[0]),
        (w_h, w),
        *[(x_refs[p].at[seq], x_s.at[p]) for p in range(1, 4)],
        (wo_h, wo),
    )
    get[1].wait()
    for p in range(4):
        r0 = block_start(meta, p, rows)
        get[p + (p > 0)].wait()
        xhat, _ = norm_rows(x_s[p].astype(F32))
        nb = (xhat * g1[...] + b1[...]).astype(BF)
        normed_o[pl.ds(r0, rows), :] = nb
        qkv_o[pl.ds(r0, rows), :] = (dot_nt(nb, w[...]) + bias[...]).astype(BF)

    put = copies(out_sem, (normed_o, normed_h), (qkv_o, qkv_h))

    def attend(q0, q_rows, k0, k_rows, first, last):
        key_at = lax.broadcasted_iota(jnp.int32, (1, k_rows), 1) + k0
        allowed = (key_at >= first) & (key_at < last)
        row_at = lax.broadcasted_iota(jnp.int32, (q_rows, 1), 0) + q0
        scores, outs = [], []
        for h in range(heads):
            col = h * 3 * HEAD_DIM
            q = qkv_o[pl.ds(q0, q_rows), col : col + HEAD_DIM] * BF(SCALE)
            k = qkv_o[pl.ds(k0, k_rows), col + HEAD_DIM : col + 2 * HEAD_DIM]
            scores.append(dot_nt(q, k))
        for h in range(heads):
            v = qkv_o[pl.ds(k0, k_rows), (h * 3 + 2) * HEAD_DIM : (h * 3 + 3) * HEAD_DIM]
            s = jnp.where(allowed, scores[h], MASKED)
            e = jnp.exp(s - jnp.max(s, axis=1, keepdims=True))
            probs = (e * (1.0 / jnp.sum(e, axis=1, keepdims=True))).astype(BF)
            outs.append(dot_nn(probs, v).astype(BF))
        new = jnp.concatenate(outs, axis=1)
        old = att_o[pl.ds(q0, q_rows), :]
        att_o[pl.ds(q0, q_rows), :] = jnp.where(row_at >= first, new, old)

    def one_clip(c, first):
        last = first + lens[seq, c]
        w0 = clip_start(first, length)
        attend(w0, WINDOW, w0, WINDOW, first, last)
        return last

    first = lax.fori_loop(0, clips, one_clip, jnp.int32(0), unroll=2)
    k0, step, tiles = pad_range(clips, length)

    def pad_tile(i, carry):
        attend(pl.multiple_of(k0 + i * step, 16), step, k0, length - k0, first, length)
        return carry

    lax.fori_loop((first - k0) // step, tiles, pad_tile, jnp.int32(0))

    att_put = pltpu.make_async_copy(att_o, att_h, out_sem.at[2])
    att_put.start()
    get[5].wait()
    for p in range(4):
        r0 = block_start(meta, p, rows)
        part = dot_nn(att_o[pl.ds(r0, rows), :], wo[...]).astype(BF)
        (keep_o, send_o)[p & 1][chip_slot(meta, p)] = part
    for c in [*put, att_put]:
        c.wait()


def stage_b(seq, first_seq, last_seq, rows, blocks, meta, *refs):
    xs, ms, cots, refs = refs[:4], refs[4:6], refs[6:10], refs[10:]
    ob, g2, b2, wu_h, hb, wd_h = refs[:6]
    refs = refs[6:]
    if not first_seq:
        old_up, old_down, old_vec = refs[:3]
        refs = refs[3:]
    keep_fh, send_fh, keep_n, send_n, xhat_h, inv_h = refs[:6]
    refs = refs[6:]
    if last_seq:
        grads_o, vec_o = refs[:2]
        refs = refs[2:]
    else:
        up_o, down_o, vec_o = refs[:3]
        refs = refs[3:]
    n2_s, act_s, ug_s, cot_s, x_s, wu, wd, keep_f, send_f, xhat_o, inv_o, in_sem, out_sem = refs
    pieces = []
    for p in range(4):
        here = pl.ds(p * rows, rows)
        pieces += [(xs[p].at[seq], x_s.at[p]), (cots[p].at[seq], cot_s.at[here, :])]
        if p == 0:
            pieces += [(wu_h, wu), (wd_h, wd)]
    get = copies(in_sem, *pieces)
    get[2].wait()
    get[3].wait()
    d = wu.shape[0]
    up_sum = jnp.zeros((1, wu.shape[1]), F32)
    down_sum = jnp.zeros((1, d), F32)
    for p in range(4):
        slot = chip_slot(meta, p)
        here = slice(p * rows, p * rows + rows)
        for c in get[2 * p + 2 * (p > 0) : 2 * p + 2 * (p > 0) + 2]:
            c.wait()
        mid = x_s[p].astype(F32) + ms[p & 1][slot].astype(F32) + ob[...]
        xhat, inv = norm_rows(mid)
        xhat_o[here, :] = xhat.astype(BF)
        inv_o[here, :] = inv
        n2 = (xhat * g2[...] + b2[...]).astype(BF)
        n2_s[here, :] = n2
        u = dot_nn(n2, wu[...]) + hb[...]
        cdf, pdf = phi_parts(u)
        act = (u * cdf).astype(BF)
        act_s[here, :] = act
        (keep_f, send_f)[p & 1][slot] = dot_nn(act, wd[...]).astype(BF)
        cot = cot_s[here, :]
        down_sum = down_sum + jnp.sum(cot.astype(F32), axis=0, keepdims=True)
        ug = (dot_nt(cot, wd[...]) * (cdf + u * pdf)).astype(BF)
        ug_s[here, :] = ug
        up_sum = up_sum + jnp.sum(ug.astype(F32), axis=0, keepdims=True)
        (keep_n, send_n)[p & 1][slot] = dot_nt(ug, wu[...]).astype(BF)
    put = copies(
        out_sem, (keep_f, keep_fh), (send_f, send_fh), (xhat_o, xhat_h), (inv_o, inv_h)
    )
    grad_up = dot_tn(n2_s[...], ug_s[...])
    grad_down = dot_tn(act_s[...], cot_s[...])
    if not first_seq:
        grad_up = grad_up + old_up[...]
        grad_down = grad_down + old_down[...]
        up_sum = up_sum + old_vec[V_UP : V_UP + 1, :]
        down_sum = down_sum + old_vec[V_DOWN : V_DOWN + 1, :]
    vec_o[V_UP : V_UP + 1, :] = up_sum
    vec_o[V_DOWN : V_DOWN + 1, :] = down_sum
    if not last_seq:
        up_o[...] = grad_up
        down_o[...] = grad_down
    else:
        each = d // blocks
        for j in range(blocks):
            at = lax.bitwise_xor(meta[1], jnp.int32(j))
            grads_o[at, :each, :] = grad_up[j * each : j * each + each].astype(BF)
            grads_o[at, each:, :] = grad_down[j * each : j * each + each].astype(BF)
    for c in put:
        c.wait()


def stage_c(seq, heads, length, rows, meta, lens, *refs):
    ns, cots, refs = refs[:2], refs[2:6], refs[6:]
    xhat_h, inv_h, g2, wo_h, qkv_h, mg_h, ag_s, dq_s, vec_o = refs[:9]
    da_s, kv_acc, q_acc, cot_s, xhat_i, inv_i, wo, qkv, mg_o, in_sem, out_sem = refs[9:]
    pieces = []
    for p in range(4):
        here = pl.ds(p * rows, rows)
        pieces += [(cots[p].at[seq], cot_s.at[p])]
        pieces += [(ref.at[here, :], dst.at[here, :]) for ref, dst in ((xhat_h, xhat_i), (inv_h, inv_i))]
        if p == 0:
            pieces += [(wo_h, wo)]
    get = copies(in_sem, *pieces, (qkv_h, qkv))
    get[3].wait()
    clips = lens.shape[1]
    d = g2.shape[1]
    sums = {k: jnp.zeros((1, d), F32) for k in (V_GAIN2, V_SHIFT2, V_OUT)}
    for p in range(4):
        slot = chip_slot(meta, p)
        here = slice(p * rows, p * rows + rows)
        r0 = block_start(meta, p, rows)
        for c in get[3 * p + (p > 0) : 3 * p + (p > 0) + 3]:
            c.wait()
        n = ns[p & 1][slot].astype(F32)
        xhat = xhat_i[here, :].astype(F32)
        e = n * g2[...]
        mean_e = jnp.mean(e, axis=-1, keepdims=True)
        mean_ex = jnp.mean(e * xhat, axis=-1, keepdims=True)
        mg = cot_s[p].astype(F32) + inv_i[here, :] * (e - mean_e - xhat * mean_ex)
        if p == 0:
            mg_o[...] = mg
        ag = mg.astype(BF)
        ag_s[pl.ds(r0, rows), :] = ag
        da_s[pl.ds(r0, rows), :] = dot_nt(ag, wo[...]).astype(BF)
        sums[V_GAIN2] += jnp.sum(n * xhat, axis=0, keepdims=True)
        sums[V_SHIFT2] += jnp.sum(n, axis=0, keepdims=True)
        sums[V_OUT] += jnp.sum(ag.astype(F32), axis=0, keepdims=True)

    put = pltpu.make_async_copy(mg_o, mg_h, out_sem.at[0])
    put.start()
    get[13].wait()

    def attend_back(q0, q_rows, k0, k_rows, first, last):
        q_at = lax.broadcasted_iota(jnp.int32, (k_rows, q_rows), 1) + q0
        k_at = lax.broadcasted_iota(jnp.int32, (k_rows, q_rows), 0) + k0
        allowed = (k_at >= first) & (k_at < last) & (q_at >= first) & (q_at < last)
        qs, ks, dos, scores, prob_grads, sms, dss = [], [], [], [], [], [], []
        for h in range(heads):
            col = h * 3 * HEAD_DIM
            qs.append(qkv[pl.ds(q0, q_rows), col : col + HEAD_DIM] * BF(SCALE))
            ks.append(qkv[pl.ds(k0, k_rows), col + HEAD_DIM : col + 2 * HEAD_DIM])
            v = qkv[pl.ds(k0, k_rows), col + 2 * HEAD_DIM : col + 3 * HEAD_DIM]
            dos.append(da_s[pl.ds(q0, q_rows), h * HEAD_DIM : h * HEAD_DIM + HEAD_DIM])
            scores.append(dot_nt(ks[h], qs[h]))
            prob_grads.append(dot_nt(v, dos[h]))
        for h in range(heads):
            s = jnp.where(allowed, scores[h], MASKED)
            e = jnp.exp(s - jnp.max(s, axis=0, keepdims=True))
            sm = jnp.where(allowed, e * (1.0 / jnp.sum(e, axis=0, keepdims=True)), 0.0)
            t = sm * prob_grads[h]
            dss.append((t - sm * jnp.sum(t, axis=0, keepdims=True)).astype(BF))
            sms.append(sm.astype(BF))
        dv = [dot_nn(sms[h], dos[h]) for h in range(heads)]
        dk = [dot_nn(dss[h], qs[h]) for h in range(heads)]
        dq = [dot_tn(dss[h], ks[h]) * SCALE for h in range(heads)]
        return dq, dk, dv

    def one_clip(c, first):
        last = first + lens[seq, c]
        w0 = clip_start(first, length)
        dq, dk, dv = attend_back(w0, WINDOW, w0, WINDOW, first, last)
        new = jnp.concatenate(
            [part[h].astype(BF) for h in range(heads) for part in (dq, dk, dv)], axis=1
        )
        row_at = lax.broadcasted_iota(jnp.int32, (WINDOW, 1), 0) + w0
        old = dq_s[pl.ds(w0, WINDOW), :]
        dq_s[pl.ds(w0, WINDOW), :] = jnp.where(row_at >= first, new, old)
        return last

    first = lax.fori_loop(0, clips, one_clip, jnp.int32(0), unroll=2)
    k0, step, tiles = pad_range(clips, length)
    k_rows = length - k0
    kv_acc[...] = jnp.zeros_like(kv_acc)

    def pad_tile(i, carry):
        at = pl.multiple_of(i * step, 16)
        dq, dk, dv = attend_back(k0 + at, step, k0, k_rows, first, length)
        for h in range(heads):
            kv_acc[2 * h] += dk[h]
            kv_acc[2 * h + 1] += dv[h]
            q_acc[h, pl.ds(at, step), :] = dq[h].astype(BF)
        return carry

    lax.fori_loop((first - k0) // step, tiles, pad_tile, jnp.int32(0))
    new = jnp.concatenate(
        [
            part.astype(BF)
            for h in range(heads)
            for part in (q_acc[h], kv_acc[2 * h], kv_acc[2 * h + 1])
        ],
        axis=1,
    )
    row_at = lax.broadcasted_iota(jnp.int32, (k_rows, 1), 0) + k0
    dq_s[k0:, :] = jnp.where(row_at >= first, new, dq_s[k0:, :])
    for k in sums:
        vec_o[k : k + 1, :] = sums[k]
    put.wait()


def stage_grads(first_seq, last_seq, rows, blocks, meta, *refs):
    ag_s, dq_s, vec_a, normed_h, att_h, w_h, g1, b1 = refs[:8]
    refs = refs[8:]
    if not first_seq:
        old_qkv, old_out, old_vec = refs[:3]
        refs = refs[3:]
    if last_seq:
        vec_b, refs = refs[0], refs[1:]
    keep_o, send_o = refs[:2]
    refs = refs[2:]
    if last_seq:
        grads_o, refs = refs[0], refs[1:]
    else:
        qkv_o, out_o, vec_o = refs[:3]
        refs = refs[3:]
    normed, att, w, in_sem = refs
    get = copies(in_sem, (w_h, w), (normed_h, normed), (att_h, att))
    d = g1.shape[1]
    sums = {k: vec_a[k : k + 1, :] for k in (V_GAIN2, V_SHIFT2, V_OUT)}
    sums[V_GAIN1] = jnp.zeros((1, d), F32)
    sums[V_SHIFT1] = jnp.zeros((1, d), F32)
    for c in get:
        c.wait()
    grad_out = dot_tn(att[...], ag_s[...])
    grad_qkv = dot_tn(dq_s[...], normed[...])
    qkv_sum = jnp.sum(dq_s[...].astype(F32), axis=0, keepdims=True)
    for p in range(4):
        r0 = block_start(meta, p, rows)
        ng = dot_nn(dq_s[pl.ds(r0, rows), :], w[...])
        sums[V_SHIFT1] += jnp.sum(ng, axis=0, keepdims=True)
        sums[V_GAIN1] += jnp.sum(ng * normed[pl.ds(r0, rows), :].astype(F32), axis=0, keepdims=True)
        (keep_o, send_o)[p & 1][chip_slot(meta, p)] = ng.astype(BF)
    sums[V_GAIN1] = (sums[V_GAIN1] - b1[...] * sums[V_SHIFT1]) / g1[...]
    sums[V_QKV] = jnp.concatenate([qkv_sum, jnp.zeros((1, d - qkv_sum.shape[1]), F32)], axis=1)
    if not first_seq:
        grad_qkv = grad_qkv + old_qkv[...]
        grad_out = grad_out + old_out[...]
        for k in sums:
            sums[k] += old_vec[k : k + 1, :]
    if not last_seq:
        qkv_o[...] = grad_qkv
        out_o[...] = grad_out
        for k in sums:
            vec_o[k : k + 1, :] = sums[k]
        return
    for k in (V_UP, V_DOWN):
        sums[k] = vec_b[k : k + 1, :]
    each = d // blocks
    wide = grad_qkv.shape[0]
    for j in range(blocks):
        at = lax.bitwise_xor(meta[1], jnp.int32(j))
        r = j * each
        part = grad_qkv[r : r + each] if r < wide else grad_out[r - wide : r - wide + each]
        grads_o[at, :each, :] = part.astype(BF)
        grads_o[at, each:, :] = jnp.broadcast_to(sums[j], (VEC_ROWS, d)).astype(BF)


def run_a(seq, heads, length, rows, d, meta, lens, xs, g1, b1, w, bias, wo):
    wide, attn = 3 * heads * HEAD_DIM, heads * HEAD_DIM
    sd = jax.ShapeDtypeStruct
    return call(
        functools.partial(stage_a, seq, heads, length, rows),
        [sd((length, d), BF), sd((length, wide), BF), sd((length, attn), BF)]
        + [sd((2, rows, d), BF)] * 2,
        [meta, lens],
        [*xs, g1, b1, w, bias, wo],
        [vm(4, rows, d), vm(wide, d), vm(attn, d), vm(length, d), vm(length, wide)]
        + [vm(length, attn), sem(6), sem(3)],
        LIMIT_A,
        2 * length * d * (wide + attn) * 2,
        (0, 1, 2, 3, 6, 8),
        (0, 1, 2),
    )


def run_b(seq, first_seq, last_seq, rows, d, hidden, blocks, meta, xs, ms, cots, ob, g2, b2, wu, hb, wd, carry):
    sd = jax.ShapeDtypeStruct
    length = 4 * rows
    each = d // blocks
    return call(
        functools.partial(stage_b, seq, first_seq, last_seq, rows, blocks),
        [sd((2, rows, d), BF)] * 4
        + [sd((length, d), BF), sd((length, 1), F32)]
        + (
            [sd((blocks, 2 * each, d), BF)]
            if last_seq
            else [sd((d, hidden), F32), sd((hidden, d), F32)]
        )
        + [sd((8, d), F32)],
        [meta],
        [*xs, *ms, *cots, ob, g2, b2, wu, hb, wd, *carry],
        [pltpu.VMEM((length, d), BF), pltpu.VMEM((length, hidden), BF)]
        + [pltpu.VMEM((length, hidden), BF), pltpu.VMEM((length, d), BF)]
        + [vm(4, rows, d), vm(d, hidden), vm(hidden, d), vm(2, rows, d), vm(2, rows, d)]
        + [vm(length, d), vm(length, 1, dtype=F32), sem(10), sem(4)],
        LIMIT_B,
        12 * length * d * hidden,
        (0, 1, 2, 3, 6, 7, 8, 9, 13, 15),
        (0, 1, 4, 5),
    )


def run_c(seq, heads, length, rows, d, clips, meta, lens, arrays):
    sd = jax.ShapeDtypeStruct
    wide, attn = 3 * heads * HEAD_DIM, heads * HEAD_DIM
    k_rows = length - pad_range(clips, length)[0]
    return call(
        functools.partial(stage_c, seq, heads, length, rows),
        [sd((rows, d), F32), sd((length, d), BF), sd((length, wide), BF), sd((8, d), F32)],
        [meta, lens],
        arrays,
        [vm(length, attn), vm(2 * heads, k_rows, HEAD_DIM, dtype=F32), vm(heads, k_rows, HEAD_DIM)]
        + [vm(4, rows, d), vm(length, d), vm(length, 1, dtype=F32), vm(attn, d)]
        + [vm(length, wide), vm(rows, d, dtype=F32), sem(14), sem(1)],
        LIMIT_C,
        4 * length * d * attn * 2,
        (2, 3, 4, 5, 6, 7, 9, 10),
        (0,),
    )


def run_grads(first_seq, last_seq, rows, blocks, wide, meta, arrays):
    sd = jax.ShapeDtypeStruct
    length, d = arrays[0].shape
    attn = d - wide
    each = d // blocks
    return call(
        functools.partial(stage_grads, first_seq, last_seq, rows, blocks),
        [sd((2, rows, d), BF), sd((2, rows, d), BF)]
        + (
            [sd((blocks, each + VEC_ROWS, d), BF)]
            if last_seq
            else [sd((wide, d), F32), sd((attn, d), F32), sd((8, d), F32)]
        ),
        [meta],
        arrays,
        [vm(length, d), vm(length, attn), vm(wide, d), sem(3)],
        LIMIT_A,
        4 * length * d * d,
        (3, 4, 5),
        (),
    )


def stage_d(seq, meta, x, mg, keep, got, far, g1, out):
    xhat, inv = norm_rows(x[seq].astype(F32))
    slot = meta[0] >> 1
    n = keep[slot].astype(F32) + got[slot].astype(F32) + far[...].astype(F32)
    e = n * g1[...]
    mean_e = jnp.mean(e, axis=-1, keepdims=True)
    mean_ex = jnp.mean(e * xhat, axis=-1, keepdims=True)
    out[...] = (mg[...] + inv * (e - mean_e - xhat * mean_ex)).astype(BF)


def unpack_ff(each, d, near, far, meta, up_o, down_o):
    for j in range(8):
        at = lax.bitwise_xor(meta[1], jnp.int32(j))
        rows = slice(j * each, j * each + each)

        @pl.when(at < 4)
        def _():
            block = near[jnp.minimum(at, 3)].astype(F32)
            up_o[rows, :] = block[:each]
            down_o[rows, :] = block[each:]

        @pl.when(at >= 4)
        def _():
            block = far[jnp.maximum(at - 4, 0)].astype(F32)
            up_o[rows, :] = block[:each]
            down_o[rows, :] = block[each:]


def unpack_attn(each, wide, near, far, meta, qkv_o, out_o, vec_o):
    for j in range(8):
        at = lax.bitwise_xor(meta[1], jnp.int32(j))
        r = j * each

        def put(block):
            if r < wide:
                qkv_o[r : r + each, :] = block[:each]
            else:
                out_o[r - wide : r - wide + each, :] = block[:each]
            vec_o[j : j + 1, :] = block[each : each + 1, :]

        @pl.when(at < 4)
        def _():
            put(near[jnp.minimum(at, 3)].astype(F32))

        @pl.when(at >= 4)
        def _():
            put(far[jnp.maximum(at - 4, 0)].astype(F32))


def on_device(
    tokens,
    clip_lengths,
    cotangent,
    query_key_value_weight,
    qv_bias,
    output_weight,
    out_bias,
    gain1,
    shift1,
    gain2,
    shift2,
    up_weight,
    hidden_bias,
    down_weight,
    down_bias,
):
    n_dp = lax.axis_size("dp")
    n_tensor = lax.axis_size("tensor")
    seqs, rows, d = tokens.shape
    length = rows * n_tensor
    heads = output_weight.shape[0] // HEAD_DIM
    wide = 3 * HEAD_DIM * heads
    hidden = up_weight.shape[1]
    blocks = 8
    each = d // blocks

    def core_swap(v):
        return lax.ppermute(v, "tensor", [(t, t ^ 1) for t in range(n_tensor)])

    def chip_swap(v):
        return lax.ppermute(v, "tensor", [(t, t ^ 2) for t in range(n_tensor)])

    t = lax.axis_index("tensor")
    dp_at = lax.axis_index("dp")
    orders = ((0, 1, 2), (1, 0, 2))
    if n_dp == 8:

        def place(order):
            return sum(((dp_at >> order[k]) & 1) << (2 - k) for k in range(3))

        label = jnp.where(t % 2 == 0, place(orders[0]), place(orders[1]))
    else:
        label = jnp.zeros_like(dp_at)
    meta = jnp.stack([t, label]).astype(jnp.int32)

    def add(a, b):
        return (a.astype(F32) + b.astype(F32)).astype(BF)

    def after(value, *others):
        return lax.optimization_barrier((value, others))[0]

    def step_perm(k):
        pairs = []
        for dev in range(n_dp):
            for s in range(n_tensor):
                other = dev ^ (1 << orders[s % 2][k])
                pairs.append((dev * n_tensor + s, other * n_tensor + s))
        return pairs

    def reduce_get(held, k):
        return lax.ppermute(held[held.shape[0] // 2 :], ("dp", "tensor"), step_perm(k))

    def gather_step(held, k):
        return lax.ppermute(held, ("dp", "tensor"), step_perm(k))

    def after(value, *others):
        return lax.optimization_barrier((value, others))[0]

    def step_perm(k):
        pairs = []
        for dev in range(n_dp):
            for s in range(n_tensor):
                other = dev ^ (1 << orders[s % 2][k])
                pairs.append((dev * n_tensor + s, other * n_tensor + s))
        return pairs

    def reduce_get(held, k):
        return lax.ppermute(held[held.shape[0] // 2 :], ("dp", "tensor"), step_perm(k))

    def reduce_step(held, k):
        return add(held[: held.shape[0] // 2], reduce_get(held, k))

    def gather_step(held, k):
        return lax.ppermute(held, ("dp", "tensor"), step_perm(k))

    def gather_all(held):
        for k in (2, 1):
            held = jnp.concatenate([held, gather_step(held, k)], axis=0)
        return held, gather_step(held, 0)

    def after(value, *others):
        return lax.optimization_barrier((value, others))[0]

    def step_perm(k):
        pairs = []
        for dev in range(n_dp):
            for s in range(n_tensor):
                other = dev ^ (1 << orders[s % 2][k])
                pairs.append((dev * n_tensor + s, other * n_tensor + s))
        return pairs

    def all_reduce(buf):
        if n_dp != 8:
            full = lax.psum(buf, "dp")
            return full[:4], full[4:]
        held = buf
        for k in range(3):
            half = held.shape[0] // 2
            got = lax.ppermute(held[half:], ("dp", "tensor"), step_perm(k))
            held = add(held[:half], got)
        for k in (2, 1):
            got = lax.ppermute(held, ("dp", "tensor"), step_perm(k))
            held = jnp.concatenate([held, got], axis=0)
        return held, lax.ppermute(held, ("dp", "tensor"), step_perm(0))

    def row(v):
        return v.reshape(1, -1)

    pairs = qv_bias.reshape(heads, 2, HEAD_DIM)
    bias = row(jnp.stack([pairs[:, 0], jnp.zeros_like(pairs[:, 0]), pairs[:, 1]], axis=1))
    g1, b1, g2, b2 = row(gain1), row(shift1), row(gain2), row(shift2)
    ob, hb = row(out_bias), row(hidden_bias)
    chip_at = t >> 1

    w_t = query_key_value_weight.T

    def spread(v, *first):
        near = core_swap(v)
        across = after(chip_swap(v), *first)
        return [v, near, across, core_swap(across)]

    def chip_sum(keep, send):
        return add(keep, core_swap(send))

    def all_rows(chip, far):
        own = add(chip, far)
        return [own, core_swap(own)]

    def peer_rows(keep, got):
        return add(keep[1 - chip_at], got[1 - chip_at])

    xs = spread(tokens, g1, b1, g2, b2, ob, hb, bias, meta)
    cot_near = core_swap(cotangent)
    beside = chip_swap(cotangent)

    kept, chips, fars = [], [], []
    for s in range(seqs):
        outs = run_a(
            s, heads, length, rows, d, meta, clip_lengths, after(xs, *chips[-1:]), g1, b1,
            w_t, bias, output_weight,
        )
        kept.append(outs[:3])
        if s == 0:
            beside = after(beside, outs[3])
            cots = [cotangent, cot_near, beside, core_swap(beside)]
        chips.append(chip_sum(outs[3], after(outs[4], beside)))
        beside = chip_swap(chips[s])
        fars.append(beside)

    mids, stats, ff_keep, ff_send, n_chips, n_fars = [], [], [], [], [], []
    carry = []
    for s in range(seqs):
        mids.append(all_rows(chips[s], fars[s]))
        outs = run_b(
            s, s == 0, s == seqs - 1, rows, d, hidden, blocks, meta, xs,
            after(mids[s], *(chips[-1:] + n_chips[-1:])), cots,
            ob, g2, b2, up_weight, hb, down_weight, carry,
        )
        n_chips.append(chip_sum(outs[2], after(outs[3], beside)))
        beside = chip_swap(n_chips[s])
        n_fars.append(beside)
        ff_keep.append(outs[0])
        ff_send.append(outs[1])
        stats.append(outs[4:6])
        carry = outs[6:]
    ff_grads, vec_b = carry

    moves = [("halve", 0), ("halve", 1), ("halve", 2), ("double", 2), ("double", 1)]

    def send_move(held):
        kind, k = moves[0]
        return reduce_get(held, k) if kind == "halve" else gather_step(held, k)

    def take_move(held, part):
        if moves.pop(0)[0] == "halve":
            return add(held[: held.shape[0] // 2], part)
        return jnp.concatenate([held, part], axis=0)

    by_hand = n_dp == 8 and seqs == 2
    backs, peers, far_rows = [], [], []
    carry = []
    held = ff_grads
    for s in range(seqs):
        last = s == seqs - 1
        n_now = after(all_rows(n_chips[s], n_fars[s]), *n_chips[-1:], held)
        mg, ag, dq, vec_a = run_c(
            s, heads, length, rows, d, clip_lengths.shape[1], meta, clip_lengths,
            [*n_now, *cots, *stats[s], g2, output_weight, kept[s][1]],
        )
        if by_hand:
            held = take_move(held, after(send_move(held), dq))
            dq = after(dq, held)
        outs = run_grads(
            s == 0, last, rows, blocks, wide, meta,
            [ag, dq, vec_a, kept[s][0], kept[s][2], w_t, g1, b1, *carry] + ([vec_b] if last else []),
        )
        keep, send = outs[:2]
        carry = outs[2:]
        waits = [] if last else [beside]
        if by_hand and last:
            part = send_move(held)
        elif by_hand:
            held = take_move(held, after(send_move(held), send))
        got = core_swap(after(send, *waits))
        peers.append(peer_rows(keep, got))
        beside = chip_swap(peers[s])
        far_rows.append(beside)
        backs.append((mg, keep, got))
    at_grads = carry[0]
    ff_got = [core_swap(after(send, vec_a)) for send in ff_send]
    ff_peers = [peer_rows(keep, got) for keep, got in zip(ff_keep, ff_got)]
    ff_far_rows = [chip_swap(v) for v in ff_peers]
    whole = pl.BlockSpec(memory_space=pltpu.VMEM)

    def input_rows(s):
        return pl.pallas_call(
            functools.partial(stage_d, s),
            out_shape=jax.ShapeDtypeStruct((rows, d), BF),
            in_specs=[pl.BlockSpec(memory_space=pltpu.SMEM)] + [whole] * 6,
            out_specs=whole,
            compiler_params=pltpu.CompilerParams(vmem_limit_bytes=16 << 20),
        )(meta, tokens, *backs[s], far_rows[s], g1)

    def output_rows(s):
        ff = ff_keep[s][chip_at].astype(F32) + ff_got[s][chip_at].astype(F32)
        middle = tokens[s].astype(F32) + mids[s][0][chip_at].astype(F32) + out_bias
        return (middle + (ff + ff_far_rows[s].astype(F32) + down_bias)).astype(BF)

    input_grad = jnp.stack([input_rows(s) for s in range(seqs)])
    block_out = jnp.stack([output_rows(s) for s in range(seqs)])
    if by_hand:
        at_held = add(at_grads[:4], after(reduce_get(at_grads, 0), *ff_peers))
        held = take_move(held, after(part, at_held))
        part = send_move(held)
        at_held = add(at_held[:2], reduce_get(at_held, 1))
        at_held = add(at_held[:1], reduce_get(at_held, 2))
        ff_near = take_move(held, after(part, at_held, input_grad))
        ff_far = gather_step(ff_near, 0)
        at_held = jnp.concatenate([at_held, gather_step(at_held, 2)], axis=0)
        part = after(gather_step(at_held, 1), block_out)
        at_near = jnp.concatenate([at_held, part], axis=0)
        at_far = gather_step(at_near, 0)
    else:
        ff_sum, at_sum = lax.psum((ff_grads, at_grads), "dp")
        ff_near, ff_far, at_near, at_far = ff_sum[:4], ff_sum[4:], at_sum[:4], at_sum[4:]

    def unpack(body, near, far, out_shape):
        whole = pl.BlockSpec(memory_space=pltpu.VMEM)
        return pl.pallas_call(
            body,
            out_shape=out_shape,
            in_specs=[whole, whole, pl.BlockSpec(memory_space=pltpu.SMEM)],
            out_specs=[whole] * len(out_shape),
            compiler_params=pltpu.CompilerParams(vmem_limit_bytes=24 << 20),
        )(near, far, meta)

    grad_up, grad_down = unpack(
        functools.partial(unpack_ff, each, d),
        ff_near,
        ff_far,
        [jax.ShapeDtypeStruct((d, hidden), F32), jax.ShapeDtypeStruct((hidden, d), F32)],
    )
    at_far = after(at_far, block_out, input_grad, grad_up, grad_down)

    def vec_row(j):
        at = label ^ j
        return jnp.where(at < 4, at_near[at & 3, each], at_far[at & 3, each]).astype(F32)

    norm1 = jnp.stack([vec_row(V_GAIN1), vec_row(V_SHIFT1)])
    across = lax.ppermute(norm1, "tensor", [(t, t ^ 3) for t in range(n_tensor)])
    near = core_swap(norm1)
    at_near = after(at_near, near)
    norm1 = (norm1 + near) + (chip_swap(norm1) + across)
    grad_qkv, grad_out, vec = unpack(
        functools.partial(unpack_attn, each, wide),
        at_near,
        at_far,
        [
            jax.ShapeDtypeStruct((wide, d), F32),
            jax.ShapeDtypeStruct((d - wide, d), F32),
            jax.ShapeDtypeStruct((8, d), F32),
        ],
    )
    qkv_sum = vec[V_QKV, :wide].reshape(heads, 3, HEAD_DIM)
    return (
        block_out,
        input_grad,
        grad_qkv.T,
        qkv_sum[:, ::2].reshape(-1),
        grad_out,
        vec[V_OUT],
        norm1[0],
        norm1[1],
        vec[V_GAIN2],
        vec[V_SHIFT2],
        grad_up,
        vec[V_UP],
        grad_down,
        vec[V_DOWN],
    )


def solution(mesh):
    placed = (
        P("dp", "tensor", None),
        P("dp", None),
        P("dp", "tensor", None),
        P(None, "tensor"),
        P("tensor"),
        P("tensor", None),
        P(),
        P(),
        P(),
        P(),
        P(),
        P(None, "tensor"),
        P("tensor"),
        P("tensor", None),
        P(),
    )
    return jax.shard_map(
        on_device,
        mesh=mesh,
        in_specs=placed,
        out_specs=(
            P("dp", "tensor", None),
            P("dp", "tensor", None),
            P(None, "tensor"),
            P("tensor"),
            P("tensor", None),
            P(),
            P(),
            P(),
            P(),
            P(),
            P(None, "tensor"),
            P("tensor"),
            P("tensor", None),
            P(),
        ),
        check_vma=False,
    )
```

```python
import functools

import jax
import jax.numpy as jnp
from jax import lax
from jax.experimental import pallas as pl
from jax.experimental.pallas import tpu as pltpu
from jax.sharding import PartitionSpec as P

HEAD_DIM = 64
EPS = 1e-06
SCALE = HEAD_DIM ** (-0.5)
BF = jnp.bfloat16
F32 = jnp.float32
LONGEST = 170
WINDOW = 192
MASKED = -1e30
VEC_ROWS = 16
COST_SCALE = 1
LIMIT_A, LIMIT_B, LIMIT_C = 20, 36, 32

V_UP, V_DOWN, V_GAIN2, V_SHIFT2, V_OUT, V_GAIN1, V_SHIFT1, V_QKV = range(8)


def dot_nn(a, b):
    return lax.dot_general(a, b, (((1,), (0,)), ((), ())), preferred_element_type=F32)


def dot_nt(a, b):
    return lax.dot_general(a, b, (((1,), (1,)), ((), ())), preferred_element_type=F32)


def dot_tn(a, b):
    return lax.dot_general(a, b, (((0,), (0,)), ((), ())), preferred_element_type=F32)


def call(body, out_shape, scalars, arrays, scratch, limit_mb, flops, far_in, far_out):
    whole = pl.BlockSpec(memory_space=pltpu.VMEM)
    far = pl.BlockSpec(memory_space=pltpu.HBM)
    moved = sum(a.size * a.dtype.itemsize for a in arrays) + sum(
        o.size * o.dtype.itemsize for o in out_shape
    )
    return pl.pallas_call(
        body,
        out_shape=[pltpu.HBM(o.shape, o.dtype) if i in far_out else o for i, o in enumerate(out_shape)],
        in_specs=[pl.BlockSpec(memory_space=pltpu.SMEM)] * len(scalars)
        + [far if i in far_in else whole for i in range(len(arrays))],
        out_specs=[far if i in far_out else whole for i in range(len(out_shape))],
        scratch_shapes=scratch,
        compiler_params=pltpu.CompilerParams(vmem_limit_bytes=limit_mb << 20),
        cost_estimate=pl.CostEstimate(flops=flops * COST_SCALE, transcendentals=0, bytes_accessed=moved),
    )(
        *scalars,
        *[
            pltpu.with_memory_space_constraint(a, pltpu.HBM) if i in far_in else a
            for i, a in enumerate(arrays)
        ],
    )


def sem(n):
    return pltpu.SemaphoreType.DMA((n,))


def vm(*shape, dtype=BF):
    return pltpu.VMEM(shape, dtype)


def copies(done, *pairs):
    made = [pltpu.make_async_copy(src, dst, done.at[i]) for i, (src, dst) in enumerate(pairs)]
    for c in made:
        c.start()
    return made


def block_start(meta, p, rows):
    return pl.multiple_of(lax.bitwise_xor(meta[0], jnp.int32(p)) * rows, rows)


def chip_slot(meta, p):
    return lax.bitwise_xor(meta[0] >> 1, jnp.int32(p >> 1))


def norm_rows(x):
    mean = jnp.mean(x, axis=-1, keepdims=True)
    centred = x - mean
    var = jnp.mean(centred * centred, axis=-1, keepdims=True)
    inv = lax.rsqrt(var + EPS)
    return centred * inv, inv


def phi_parts(u):
    cdf = 0.5 * (1.0 + lax.erf(u * 0.7071067811865476))
    return cdf, jnp.exp(u * u * -0.5) * 0.3989422804014327


def pad_range(clips, length):
    k0 = clips * 100 // 64 * 64
    step = 112 if (length - k0) % 112 == 0 else 64
    return k0, step, (length - k0) // step


def clip_start(first, length):
    return pl.multiple_of(jnp.minimum(first // 16 * 16, length - WINDOW), 16)


def stage_a(seq, heads, length, rows, meta, lens, *refs):
    x_refs, (g1, b1, w_h, bias, wo_h), refs = refs[:4], refs[4:9], refs[9:]
    normed_h, qkv_h, att_h, keep_o, send_o, x_s, w, wo, normed_o, qkv_o, att_o, in_sem, out_sem = refs
    clips = lens.shape[1]
    get = copies(
        in_sem,
        (x_refs[0].at[seq], x_s.at[0]),
        (w_h, w),
        *[(x_refs[p].at[seq], x_s.at[p]) for p in range(1, 4)],
        (wo_h, wo),
    )
    get[1].wait()
    for p in range(4):
        r0 = block_start(meta, p, rows)
        get[p + (p > 0)].wait()
        xhat, _ = norm_rows(x_s[p].astype(F32))
        nb = (xhat * g1[...] + b1[...]).astype(BF)
        normed_o[pl.ds(r0, rows), :] = nb
        qkv_o[pl.ds(r0, rows), :] = (dot_nt(nb, w[...]) + bias[...]).astype(BF)

    put = copies(out_sem, (normed_o, normed_h), (qkv_o, qkv_h))

    def attend(q0, q_rows, k0, k_rows, first, last):
        key_at = lax.broadcasted_iota(jnp.int32, (1, k_rows), 1) + k0
        allowed = (key_at >= first) & (key_at < last)
        row_at = lax.broadcasted_iota(jnp.int32, (q_rows, 1), 0) + q0
        scores, outs = [], []
        for h in range(heads):
            col = h * 3 * HEAD_DIM
            q = qkv_o[pl.ds(q0, q_rows), col : col + HEAD_DIM] * BF(SCALE)
            k = qkv_o[pl.ds(k0, k_rows), col + HEAD_DIM : col + 2 * HEAD_DIM]
            scores.append(dot_nt(q, k))
        for h in range(heads):
            v = qkv_o[pl.ds(k0, k_rows), (h * 3 + 2) * HEAD_DIM : (h * 3 + 3) * HEAD_DIM]
            s = jnp.where(allowed, scores[h], MASKED)
            e = jnp.exp(s - jnp.max(s, axis=1, keepdims=True))
            probs = (e * (1.0 / jnp.sum(e, axis=1, keepdims=True))).astype(BF)
            outs.append(dot_nn(probs, v).astype(BF))
        new = jnp.concatenate(outs, axis=1)
        old = att_o[pl.ds(q0, q_rows), :]
        att_o[pl.ds(q0, q_rows), :] = jnp.where(row_at >= first, new, old)

    def one_clip(c, first):
        last = first + lens[seq, c]
        w0 = clip_start(first, length)
        attend(w0, WINDOW, w0, WINDOW, first, last)
        return last

    first = lax.fori_loop(0, clips, one_clip, jnp.int32(0), unroll=2)
    k0, step, tiles = pad_range(clips, length)

    def pad_tile(i, carry):
        attend(pl.multiple_of(k0 + i * step, 16), step, k0, length - k0, first, length)
        return carry

    lax.fori_loop((first - k0) // step, tiles, pad_tile, jnp.int32(0))

    att_put = pltpu.make_async_copy(att_o, att_h, out_sem.at[2])
    att_put.start()
    get[5].wait()
    for p in range(4):
        r0 = block_start(meta, p, rows)
        part = dot_nn(att_o[pl.ds(r0, rows), :], wo[...]).astype(BF)
        (keep_o, send_o)[p & 1][chip_slot(meta, p)] = part
    for c in [*put, att_put]:
        c.wait()


def stage_b(seq, first_seq, last_seq, rows, blocks, meta, *refs):
    xs, ms, cots, refs = refs[:4], refs[4:6], refs[6:10], refs[10:]
    ob, g2, b2, wu_h, hb, wd_h = refs[:6]
    refs = refs[6:]
    if not first_seq:
        old_up, old_down, old_vec = refs[:3]
        refs = refs[3:]
    keep_fh, send_fh, keep_n, send_n, xhat_h, inv_h = refs[:6]
    refs = refs[6:]
    if last_seq:
        grads_o, vec_o = refs[:2]
        refs = refs[2:]
    else:
        up_o, down_o, vec_o = refs[:3]
        refs = refs[3:]
    n2_s, act_s, ug_s, cot_s, x_s, wu, wd, keep_f, send_f, xhat_o, inv_o, in_sem, out_sem = refs
    pieces = []
    for p in range(4):
        here = pl.ds(p * rows, rows)
        pieces += [(xs[p].at[seq], x_s.at[p]), (cots[p].at[seq], cot_s.at[here, :])]
        if p == 0:
            pieces += [(wu_h, wu), (wd_h, wd)]
    get = copies(in_sem, *pieces)
    get[2].wait()
    get[3].wait()
    d = wu.shape[0]
    up_sum = jnp.zeros((1, wu.shape[1]), F32)
    down_sum = jnp.zeros((1, d), F32)
    for p in range(4):
        slot = chip_slot(meta, p)
        here = slice(p * rows, p * rows + rows)
        for c in get[2 * p + 2 * (p > 0) : 2 * p + 2 * (p > 0) + 2]:
            c.wait()
        mid = x_s[p].astype(F32) + ms[p & 1][slot].astype(F32) + ob[...]
        xhat, inv = norm_rows(mid)
        xhat_o[here, :] = xhat.astype(BF)
        inv_o[here, :] = inv
        n2 = (xhat * g2[...] + b2[...]).astype(BF)
        n2_s[here, :] = n2
        u = dot_nn(n2, wu[...]) + hb[...]
        cdf, pdf = phi_parts(u)
        act = (u * cdf).astype(BF)
        act_s[here, :] = act
        (keep_f, send_f)[p & 1][slot] = dot_nn(act, wd[...]).astype(BF)
        cot = cot_s[here, :]
        down_sum = down_sum + jnp.sum(cot.astype(F32), axis=0, keepdims=True)
        ug = (dot_nt(cot, wd[...]) * (cdf + u * pdf)).astype(BF)
        ug_s[here, :] = ug
        up_sum = up_sum + jnp.sum(ug.astype(F32), axis=0, keepdims=True)
        (keep_n, send_n)[p & 1][slot] = dot_nt(ug, wu[...]).astype(BF)
    put = copies(
        out_sem, (keep_f, keep_fh), (send_f, send_fh), (xhat_o, xhat_h), (inv_o, inv_h)
    )
    grad_up = dot_tn(n2_s[...], ug_s[...])
    grad_down = dot_tn(act_s[...], cot_s[...])
    if not first_seq:
        grad_up = grad_up + old_up[...]
        grad_down = grad_down + old_down[...]
        up_sum = up_sum + old_vec[V_UP : V_UP + 1, :]
        down_sum = down_sum + old_vec[V_DOWN : V_DOWN + 1, :]
    vec_o[V_UP : V_UP + 1, :] = up_sum
    vec_o[V_DOWN : V_DOWN + 1, :] = down_sum
    if not last_seq:
        up_o[...] = grad_up
        down_o[...] = grad_down
    else:
        each = d // blocks
        for j in range(blocks):
            at = lax.bitwise_xor(meta[1], jnp.int32(j))
            grads_o[at, :each, :] = grad_up[j * each : j * each + each].astype(BF)
            grads_o[at, each:, :] = grad_down[j * each : j * each + each].astype(BF)
    for c in put:
        c.wait()


def stage_c(seq, heads, length, rows, meta, lens, *refs):
    ns, cots, refs = refs[:2], refs[2:6], refs[6:]
    xhat_h, inv_h, g2, wo_h, qkv_h, mg_h, ag_s, dq_s, vec_o = refs[:9]
    da_s, kv_acc, q_acc, cot_s, xhat_i, inv_i, wo, qkv, mg_o, in_sem, out_sem = refs[9:]
    pieces = []
    for p in range(4):
        here = pl.ds(p * rows, rows)
        pieces += [(cots[p].at[seq], cot_s.at[p])]
        pieces += [(ref.at[here, :], dst.at[here, :]) for ref, dst in ((xhat_h, xhat_i), (inv_h, inv_i))]
        if p == 0:
            pieces += [(wo_h, wo)]
    get = copies(in_sem, *pieces, (qkv_h, qkv))
    get[3].wait()
    clips = lens.shape[1]
    d = g2.shape[1]
    sums = {k: jnp.zeros((1, d), F32) for k in (V_GAIN2, V_SHIFT2, V_OUT)}
    for p in range(4):
        slot = chip_slot(meta, p)
        here = slice(p * rows, p * rows + rows)
        r0 = block_start(meta, p, rows)
        for c in [get[:3], get[4:13], [], []][p]:
            c.wait()
        n = ns[p & 1][slot].astype(F32)
        xhat = xhat_i[here, :].astype(F32)
        e = n * g2[...]
        mean_e = jnp.mean(e, axis=-1, keepdims=True)
        mean_ex = jnp.mean(e * xhat, axis=-1, keepdims=True)
        mg = cot_s[p].astype(F32) + inv_i[here, :] * (e - mean_e - xhat * mean_ex)
        if p == 0:
            mg_o[...] = mg
        ag = mg.astype(BF)
        ag_s[pl.ds(r0, rows), :] = ag
        da_s[pl.ds(r0, rows), :] = dot_nt(ag, wo[...]).astype(BF)
        sums[V_GAIN2] += jnp.sum(n * xhat, axis=0, keepdims=True)
        sums[V_SHIFT2] += jnp.sum(n, axis=0, keepdims=True)
        sums[V_OUT] += jnp.sum(ag.astype(F32), axis=0, keepdims=True)

    put = pltpu.make_async_copy(mg_o, mg_h, out_sem.at[0])
    put.start()
    get[13].wait()

    def attend_back(q0, q_rows, k0, k_rows, first, last):
        q_at = lax.broadcasted_iota(jnp.int32, (k_rows, q_rows), 1) + q0
        k_at = lax.broadcasted_iota(jnp.int32, (k_rows, q_rows), 0) + k0
        allowed = (k_at >= first) & (k_at < last) & (q_at >= first) & (q_at < last)
        qs, ks, dos, scores, prob_grads, sms, dss = [], [], [], [], [], [], []
        for h in range(heads):
            col = h * 3 * HEAD_DIM
            qs.append(qkv[pl.ds(q0, q_rows), col : col + HEAD_DIM] * BF(SCALE))
            ks.append(qkv[pl.ds(k0, k_rows), col + HEAD_DIM : col + 2 * HEAD_DIM])
            v = qkv[pl.ds(k0, k_rows), col + 2 * HEAD_DIM : col + 3 * HEAD_DIM]
            dos.append(da_s[pl.ds(q0, q_rows), h * HEAD_DIM : h * HEAD_DIM + HEAD_DIM])
            scores.append(dot_nt(ks[h], qs[h]))
            prob_grads.append(dot_nt(v, dos[h]))
        for h in range(heads):
            s = jnp.where(allowed, scores[h], MASKED)
            e = jnp.exp(s - jnp.max(s, axis=0, keepdims=True))
            sm = jnp.where(allowed, e * (1.0 / jnp.sum(e, axis=0, keepdims=True)), 0.0)
            t = sm * prob_grads[h]
            dss.append((t - sm * jnp.sum(t, axis=0, keepdims=True)).astype(BF))
            sms.append(sm.astype(BF))
        dv = [dot_nn(sms[h], dos[h]) for h in range(heads)]
        dk = [dot_nn(dss[h], qs[h]) for h in range(heads)]
        dq = [dot_tn(dss[h], ks[h]) * SCALE for h in range(heads)]
        return dq, dk, dv

    def one_clip(c, first):
        last = first + lens[seq, c]
        w0 = clip_start(first, length)
        dq, dk, dv = attend_back(w0, WINDOW, w0, WINDOW, first, last)
        new = jnp.concatenate(
            [part[h].astype(BF) for h in range(heads) for part in (dq, dk, dv)], axis=1
        )
        row_at = lax.broadcasted_iota(jnp.int32, (WINDOW, 1), 0) + w0
        old = dq_s[pl.ds(w0, WINDOW), :]
        dq_s[pl.ds(w0, WINDOW), :] = jnp.where(row_at >= first, new, old)
        return last

    first = lax.fori_loop(0, clips, one_clip, jnp.int32(0), unroll=2)
    k0, step, tiles = pad_range(clips, length)
    k_rows = length - k0
    kv_acc[...] = jnp.zeros_like(kv_acc)

    def pad_tile(i, carry):
        at = pl.multiple_of(i * step, 16)
        dq, dk, dv = attend_back(k0 + at, step, k0, k_rows, first, length)
        for h in range(heads):
            kv_acc[2 * h] += dk[h]
            kv_acc[2 * h + 1] += dv[h]
            q_acc[h, pl.ds(at, step), :] = dq[h].astype(BF)
        return carry

    lax.fori_loop((first - k0) // step, tiles, pad_tile, jnp.int32(0))
    new = jnp.concatenate(
        [
            part.astype(BF)
            for h in range(heads)
            for part in (q_acc[h], kv_acc[2 * h], kv_acc[2 * h + 1])
        ],
        axis=1,
    )
    row_at = lax.broadcasted_iota(jnp.int32, (k_rows, 1), 0) + k0
    dq_s[k0:, :] = jnp.where(row_at >= first, new, dq_s[k0:, :])
    for k in sums:
        vec_o[k : k + 1, :] = sums[k]
    put.wait()


def stage_grads(first_seq, last_seq, rows, blocks, meta, *refs):
    ag_s, dq_s, vec_a, normed_h, att_h, w_h, g1, b1 = refs[:8]
    refs = refs[8:]
    if not first_seq:
        old_qkv, old_out, old_vec = refs[:3]
        refs = refs[3:]
    if last_seq:
        vec_b, refs = refs[0], refs[1:]
    keep_o, send_o = refs[:2]
    refs = refs[2:]
    if last_seq:
        grads_o, refs = refs[0], refs[1:]
    else:
        qkv_o, out_o, vec_o = refs[:3]
        refs = refs[3:]
    normed, att, w, in_sem = refs
    get = copies(in_sem, (w_h, w), (normed_h, normed), (att_h, att))
    d = g1.shape[1]
    sums = {k: vec_a[k : k + 1, :] for k in (V_GAIN2, V_SHIFT2, V_OUT)}
    sums[V_GAIN1] = jnp.zeros((1, d), F32)
    sums[V_SHIFT1] = jnp.zeros((1, d), F32)
    for c in get:
        c.wait()
    grad_out = dot_tn(att[...], ag_s[...])
    grad_qkv = dot_tn(dq_s[...], normed[...])
    qkv_sum = jnp.sum(dq_s[...].astype(F32), axis=0, keepdims=True)
    for p in range(4):
        r0 = block_start(meta, p, rows)
        ng = dot_nn(dq_s[pl.ds(r0, rows), :], w[...])
        sums[V_SHIFT1] += jnp.sum(ng, axis=0, keepdims=True)
        sums[V_GAIN1] += jnp.sum(ng * normed[pl.ds(r0, rows), :].astype(F32), axis=0, keepdims=True)
        (keep_o, send_o)[p & 1][chip_slot(meta, p)] = ng.astype(BF)
    sums[V_GAIN1] = (sums[V_GAIN1] - b1[...] * sums[V_SHIFT1]) / g1[...]
    sums[V_QKV] = jnp.concatenate([qkv_sum, jnp.zeros((1, d - qkv_sum.shape[1]), F32)], axis=1)
    if not first_seq:
        grad_qkv = grad_qkv + old_qkv[...]
        grad_out = grad_out + old_out[...]
        for k in sums:
            sums[k] += old_vec[k : k + 1, :]
    if not last_seq:
        qkv_o[...] = grad_qkv
        out_o[...] = grad_out
        for k in sums:
            vec_o[k : k + 1, :] = sums[k]
        return
    for k in (V_UP, V_DOWN):
        sums[k] = vec_b[k : k + 1, :]
    each = d // blocks
    wide = grad_qkv.shape[0]
    for j in range(blocks):
        at = lax.bitwise_xor(meta[1], jnp.int32(j))
        r = j * each
        part = grad_qkv[r : r + each] if r < wide else grad_out[r - wide : r - wide + each]
        grads_o[at, :each, :] = part.astype(BF)
        grads_o[at, each:, :] = jnp.broadcast_to(sums[j], (VEC_ROWS, d)).astype(BF)


def run_a(seq, heads, length, rows, d, meta, lens, xs, g1, b1, w, bias, wo):
    wide, attn = 3 * heads * HEAD_DIM, heads * HEAD_DIM
    sd = jax.ShapeDtypeStruct
    return call(
        functools.partial(stage_a, seq, heads, length, rows),
        [sd((length, d), BF), sd((length, wide), BF), sd((length, attn), BF)]
        + [sd((2, rows, d), BF)] * 2,
        [meta, lens],
        [*xs, g1, b1, w, bias, wo],
        [vm(4, rows, d), vm(wide, d), vm(attn, d), vm(length, d), vm(length, wide)]
        + [vm(length, attn), sem(6), sem(3)],
        LIMIT_A,
        2 * length * d * (wide + attn) * 2,
        (0, 1, 2, 3, 6, 8),
        (0, 1, 2),
    )


def run_b(seq, first_seq, last_seq, rows, d, hidden, blocks, meta, xs, ms, cots, ob, g2, b2, wu, hb, wd, carry):
    sd = jax.ShapeDtypeStruct
    length = 4 * rows
    each = d // blocks
    return call(
        functools.partial(stage_b, seq, first_seq, last_seq, rows, blocks),
        [sd((2, rows, d), BF)] * 4
        + [sd((length, d), BF), sd((length, 1), F32)]
        + (
            [sd((blocks, 2 * each, d), BF)]
            if last_seq
            else [sd((d, hidden), F32), sd((hidden, d), F32)]
        )
        + [sd((8, d), F32)],
        [meta],
        [*xs, *ms, *cots, ob, g2, b2, wu, hb, wd, *carry],
        [pltpu.VMEM((length, d), BF), pltpu.VMEM((length, hidden), BF)]
        + [pltpu.VMEM((length, hidden), BF), pltpu.VMEM((length, d), BF)]
        + [vm(4, rows, d), vm(d, hidden), vm(hidden, d), vm(2, rows, d), vm(2, rows, d)]
        + [vm(length, d), vm(length, 1, dtype=F32), sem(10), sem(4)],
        LIMIT_B,
        12 * length * d * hidden,
        (0, 1, 2, 3, 6, 7, 8, 9, 13, 15),
        (0, 1, 4, 5),
    )


def run_c(seq, heads, length, rows, d, clips, meta, lens, arrays):
    sd = jax.ShapeDtypeStruct
    wide, attn = 3 * heads * HEAD_DIM, heads * HEAD_DIM
    k_rows = length - pad_range(clips, length)[0]
    return call(
        functools.partial(stage_c, seq, heads, length, rows),
        [sd((rows, d), F32), sd((length, d), BF), sd((length, wide), BF), sd((8, d), F32)],
        [meta, lens],
        arrays,
        [vm(length, attn), vm(2 * heads, k_rows, HEAD_DIM, dtype=F32), vm(heads, k_rows, HEAD_DIM)]
        + [vm(4, rows, d), vm(length, d), vm(length, 1, dtype=F32), vm(attn, d)]
        + [vm(length, wide), vm(rows, d, dtype=F32), sem(14), sem(1)],
        LIMIT_C,
        4 * length * d * attn * 2,
        (2, 3, 4, 5, 6, 7, 9, 10),
        (0,),
    )


def run_grads(first_seq, last_seq, rows, blocks, wide, meta, arrays):
    sd = jax.ShapeDtypeStruct
    length, d = arrays[0].shape
    attn = d - wide
    each = d // blocks
    return call(
        functools.partial(stage_grads, first_seq, last_seq, rows, blocks),
        [sd((2, rows, d), BF), sd((2, rows, d), BF)]
        + (
            [sd((blocks, each + VEC_ROWS, d), BF)]
            if last_seq
            else [sd((wide, d), F32), sd((attn, d), F32), sd((8, d), F32)]
        ),
        [meta],
        arrays,
        [vm(length, d), vm(length, attn), vm(wide, d), sem(3)],
        LIMIT_A,
        4 * length * d * d,
        (3, 4, 5),
        (),
    )


def stage_d(seq, meta, x, mg, keep, got, far, g1, out):
    xhat, inv = norm_rows(x[seq].astype(F32))
    slot = meta[0] >> 1
    n = keep[slot].astype(F32) + got[slot].astype(F32) + far[...].astype(F32)
    e = n * g1[...]
    mean_e = jnp.mean(e, axis=-1, keepdims=True)
    mean_ex = jnp.mean(e * xhat, axis=-1, keepdims=True)
    out[...] = (mg[...] + inv * (e - mean_e - xhat * mean_ex)).astype(BF)


def unpack_ff(each, d, near, far, meta, up_o, down_o):
    for j in range(8):
        at = lax.bitwise_xor(meta[1], jnp.int32(j))
        rows = slice(j * each, j * each + each)

        @pl.when(at < 4)
        def _():
            block = near[jnp.minimum(at, 3)].astype(F32)
            up_o[rows, :] = block[:each]
            down_o[rows, :] = block[each:]

        @pl.when(at >= 4)
        def _():
            block = far[jnp.maximum(at - 4, 0)].astype(F32)
            up_o[rows, :] = block[:each]
            down_o[rows, :] = block[each:]


def unpack_attn(each, wide, near, far, meta, qkv_o, out_o, vec_o):
    for j in range(8):
        at = lax.bitwise_xor(meta[1], jnp.int32(j))
        r = j * each

        def put(block):
            if r < wide:
                qkv_o[r : r + each, :] = block[:each]
            else:
                out_o[r - wide : r - wide + each, :] = block[:each]
            vec_o[j : j + 1, :] = block[each : each + 1, :]

        @pl.when(at < 4)
        def _():
            put(near[jnp.minimum(at, 3)].astype(F32))

        @pl.when(at >= 4)
        def _():
            put(far[jnp.maximum(at - 4, 0)].astype(F32))


def on_device(
    tokens,
    clip_lengths,
    cotangent,
    query_key_value_weight,
    qv_bias,
    output_weight,
    out_bias,
    gain1,
    shift1,
    gain2,
    shift2,
    up_weight,
    hidden_bias,
    down_weight,
    down_bias,
):
    n_dp = lax.axis_size("dp")
    n_tensor = lax.axis_size("tensor")
    seqs, rows, d = tokens.shape
    length = rows * n_tensor
    heads = output_weight.shape[0] // HEAD_DIM
    wide = 3 * HEAD_DIM * heads
    hidden = up_weight.shape[1]
    blocks = 8
    each = d // blocks

    def core_swap(v):
        return lax.ppermute(v, "tensor", [(t, t ^ 1) for t in range(n_tensor)])

    def chip_swap(v):
        return lax.ppermute(v, "tensor", [(t, t ^ 2) for t in range(n_tensor)])

    t = lax.axis_index("tensor")
    dp_at = lax.axis_index("dp")
    orders = ((0, 1, 2), (1, 0, 2))
    if n_dp == 8:

        def place(order):
            return sum(((dp_at >> order[k]) & 1) << (2 - k) for k in range(3))

        label = jnp.where(t % 2 == 0, place(orders[0]), place(orders[1]))
    else:
        label = jnp.zeros_like(dp_at)
    meta = jnp.stack([t, label]).astype(jnp.int32)

    def add(a, b):
        return (a.astype(F32) + b.astype(F32)).astype(BF)

    def after(value, *others):
        return lax.optimization_barrier((value, others))[0]

    def step_perm(k):
        pairs = []
        for dev in range(n_dp):
            for s in range(n_tensor):
                other = dev ^ (1 << orders[s % 2][k])
                pairs.append((dev * n_tensor + s, other * n_tensor + s))
        return pairs

    def reduce_get(held, k):
        return lax.ppermute(held[held.shape[0] // 2 :], ("dp", "tensor"), step_perm(k))

    def gather_step(held, k):
        return lax.ppermute(held, ("dp", "tensor"), step_perm(k))

    def after(value, *others):
        return lax.optimization_barrier((value, others))[0]

    def step_perm(k):
        pairs = []
        for dev in range(n_dp):
            for s in range(n_tensor):
                other = dev ^ (1 << orders[s % 2][k])
                pairs.append((dev * n_tensor + s, other * n_tensor + s))
        return pairs

    def reduce_get(held, k):
        return lax.ppermute(held[held.shape[0] // 2 :], ("dp", "tensor"), step_perm(k))

    def reduce_step(held, k):
        return add(held[: held.shape[0] // 2], reduce_get(held, k))

    def gather_step(held, k):
        return lax.ppermute(held, ("dp", "tensor"), step_perm(k))

    def gather_all(held):
        for k in (2, 1):
            held = jnp.concatenate([held, gather_step(held, k)], axis=0)
        return held, gather_step(held, 0)

    def after(value, *others):
        return lax.optimization_barrier((value, others))[0]

    def step_perm(k):
        pairs = []
        for dev in range(n_dp):
            for s in range(n_tensor):
                other = dev ^ (1 << orders[s % 2][k])
                pairs.append((dev * n_tensor + s, other * n_tensor + s))
        return pairs

    def all_reduce(buf):
        if n_dp != 8:
            full = lax.psum(buf, "dp")
            return full[:4], full[4:]
        held = buf
        for k in range(3):
            half = held.shape[0] // 2
            got = lax.ppermute(held[half:], ("dp", "tensor"), step_perm(k))
            held = add(held[:half], got)
        for k in (2, 1):
            got = lax.ppermute(held, ("dp", "tensor"), step_perm(k))
            held = jnp.concatenate([held, got], axis=0)
        return held, lax.ppermute(held, ("dp", "tensor"), step_perm(0))

    def row(v):
        return v.reshape(1, -1)

    pairs = qv_bias.reshape(heads, 2, HEAD_DIM)
    bias = row(jnp.stack([pairs[:, 0], jnp.zeros_like(pairs[:, 0]), pairs[:, 1]], axis=1))
    g1, b1, g2, b2 = row(gain1), row(shift1), row(gain2), row(shift2)
    ob, hb = row(out_bias), row(hidden_bias)
    chip_at = t >> 1

    w_t = query_key_value_weight.T

    def spread(v, *first):
        near = core_swap(v)
        across = after(chip_swap(v), *first)
        return [v, near, across, core_swap(across)]

    def chip_sum(keep, send):
        return add(keep, core_swap(send))

    def all_rows(chip, far):
        own = add(chip, far)
        return [own, core_swap(own)]

    def peer_rows(keep, got):
        return add(keep[1 - chip_at], got[1 - chip_at])

    xs = spread(tokens, g1, b1, g2, b2, ob, hb, bias, meta)
    cot_near = core_swap(cotangent)
    beside = chip_swap(cotangent)

    kept, chips, fars = [], [], []
    for s in range(seqs):
        outs = run_a(
            s, heads, length, rows, d, meta, clip_lengths, after(xs, *chips[-1:]), g1, b1,
            w_t, bias, output_weight,
        )
        kept.append(outs[:3])
        if s == 0:
            beside = after(beside, outs[3])
            cots = [cotangent, cot_near, beside, core_swap(beside)]
        chips.append(chip_sum(outs[3], after(outs[4], beside)))
        beside = chip_swap(chips[s])
        fars.append(beside)

    mids, stats, ff_keep, ff_send, n_chips, n_fars = [], [], [], [], [], []
    carry = []
    for s in range(seqs):
        mids.append(all_rows(chips[s], fars[s]))
        outs = run_b(
            s, s == 0, s == seqs - 1, rows, d, hidden, blocks, meta, xs,
            after(mids[s], *(chips[-1:] + n_chips[-1:])), cots,
            ob, g2, b2, up_weight, hb, down_weight, carry,
        )
        n_chips.append(chip_sum(outs[2], after(outs[3], beside)))
        beside = chip_swap(n_chips[s])
        n_fars.append(beside)
        ff_keep.append(outs[0])
        ff_send.append(outs[1])
        stats.append(outs[4:6])
        carry = outs[6:]
    ff_grads, vec_b = carry

    moves = [("halve", 0), ("halve", 1), ("halve", 2), ("double", 2), ("double", 1)]

    def send_move(held):
        kind, k = moves[0]
        return reduce_get(held, k) if kind == "halve" else gather_step(held, k)

    def take_move(held, part):
        if moves.pop(0)[0] == "halve":
            return add(held[: held.shape[0] // 2], part)
        return jnp.concatenate([held, part], axis=0)

    by_hand = n_dp == 8 and seqs == 2
    backs, peers, far_rows = [], [], []
    carry = []
    held = ff_grads
    for s in range(seqs):
        last = s == seqs - 1
        far_now = after(n_fars[s], *[b[1] for b in backs[-1:]])
        n_now = after(all_rows(n_chips[s], far_now), *n_chips[-1:], held)
        mg, ag, dq, vec_a = run_c(
            s, heads, length, rows, d, clip_lengths.shape[1], meta, clip_lengths,
            [*n_now, *cots, *stats[s], g2, output_weight, kept[s][1]],
        )
        if by_hand:
            held = take_move(held, after(send_move(held), dq))
            dq = after(dq, held)
        outs = run_grads(
            s == 0, last, rows, blocks, wide, meta,
            [ag, dq, vec_a, kept[s][0], kept[s][2], w_t, g1, b1, *carry] + ([vec_b] if last else []),
        )
        keep, send = outs[:2]
        carry = outs[2:]
        waits = [] if last else [beside]
        if by_hand and last:
            part = send_move(held)
        elif by_hand:
            held = take_move(held, after(send_move(held), send))
        got = core_swap(after(send, *waits))
        peers.append(peer_rows(keep, got))
        beside = chip_swap(peers[s])
        far_rows.append(beside)
        backs.append((mg, keep, got))
    at_grads = carry[0]
    ff_got = [core_swap(after(send, vec_a)) for send in ff_send]
    ff_peers = [peer_rows(keep, got) for keep, got in zip(ff_keep, ff_got)]
    ff_far_rows = [chip_swap(v) for v in ff_peers]
    whole = pl.BlockSpec(memory_space=pltpu.VMEM)

    def input_rows(s):
        return pl.pallas_call(
            functools.partial(stage_d, s),
            out_shape=jax.ShapeDtypeStruct((rows, d), BF),
            in_specs=[pl.BlockSpec(memory_space=pltpu.SMEM)] + [whole] * 6,
            out_specs=whole,
            compiler_params=pltpu.CompilerParams(vmem_limit_bytes=16 << 20),
        )(meta, tokens, *backs[s], far_rows[s], g1)

    def output_rows(s):
        ff = ff_keep[s][chip_at].astype(F32) + ff_got[s][chip_at].astype(F32)
        middle = tokens[s].astype(F32) + mids[s][0][chip_at].astype(F32) + out_bias
        return (middle + (ff + ff_far_rows[s].astype(F32) + down_bias)).astype(BF)

    input_grad = jnp.stack([input_rows(s) for s in range(seqs)])
    block_out = jnp.stack([output_rows(s) for s in range(seqs)])
    if by_hand:
        at_held = add(at_grads[:4], after(reduce_get(at_grads, 0), *ff_peers))
        held = take_move(held, after(part, at_held))
        part = send_move(held)
        at_held = add(at_held[:2], reduce_get(at_held, 1))
        at_held = add(at_held[:1], reduce_get(at_held, 2))
        ff_near = take_move(held, after(part, at_held, input_grad))
        ff_far = gather_step(ff_near, 0)
        at_held = jnp.concatenate([at_held, gather_step(at_held, 2)], axis=0)
        part = after(gather_step(at_held, 1), block_out)
        at_near = jnp.concatenate([at_held, part], axis=0)
        at_far = gather_step(at_near, 0)
    else:
        ff_sum, at_sum = lax.psum((ff_grads, at_grads), "dp")
        ff_near, ff_far, at_near, at_far = ff_sum[:4], ff_sum[4:], at_sum[:4], at_sum[4:]

    def unpack(body, near, far, out_shape):
        whole = pl.BlockSpec(memory_space=pltpu.VMEM)
        return pl.pallas_call(
            body,
            out_shape=out_shape,
            in_specs=[whole, whole, pl.BlockSpec(memory_space=pltpu.SMEM)],
            out_specs=[whole] * len(out_shape),
            compiler_params=pltpu.CompilerParams(vmem_limit_bytes=24 << 20),
        )(near, far, meta)

    grad_up, grad_down = unpack(
        functools.partial(unpack_ff, each, d),
        ff_near,
        ff_far,
        [jax.ShapeDtypeStruct((d, hidden), F32), jax.ShapeDtypeStruct((hidden, d), F32)],
    )
    at_far = after(at_far, block_out, input_grad, grad_up, grad_down)

    def vec_row(j):
        at = label ^ j
        return jnp.where(at < 4, at_near[at & 3, each], at_far[at & 3, each]).astype(F32)

    norm1 = jnp.stack([vec_row(V_GAIN1), vec_row(V_SHIFT1)])
    across = lax.ppermute(norm1, "tensor", [(t, t ^ 3) for t in range(n_tensor)])
    near = core_swap(norm1)
    at_near = after(at_near, near)
    norm1 = (norm1 + near) + (chip_swap(norm1) + across)
    grad_qkv, grad_out, vec = unpack(
        functools.partial(unpack_attn, each, wide),
        at_near,
        at_far,
        [
            jax.ShapeDtypeStruct((wide, d), F32),
            jax.ShapeDtypeStruct((d - wide, d), F32),
            jax.ShapeDtypeStruct((8, d), F32),
        ],
    )
    qkv_sum = vec[V_QKV, :wide].reshape(heads, 3, HEAD_DIM)
    return (
        block_out,
        input_grad,
        grad_qkv.T,
        qkv_sum[:, ::2].reshape(-1),
        grad_out,
        vec[V_OUT],
        norm1[0],
        norm1[1],
        vec[V_GAIN2],
        vec[V_SHIFT2],
        grad_up,
        vec[V_UP],
        grad_down,
        vec[V_DOWN],
    )


def solution(mesh):
    placed = (
        P("dp", "tensor", None),
        P("dp", None),
        P("dp", "tensor", None),
        P(None, "tensor"),
        P("tensor"),
        P("tensor", None),
        P(),
        P(),
        P(),
        P(),
        P(),
        P(None, "tensor"),
        P("tensor"),
        P("tensor", None),
        P(),
    )
    return jax.shard_map(
        on_device,
        mesh=mesh,
        in_specs=placed,
        out_specs=(
            P("dp", "tensor", None),
            P("dp", "tensor", None),
            P(None, "tensor"),
            P("tensor"),
            P("tensor", None),
            P(),
            P(),
            P(),
            P(),
            P(),
            P(None, "tensor"),
            P("tensor"),
            P("tensor", None),
            P(),
        ),
        check_vma=False,
    )
```

```python
import functools

import jax
import jax.numpy as jnp
from jax import lax
from jax.experimental import pallas as pl
from jax.experimental.pallas import tpu as pltpu
from jax.sharding import PartitionSpec as P

HEAD_DIM = 64
EPS = 1e-06
SCALE = HEAD_DIM ** (-0.5)
BF = jnp.bfloat16
F32 = jnp.float32
LONGEST = 170
WINDOW = 192
MASKED = -1e30
VEC_ROWS = 8
COST_SCALE = 1
LIMIT_A, LIMIT_B, LIMIT_C = 20, 36, 32

V_UP, V_DOWN, V_GAIN2, V_SHIFT2, V_OUT, V_GAIN1, V_SHIFT1, V_QKV = range(8)


def dot_nn(a, b):
    return lax.dot_general(a, b, (((1,), (0,)), ((), ())), preferred_element_type=F32)


def dot_nt(a, b):
    return lax.dot_general(a, b, (((1,), (1,)), ((), ())), preferred_element_type=F32)


def dot_tn(a, b):
    return lax.dot_general(a, b, (((0,), (0,)), ((), ())), preferred_element_type=F32)


def call(body, out_shape, scalars, arrays, scratch, limit_mb, flops, far_in, far_out):
    whole = pl.BlockSpec(memory_space=pltpu.VMEM)
    far = pl.BlockSpec(memory_space=pltpu.HBM)
    moved = sum(a.size * a.dtype.itemsize for a in arrays) + sum(
        o.size * o.dtype.itemsize for o in out_shape
    )
    return pl.pallas_call(
        body,
        out_shape=[pltpu.HBM(o.shape, o.dtype) if i in far_out else o for i, o in enumerate(out_shape)],
        in_specs=[pl.BlockSpec(memory_space=pltpu.SMEM)] * len(scalars)
        + [far if i in far_in else whole for i in range(len(arrays))],
        out_specs=[far if i in far_out else whole for i in range(len(out_shape))],
        scratch_shapes=scratch,
        compiler_params=pltpu.CompilerParams(vmem_limit_bytes=limit_mb << 20),
        cost_estimate=pl.CostEstimate(flops=flops * COST_SCALE, transcendentals=0, bytes_accessed=moved),
    )(
        *scalars,
        *[
            pltpu.with_memory_space_constraint(a, pltpu.HBM) if i in far_in else a
            for i, a in enumerate(arrays)
        ],
    )


def sem(n):
    return pltpu.SemaphoreType.DMA((n,))


def vm(*shape, dtype=BF):
    return pltpu.VMEM(shape, dtype)


def copies(done, *pairs):
    made = [pltpu.make_async_copy(src, dst, done.at[i]) for i, (src, dst) in enumerate(pairs)]
    for c in made:
        c.start()
    return made


def block_start(meta, p, rows):
    return pl.multiple_of(lax.bitwise_xor(meta[0], jnp.int32(p)) * rows, rows)


def chip_slot(meta, p):
    return lax.bitwise_xor(meta[0] >> 1, jnp.int32(p >> 1))


def norm_rows(x):
    mean = jnp.mean(x, axis=-1, keepdims=True)
    centred = x - mean
    var = jnp.mean(centred * centred, axis=-1, keepdims=True)
    inv = lax.rsqrt(var + EPS)
    return centred * inv, inv


def phi_parts(u):
    cdf = 0.5 * (1.0 + lax.erf(u * 0.7071067811865476))
    return cdf, jnp.exp(u * u * -0.5) * 0.3989422804014327


def pad_range(clips, length):
    k0 = clips * 100 // 64 * 64
    step = 112 if (length - k0) % 112 == 0 else 64
    return k0, step, (length - k0) // step


def clip_start(first, length):
    return pl.multiple_of(jnp.minimum(first // 16 * 16, length - WINDOW), 16)


def stage_a(seq, heads, length, rows, meta, lens, *refs):
    x_refs, (g1, b1, w_h, bias, wo_h), refs = refs[:4], refs[4:9], refs[9:]
    normed_h, qkv_h, att_h, keep_o, send_o, x_s, w, wo, normed_o, qkv_o, att_o, in_sem, out_sem = refs
    clips = lens.shape[1]
    get = copies(
        in_sem,
        (x_refs[0].at[seq], x_s.at[0]),
        (w_h, w),
        *[(x_refs[p].at[seq], x_s.at[p]) for p in range(1, 4)],
        (wo_h, wo),
    )
    get[1].wait()
    for p in range(4):
        r0 = block_start(meta, p, rows)
        get[p + (p > 0)].wait()
        xhat, _ = norm_rows(x_s[p].astype(F32))
        nb = (xhat * g1[...] + b1[...]).astype(BF)
        normed_o[pl.ds(r0, rows), :] = nb
        qkv_o[pl.ds(r0, rows), :] = (dot_nt(nb, w[...]) + bias[...]).astype(BF)

    put = copies(out_sem, (normed_o, normed_h), (qkv_o, qkv_h))

    def attend(q0, q_rows, k0, k_rows, first, last):
        key_at = lax.broadcasted_iota(jnp.int32, (1, k_rows), 1) + k0
        allowed = (key_at >= first) & (key_at < last)
        row_at = lax.broadcasted_iota(jnp.int32, (q_rows, 1), 0) + q0
        scores, outs = [], []
        for h in range(heads):
            col = h * 3 * HEAD_DIM
            q = qkv_o[pl.ds(q0, q_rows), col : col + HEAD_DIM] * BF(SCALE)
            k = qkv_o[pl.ds(k0, k_rows), col + HEAD_DIM : col + 2 * HEAD_DIM]
            scores.append(dot_nt(q, k))
        for h in range(heads):
            v = qkv_o[pl.ds(k0, k_rows), (h * 3 + 2) * HEAD_DIM : (h * 3 + 3) * HEAD_DIM]
            s = jnp.where(allowed, scores[h], MASKED)
            e = jnp.exp(s - jnp.max(s, axis=1, keepdims=True))
            probs = (e * (1.0 / jnp.sum(e, axis=1, keepdims=True))).astype(BF)
            outs.append(dot_nn(probs, v).astype(BF))
        new = jnp.concatenate(outs, axis=1)
        old = att_o[pl.ds(q0, q_rows), :]
        att_o[pl.ds(q0, q_rows), :] = jnp.where(row_at >= first, new, old)

    def one_clip(c, first):
        last = first + lens[seq, c]
        w0 = clip_start(first, length)
        attend(w0, WINDOW, w0, WINDOW, first, last)
        return last

    first = lax.fori_loop(0, clips, one_clip, jnp.int32(0), unroll=2)
    k0, step, tiles = pad_range(clips, length)

    def pad_tile(i, carry):
        attend(pl.multiple_of(k0 + i * step, 16), step, k0, length - k0, first, length)
        return carry

    lax.fori_loop((first - k0) // step, tiles, pad_tile, jnp.int32(0))

    att_put = pltpu.make_async_copy(att_o, att_h, out_sem.at[2])
    att_put.start()
    get[5].wait()
    for p in range(4):
        r0 = block_start(meta, p, rows)
        part = dot_nn(att_o[pl.ds(r0, rows), :], wo[...]).astype(BF)
        (keep_o, send_o)[p & 1][chip_slot(meta, p)] = part
    for c in [*put, att_put]:
        c.wait()


def stage_b(seq, first_seq, last_seq, rows, blocks, meta, *refs):
    xs, ms, cots, refs = refs[:4], refs[4:6], refs[6:10], refs[10:]
    ob, g2, b2, wu_h, hb, wd_h = refs[:6]
    refs = refs[6:]
    if not first_seq:
        old_up, old_down, old_vec = refs[:3]
        refs = refs[3:]
    keep_fh, send_fh, keep_n, send_n, xhat_h, inv_h = refs[:6]
    refs = refs[6:]
    if last_seq:
        grads_o, vec_o = refs[:2]
        refs = refs[2:]
    else:
        up_o, down_o, vec_o = refs[:3]
        refs = refs[3:]
    n2_s, act_s, ug_s, cot_s, x_s, wu, wd, keep_f, send_f, xhat_o, inv_o, in_sem, out_sem = refs
    pieces = []
    for p in range(4):
        here = pl.ds(p * rows, rows)
        pieces += [(xs[p].at[seq], x_s.at[p]), (cots[p].at[seq], cot_s.at[here, :])]
        if p == 0:
            pieces += [(wu_h, wu), (wd_h, wd)]
    get = copies(in_sem, *pieces)
    get[2].wait()
    get[3].wait()
    d = wu.shape[0]
    up_sum = jnp.zeros((1, wu.shape[1]), F32)
    down_sum = jnp.zeros((1, d), F32)
    for p in range(4):
        slot = chip_slot(meta, p)
        here = slice(p * rows, p * rows + rows)
        for c in get[2 * p + 2 * (p > 0) : 2 * p + 2 * (p > 0) + 2]:
            c.wait()
        mid = x_s[p].astype(F32) + ms[p & 1][slot].astype(F32) + ob[...]
        xhat, inv = norm_rows(mid)
        xhat_o[here, :] = xhat.astype(BF)
        inv_o[here, :] = inv
        n2 = (xhat * g2[...] + b2[...]).astype(BF)
        n2_s[here, :] = n2
        u = dot_nn(n2, wu[...]) + hb[...]
        cdf, pdf = phi_parts(u)
        act = (u * cdf).astype(BF)
        act_s[here, :] = act
        (keep_f, send_f)[p & 1][slot] = dot_nn(act, wd[...]).astype(BF)
        cot = cot_s[here, :]
        down_sum = down_sum + jnp.sum(cot.astype(F32), axis=0, keepdims=True)
        ug = (dot_nt(cot, wd[...]) * (cdf + u * pdf)).astype(BF)
        ug_s[here, :] = ug
        up_sum = up_sum + jnp.sum(ug.astype(F32), axis=0, keepdims=True)
        (keep_n, send_n)[p & 1][slot] = dot_nt(ug, wu[...]).astype(BF)
    put = copies(
        out_sem, (keep_f, keep_fh), (send_f, send_fh), (xhat_o, xhat_h), (inv_o, inv_h)
    )
    grad_up = dot_tn(n2_s[...], ug_s[...])
    grad_down = dot_tn(act_s[...], cot_s[...])
    if not first_seq:
        grad_up = grad_up + old_up[...]
        grad_down = grad_down + old_down[...]
        up_sum = up_sum + old_vec[V_UP : V_UP + 1, :]
        down_sum = down_sum + old_vec[V_DOWN : V_DOWN + 1, :]
    vec_o[V_UP : V_UP + 1, :] = up_sum
    vec_o[V_DOWN : V_DOWN + 1, :] = down_sum
    if not last_seq:
        up_o[...] = grad_up
        down_o[...] = grad_down
    else:
        each = d // blocks
        for j in range(blocks):
            at = lax.bitwise_xor(meta[1], jnp.int32(j))
            grads_o[at, :each, :] = grad_up[j * each : j * each + each].astype(BF)
            grads_o[at, each:, :] = grad_down[j * each : j * each + each].astype(BF)
    for c in put:
        c.wait()


def stage_c(seq, heads, length, rows, meta, lens, *refs):
    ns, cots, refs = refs[:2], refs[2:6], refs[6:]
    xhat_h, inv_h, g2, wo_h, qkv_h, mg_h, ag_s, dq_s, vec_o = refs[:9]
    da_s, kv_acc, q_acc, cot_s, xhat_i, inv_i, wo, qkv, mg_o, in_sem, out_sem = refs[9:]
    pieces = []
    for p in range(4):
        here = pl.ds(p * rows, rows)
        pieces += [(cots[p].at[seq], cot_s.at[p])]
        pieces += [(ref.at[here, :], dst.at[here, :]) for ref, dst in ((xhat_h, xhat_i), (inv_h, inv_i))]
        if p == 0:
            pieces += [(wo_h, wo)]
    get = copies(in_sem, *pieces, (qkv_h, qkv))
    get[3].wait()
    clips = lens.shape[1]
    d = g2.shape[1]
    sums = {k: jnp.zeros((1, d), F32) for k in (V_GAIN2, V_SHIFT2, V_OUT)}
    for p in range(4):
        slot = chip_slot(meta, p)
        here = slice(p * rows, p * rows + rows)
        r0 = block_start(meta, p, rows)
        for c in [get[:3], get[4:13], [], []][p]:
            c.wait()
        n = ns[p & 1][slot].astype(F32)
        xhat = xhat_i[here, :].astype(F32)
        e = n * g2[...]
        mean_e = jnp.mean(e, axis=-1, keepdims=True)
        mean_ex = jnp.mean(e * xhat, axis=-1, keepdims=True)
        mg = cot_s[p].astype(F32) + inv_i[here, :] * (e - mean_e - xhat * mean_ex)
        if p == 0:
            mg_o[...] = mg
        ag = mg.astype(BF)
        ag_s[pl.ds(r0, rows), :] = ag
        da_s[pl.ds(r0, rows), :] = dot_nt(ag, wo[...]).astype(BF)
        sums[V_GAIN2] += jnp.sum(n * xhat, axis=0, keepdims=True)
        sums[V_SHIFT2] += jnp.sum(n, axis=0, keepdims=True)
        sums[V_OUT] += jnp.sum(ag.astype(F32), axis=0, keepdims=True)

    put = pltpu.make_async_copy(mg_o, mg_h, out_sem.at[0])
    put.start()
    get[13].wait()

    def attend_back(q0, q_rows, k0, k_rows, first, last):
        q_at = lax.broadcasted_iota(jnp.int32, (k_rows, q_rows), 1) + q0
        k_at = lax.broadcasted_iota(jnp.int32, (k_rows, q_rows), 0) + k0
        allowed = (k_at >= first) & (k_at < last) & (q_at >= first) & (q_at < last)
        qs, ks, dos, scores, prob_grads, sms, dss = [], [], [], [], [], [], []
        for h in range(heads):
            col = h * 3 * HEAD_DIM
            qs.append(qkv[pl.ds(q0, q_rows), col : col + HEAD_DIM] * BF(SCALE))
            ks.append(qkv[pl.ds(k0, k_rows), col + HEAD_DIM : col + 2 * HEAD_DIM])
            v = qkv[pl.ds(k0, k_rows), col + 2 * HEAD_DIM : col + 3 * HEAD_DIM]
            dos.append(da_s[pl.ds(q0, q_rows), h * HEAD_DIM : h * HEAD_DIM + HEAD_DIM])
            scores.append(dot_nt(ks[h], qs[h]))
            prob_grads.append(dot_nt(v, dos[h]))
        for h in range(heads):
            s = jnp.where(allowed, scores[h], MASKED)
            e = jnp.exp(s - jnp.max(s, axis=0, keepdims=True))
            sm = jnp.where(allowed, e * (1.0 / jnp.sum(e, axis=0, keepdims=True)), 0.0)
            t = sm * prob_grads[h]
            dss.append((t - sm * jnp.sum(t, axis=0, keepdims=True)).astype(BF))
            sms.append(sm.astype(BF))
        dv = [dot_nn(sms[h], dos[h]) for h in range(heads)]
        dk = [dot_nn(dss[h], qs[h]) for h in range(heads)]
        dq = [dot_tn(dss[h], ks[h]) * SCALE for h in range(heads)]
        return dq, dk, dv

    def one_clip(c, first):
        last = first + lens[seq, c]
        w0 = clip_start(first, length)
        dq, dk, dv = attend_back(w0, WINDOW, w0, WINDOW, first, last)
        new = jnp.concatenate(
            [part[h].astype(BF) for h in range(heads) for part in (dq, dk, dv)], axis=1
        )
        row_at = lax.broadcasted_iota(jnp.int32, (WINDOW, 1), 0) + w0
        old = dq_s[pl.ds(w0, WINDOW), :]
        dq_s[pl.ds(w0, WINDOW), :] = jnp.where(row_at >= first, new, old)
        return last

    first = lax.fori_loop(0, clips, one_clip, jnp.int32(0), unroll=2)
    k0, step, tiles = pad_range(clips, length)
    k_rows = length - k0
    kv_acc[...] = jnp.zeros_like(kv_acc)

    def pad_tile(i, carry):
        at = pl.multiple_of(i * step, 16)
        dq, dk, dv = attend_back(k0 + at, step, k0, k_rows, first, length)
        for h in range(heads):
            kv_acc[2 * h] += dk[h]
            kv_acc[2 * h + 1] += dv[h]
            q_acc[h, pl.ds(at, step), :] = dq[h].astype(BF)
        return carry

    lax.fori_loop((first - k0) // step, tiles, pad_tile, jnp.int32(0))
    new = jnp.concatenate(
        [
            part.astype(BF)
            for h in range(heads)
            for part in (q_acc[h], kv_acc[2 * h], kv_acc[2 * h + 1])
        ],
        axis=1,
    )
    row_at = lax.broadcasted_iota(jnp.int32, (k_rows, 1), 0) + k0
    dq_s[k0:, :] = jnp.where(row_at >= first, new, dq_s[k0:, :])
    for k in sums:
        vec_o[k : k + 1, :] = sums[k]
    put.wait()


def stage_grads(first_seq, last_seq, rows, blocks, meta, *refs):
    ag_s, dq_s, vec_a, normed_h, att_h, w_h, g1, b1 = refs[:8]
    refs = refs[8:]
    if not first_seq:
        old_qkv, old_out, old_vec = refs[:3]
        refs = refs[3:]
    if last_seq:
        vec_b, refs = refs[0], refs[1:]
    keep_o, send_o = refs[:2]
    refs = refs[2:]
    if last_seq:
        grads_o, refs = refs[0], refs[1:]
    else:
        qkv_o, out_o, vec_o = refs[:3]
        refs = refs[3:]
    normed, att, w, in_sem = refs
    get = copies(in_sem, (w_h, w), (normed_h, normed), (att_h, att))
    d = g1.shape[1]
    sums = {k: vec_a[k : k + 1, :] for k in (V_GAIN2, V_SHIFT2, V_OUT)}
    sums[V_GAIN1] = jnp.zeros((1, d), F32)
    sums[V_SHIFT1] = jnp.zeros((1, d), F32)
    for c in get:
        c.wait()
    grad_out = dot_tn(att[...], ag_s[...])
    grad_qkv = dot_tn(dq_s[...], normed[...])
    qkv_sum = jnp.sum(dq_s[...].astype(F32), axis=0, keepdims=True)
    for p in range(4):
        r0 = block_start(meta, p, rows)
        ng = dot_nn(dq_s[pl.ds(r0, rows), :], w[...])
        sums[V_SHIFT1] += jnp.sum(ng, axis=0, keepdims=True)
        sums[V_GAIN1] += jnp.sum(ng * normed[pl.ds(r0, rows), :].astype(F32), axis=0, keepdims=True)
        (keep_o, send_o)[p & 1][chip_slot(meta, p)] = ng.astype(BF)
    sums[V_GAIN1] = (sums[V_GAIN1] - b1[...] * sums[V_SHIFT1]) / g1[...]
    sums[V_QKV] = jnp.concatenate([qkv_sum, jnp.zeros((1, d - qkv_sum.shape[1]), F32)], axis=1)
    if not first_seq:
        grad_qkv = grad_qkv + old_qkv[...]
        grad_out = grad_out + old_out[...]
        for k in sums:
            sums[k] += old_vec[k : k + 1, :]
    if not last_seq:
        qkv_o[...] = grad_qkv
        out_o[...] = grad_out
        for k in sums:
            vec_o[k : k + 1, :] = sums[k]
        return
    for k in (V_UP, V_DOWN):
        sums[k] = vec_b[k : k + 1, :]
    each = d // blocks
    wide = grad_qkv.shape[0]
    for j in range(blocks):
        at = lax.bitwise_xor(meta[1], jnp.int32(j))
        r = j * each
        part = grad_qkv[r : r + each] if r < wide else grad_out[r - wide : r - wide + each]
        grads_o[at, :each, :] = part.astype(BF)
        grads_o[at, each:, :] = jnp.broadcast_to(sums[j], (VEC_ROWS, d)).astype(BF)


def run_a(seq, heads, length, rows, d, meta, lens, xs, g1, b1, w, bias, wo):
    wide, attn = 3 * heads * HEAD_DIM, heads * HEAD_DIM
    sd = jax.ShapeDtypeStruct
    return call(
        functools.partial(stage_a, seq, heads, length, rows),
        [sd((length, d), BF), sd((length, wide), BF), sd((length, attn), BF)]
        + [sd((2, rows, d), BF)] * 2,
        [meta, lens],
        [*xs, g1, b1, w, bias, wo],
        [vm(4, rows, d), vm(wide, d), vm(attn, d), vm(length, d), vm(length, wide)]
        + [vm(length, attn), sem(6), sem(3)],
        LIMIT_A,
        2 * length * d * (wide + attn) * 2,
        (0, 1, 2, 3, 6, 8),
        (0, 1, 2),
    )


def run_b(seq, first_seq, last_seq, rows, d, hidden, blocks, meta, xs, ms, cots, ob, g2, b2, wu, hb, wd, carry):
    sd = jax.ShapeDtypeStruct
    length = 4 * rows
    each = d // blocks
    return call(
        functools.partial(stage_b, seq, first_seq, last_seq, rows, blocks),
        [sd((2, rows, d), BF)] * 4
        + [sd((length, d), BF), sd((length, 1), F32)]
        + (
            [sd((blocks, 2 * each, d), BF)]
            if last_seq
            else [sd((d, hidden), F32), sd((hidden, d), F32)]
        )
        + [sd((8, d), F32)],
        [meta],
        [*xs, *ms, *cots, ob, g2, b2, wu, hb, wd, *carry],
        [pltpu.VMEM((length, d), BF), pltpu.VMEM((length, hidden), BF)]
        + [pltpu.VMEM((length, hidden), BF), pltpu.VMEM((length, d), BF)]
        + [vm(4, rows, d), vm(d, hidden), vm(hidden, d), vm(2, rows, d), vm(2, rows, d)]
        + [vm(length, d), vm(length, 1, dtype=F32), sem(10), sem(4)],
        LIMIT_B,
        12 * length * d * hidden,
        (0, 1, 2, 3, 6, 7, 8, 9, 13, 15),
        (0, 1, 4, 5),
    )


def run_c(seq, heads, length, rows, d, clips, meta, lens, arrays):
    sd = jax.ShapeDtypeStruct
    wide, attn = 3 * heads * HEAD_DIM, heads * HEAD_DIM
    k_rows = length - pad_range(clips, length)[0]
    return call(
        functools.partial(stage_c, seq, heads, length, rows),
        [sd((rows, d), F32), sd((length, d), BF), sd((length, wide), BF), sd((8, d), F32)],
        [meta, lens],
        arrays,
        [vm(length, attn), vm(2 * heads, k_rows, HEAD_DIM, dtype=F32), vm(heads, k_rows, HEAD_DIM)]
        + [vm(4, rows, d), vm(length, d), vm(length, 1, dtype=F32), vm(attn, d)]
        + [vm(length, wide), vm(rows, d, dtype=F32), sem(14), sem(1)],
        LIMIT_C,
        4 * length * d * attn * 2,
        (2, 3, 4, 5, 6, 7, 9, 10),
        (0,),
    )


def run_grads(first_seq, last_seq, rows, blocks, wide, meta, arrays):
    sd = jax.ShapeDtypeStruct
    length, d = arrays[0].shape
    attn = d - wide
    each = d // blocks
    return call(
        functools.partial(stage_grads, first_seq, last_seq, rows, blocks),
        [sd((2, rows, d), BF), sd((2, rows, d), BF)]
        + (
            [sd((blocks, each + VEC_ROWS, d), BF)]
            if last_seq
            else [sd((wide, d), F32), sd((attn, d), F32), sd((8, d), F32)]
        ),
        [meta],
        arrays,
        [vm(length, d), vm(length, attn), vm(wide, d), sem(3)],
        LIMIT_A,
        4 * length * d * d,
        (3, 4, 5),
        (),
    )


def stage_d(seq, meta, x, mg, keep, got, far, g1, out):
    xhat, inv = norm_rows(x[seq].astype(F32))
    slot = meta[0] >> 1
    n = keep[slot].astype(F32) + got[slot].astype(F32) + far[...].astype(F32)
    e = n * g1[...]
    mean_e = jnp.mean(e, axis=-1, keepdims=True)
    mean_ex = jnp.mean(e * xhat, axis=-1, keepdims=True)
    out[...] = (mg[...] + inv * (e - mean_e - xhat * mean_ex)).astype(BF)


def unpack_ff(each, d, near, far, meta, up_o, down_o):
    for j in range(8):
        at = lax.bitwise_xor(meta[1], jnp.int32(j))
        rows = slice(j * each, j * each + each)

        @pl.when(at < 4)
        def _():
            block = near[jnp.minimum(at, 3)].astype(F32)
            up_o[rows, :] = block[:each]
            down_o[rows, :] = block[each:]

        @pl.when(at >= 4)
        def _():
            block = far[jnp.maximum(at - 4, 0)].astype(F32)
            up_o[rows, :] = block[:each]
            down_o[rows, :] = block[each:]


def unpack_attn(each, wide, near, far, meta, qkv_o, out_o, vec_o):
    for j in range(8):
        at = lax.bitwise_xor(meta[1], jnp.int32(j))
        r = j * each

        def put(block):
            if r < wide:
                qkv_o[r : r + each, :] = block[:each]
            else:
                out_o[r - wide : r - wide + each, :] = block[:each]
            vec_o[j : j + 1, :] = block[each : each + 1, :]

        @pl.when(at < 4)
        def _():
            put(near[jnp.minimum(at, 3)].astype(F32))

        @pl.when(at >= 4)
        def _():
            put(far[jnp.maximum(at - 4, 0)].astype(F32))


def on_device(
    tokens,
    clip_lengths,
    cotangent,
    query_key_value_weight,
    qv_bias,
    output_weight,
    out_bias,
    gain1,
    shift1,
    gain2,
    shift2,
    up_weight,
    hidden_bias,
    down_weight,
    down_bias,
):
    n_dp = lax.axis_size("dp")
    n_tensor = lax.axis_size("tensor")
    seqs, rows, d = tokens.shape
    length = rows * n_tensor
    heads = output_weight.shape[0] // HEAD_DIM
    wide = 3 * HEAD_DIM * heads
    hidden = up_weight.shape[1]
    blocks = 8
    each = d // blocks

    def core_swap(v):
        return lax.ppermute(v, "tensor", [(t, t ^ 1) for t in range(n_tensor)])

    def chip_swap(v):
        return lax.ppermute(v, "tensor", [(t, t ^ 2) for t in range(n_tensor)])

    t = lax.axis_index("tensor")
    dp_at = lax.axis_index("dp")
    orders = ((0, 1, 2), (1, 0, 2))
    if n_dp == 8:

        def place(order):
            return sum(((dp_at >> order[k]) & 1) << (2 - k) for k in range(3))

        label = jnp.where(t % 2 == 0, place(orders[0]), place(orders[1]))
    else:
        label = jnp.zeros_like(dp_at)
    meta = jnp.stack([t, label]).astype(jnp.int32)

    def add(a, b):
        return (a.astype(F32) + b.astype(F32)).astype(BF)

    def after(value, *others):
        return lax.optimization_barrier((value, others))[0]

    def step_perm(k):
        pairs = []
        for dev in range(n_dp):
            for s in range(n_tensor):
                other = dev ^ (1 << orders[s % 2][k])
                pairs.append((dev * n_tensor + s, other * n_tensor + s))
        return pairs

    def reduce_get(held, k):
        return lax.ppermute(held[held.shape[0] // 2 :], ("dp", "tensor"), step_perm(k))

    def gather_step(held, k):
        return lax.ppermute(held, ("dp", "tensor"), step_perm(k))

    def after(value, *others):
        return lax.optimization_barrier((value, others))[0]

    def step_perm(k):
        pairs = []
        for dev in range(n_dp):
            for s in range(n_tensor):
                other = dev ^ (1 << orders[s % 2][k])
                pairs.append((dev * n_tensor + s, other * n_tensor + s))
        return pairs

    def reduce_get(held, k):
        return lax.ppermute(held[held.shape[0] // 2 :], ("dp", "tensor"), step_perm(k))

    def reduce_step(held, k):
        return add(held[: held.shape[0] // 2], reduce_get(held, k))

    def gather_step(held, k):
        return lax.ppermute(held, ("dp", "tensor"), step_perm(k))

    def gather_all(held):
        for k in (2, 1):
            held = jnp.concatenate([held, gather_step(held, k)], axis=0)
        return held, gather_step(held, 0)

    def after(value, *others):
        return lax.optimization_barrier((value, others))[0]

    def step_perm(k):
        pairs = []
        for dev in range(n_dp):
            for s in range(n_tensor):
                other = dev ^ (1 << orders[s % 2][k])
                pairs.append((dev * n_tensor + s, other * n_tensor + s))
        return pairs

    def all_reduce(buf):
        if n_dp != 8:
            full = lax.psum(buf, "dp")
            return full[:4], full[4:]
        held = buf
        for k in range(3):
            half = held.shape[0] // 2
            got = lax.ppermute(held[half:], ("dp", "tensor"), step_perm(k))
            held = add(held[:half], got)
        for k in (2, 1):
            got = lax.ppermute(held, ("dp", "tensor"), step_perm(k))
            held = jnp.concatenate([held, got], axis=0)
        return held, lax.ppermute(held, ("dp", "tensor"), step_perm(0))

    def row(v):
        return v.reshape(1, -1)

    pairs = qv_bias.reshape(heads, 2, HEAD_DIM)
    bias = row(jnp.stack([pairs[:, 0], jnp.zeros_like(pairs[:, 0]), pairs[:, 1]], axis=1))
    g1, b1, g2, b2 = row(gain1), row(shift1), row(gain2), row(shift2)
    ob, hb = row(out_bias), row(hidden_bias)
    chip_at = t >> 1

    w_t = query_key_value_weight.T

    def spread(v, *first):
        near = core_swap(v)
        across = after(chip_swap(v), *first)
        return [v, near, across, core_swap(across)]

    def chip_sum(keep, send):
        return add(keep, core_swap(send))

    def all_rows(chip, far):
        own = add(chip, far)
        return [own, core_swap(own)]

    def peer_rows(keep, got):
        return add(keep[1 - chip_at], got[1 - chip_at])

    xs = spread(tokens, g1, b1, g2, b2, ob, hb, bias, meta)
    cot_near = core_swap(cotangent)
    beside = chip_swap(cotangent)

    kept, chips, fars = [], [], []
    for s in range(seqs):
        outs = run_a(
            s, heads, length, rows, d, meta, clip_lengths, after(xs, *chips[-1:]), g1, b1,
            w_t, bias, output_weight,
        )
        kept.append(outs[:3])
        if s == 0:
            beside = after(beside, outs[3])
            cots = [cotangent, cot_near, beside, core_swap(beside)]
        chips.append(chip_sum(outs[3], after(outs[4], beside)))
        beside = chip_swap(chips[s])
        fars.append(beside)

    mids, stats, ff_keep, ff_send, n_chips, n_fars = [], [], [], [], [], []
    carry = []
    for s in range(seqs):
        mids.append(all_rows(chips[s], fars[s]))
        outs = run_b(
            s, s == 0, s == seqs - 1, rows, d, hidden, blocks, meta, xs,
            after(mids[s], *(chips[-1:] + n_chips[-1:])), cots,
            ob, g2, b2, up_weight, hb, down_weight, carry,
        )
        n_chips.append(chip_sum(outs[2], after(outs[3], beside)))
        beside = chip_swap(n_chips[s])
        n_fars.append(beside)
        ff_keep.append(outs[0])
        ff_send.append(outs[1])
        stats.append(outs[4:6])
        carry = outs[6:]
    ff_grads, vec_b = carry

    moves = [("halve", 0), ("halve", 1), ("halve", 2), ("double", 2), ("double", 1)]

    def send_move(held):
        kind, k = moves[0]
        return reduce_get(held, k) if kind == "halve" else gather_step(held, k)

    def take_move(held, part):
        if moves.pop(0)[0] == "halve":
            return add(held[: held.shape[0] // 2], part)
        return jnp.concatenate([held, part], axis=0)

    by_hand = n_dp == 8 and seqs == 2
    backs, peers, far_rows = [], [], []
    carry = []
    held = ff_grads
    for s in range(seqs):
        last = s == seqs - 1
        far_now = after(n_fars[s], *[b[1] for b in backs[-1:]])
        n_now = after(all_rows(n_chips[s], far_now), *n_chips[-1:], held)
        mg, ag, dq, vec_a = run_c(
            s, heads, length, rows, d, clip_lengths.shape[1], meta, clip_lengths,
            [*n_now, *cots, *stats[s], g2, output_weight, kept[s][1]],
        )
        if by_hand:
            held = take_move(held, after(send_move(held), dq))
            dq = after(dq, held)
        outs = run_grads(
            s == 0, last, rows, blocks, wide, meta,
            [ag, dq, vec_a, kept[s][0], kept[s][2], w_t, g1, b1, *carry] + ([vec_b] if last else []),
        )
        keep, send = outs[:2]
        carry = outs[2:]
        waits = [] if last else [beside]
        if by_hand and last:
            part = send_move(held)
        elif by_hand:
            held = take_move(held, after(send_move(held), send))
        got = core_swap(after(send, *waits))
        peers.append(peer_rows(keep, got))
        beside = chip_swap(peers[s])
        far_rows.append(beside)
        backs.append((mg, keep, got))
    at_grads = carry[0]
    ff_got = [core_swap(after(send, vec_a)) for send in ff_send]
    ff_peers = [peer_rows(keep, got) for keep, got in zip(ff_keep, ff_got)]
    ff_far_rows = [chip_swap(v) for v in ff_peers]
    whole = pl.BlockSpec(memory_space=pltpu.VMEM)

    def input_rows(s):
        return pl.pallas_call(
            functools.partial(stage_d, s),
            out_shape=jax.ShapeDtypeStruct((rows, d), BF),
            in_specs=[pl.BlockSpec(memory_space=pltpu.SMEM)] + [whole] * 6,
            out_specs=whole,
            compiler_params=pltpu.CompilerParams(vmem_limit_bytes=16 << 20),
        )(meta, tokens, *backs[s], far_rows[s], g1)

    def output_rows(s):
        ff = ff_keep[s][chip_at].astype(F32) + ff_got[s][chip_at].astype(F32)
        middle = tokens[s].astype(F32) + mids[s][0][chip_at].astype(F32) + out_bias
        return (middle + (ff + ff_far_rows[s].astype(F32) + down_bias)).astype(BF)

    input_grad = jnp.stack([input_rows(s) for s in range(seqs)])
    block_out = jnp.stack([output_rows(s) for s in range(seqs)])
    if by_hand:
        at_held = add(at_grads[:4], after(reduce_get(at_grads, 0), *ff_peers))
        held = take_move(held, after(part, at_held))
        part = send_move(held)
        at_held = add(at_held[:2], reduce_get(at_held, 1))
        at_held = add(at_held[:1], reduce_get(at_held, 2))
        ff_near = take_move(held, after(part, at_held, input_grad))
        ff_far = gather_step(ff_near, 0)
        at_held = jnp.concatenate([at_held, gather_step(at_held, 2)], axis=0)
        part = after(gather_step(at_held, 1), block_out)
        at_near = jnp.concatenate([at_held, part], axis=0)
        at_far = gather_step(at_near, 0)
    else:
        ff_sum, at_sum = lax.psum((ff_grads, at_grads), "dp")
        ff_near, ff_far, at_near, at_far = ff_sum[:4], ff_sum[4:], at_sum[:4], at_sum[4:]

    def unpack(body, near, far, out_shape):
        whole = pl.BlockSpec(memory_space=pltpu.VMEM)
        return pl.pallas_call(
            body,
            out_shape=out_shape,
            in_specs=[whole, whole, pl.BlockSpec(memory_space=pltpu.SMEM)],
            out_specs=[whole] * len(out_shape),
            compiler_params=pltpu.CompilerParams(vmem_limit_bytes=24 << 20),
        )(near, far, meta)

    grad_up, grad_down = unpack(
        functools.partial(unpack_ff, each, d),
        ff_near,
        ff_far,
        [jax.ShapeDtypeStruct((d, hidden), F32), jax.ShapeDtypeStruct((hidden, d), F32)],
    )
    at_far = after(at_far, block_out, input_grad, grad_up, grad_down)

    def vec_row(j):
        at = label ^ j
        return jnp.where(at < 4, at_near[at & 3, each], at_far[at & 3, each]).astype(F32)

    norm1 = jnp.stack([vec_row(V_GAIN1), vec_row(V_SHIFT1)])
    across = lax.ppermute(norm1, "tensor", [(t, t ^ 3) for t in range(n_tensor)])
    near = core_swap(norm1)
    at_near = after(at_near, near)
    norm1 = (norm1 + near) + (chip_swap(norm1) + across)
    grad_qkv, grad_out, vec = unpack(
        functools.partial(unpack_attn, each, wide),
        at_near,
        at_far,
        [
            jax.ShapeDtypeStruct((wide, d), F32),
            jax.ShapeDtypeStruct((d - wide, d), F32),
            jax.ShapeDtypeStruct((8, d), F32),
        ],
    )
    qkv_sum = vec[V_QKV, :wide].reshape(heads, 3, HEAD_DIM)
    return (
        block_out,
        input_grad,
        grad_qkv.T,
        qkv_sum[:, ::2].reshape(-1),
        grad_out,
        vec[V_OUT],
        norm1[0],
        norm1[1],
        vec[V_GAIN2],
        vec[V_SHIFT2],
        grad_up,
        vec[V_UP],
        grad_down,
        vec[V_DOWN],
    )


def solution(mesh):
    placed = (
        P("dp", "tensor", None),
        P("dp", None),
        P("dp", "tensor", None),
        P(None, "tensor"),
        P("tensor"),
        P("tensor", None),
        P(),
        P(),
        P(),
        P(),
        P(),
        P(None, "tensor"),
        P("tensor"),
        P("tensor", None),
        P(),
    )
    return jax.shard_map(
        on_device,
        mesh=mesh,
        in_specs=placed,
        out_specs=(
            P("dp", "tensor", None),
            P("dp", "tensor", None),
            P(None, "tensor"),
            P("tensor"),
            P("tensor", None),
            P(),
            P(),
            P(),
            P(),
            P(),
            P(None, "tensor"),
            P("tensor"),
            P("tensor", None),
            P(),
        ),
        check_vma=False,
    )
```

```python
import functools

import jax
import jax.numpy as jnp
from jax import lax
from jax.experimental import pallas as pl
from jax.experimental.pallas import tpu as pltpu
from jax.sharding import PartitionSpec as P

HEAD_DIM = 64
EPS = 1e-06
SCALE = HEAD_DIM ** (-0.5)
BF = jnp.bfloat16
F32 = jnp.float32
LONGEST = 170
WINDOW = 192
MASKED = -1e30
VEC_ROWS = 8
COST_SCALE = 1
LIMIT_A, LIMIT_B, LIMIT_C = 20, 36, 32

V_UP, V_DOWN, V_GAIN2, V_SHIFT2, V_OUT, V_GAIN1, V_SHIFT1, V_QKV = range(8)


def dot_nn(a, b):
    return lax.dot_general(a, b, (((1,), (0,)), ((), ())), preferred_element_type=F32)


def dot_nt(a, b):
    return lax.dot_general(a, b, (((1,), (1,)), ((), ())), preferred_element_type=F32)


def dot_tn(a, b):
    return lax.dot_general(a, b, (((0,), (0,)), ((), ())), preferred_element_type=F32)


def call(body, out_shape, scalars, arrays, scratch, limit_mb, flops, far_in, far_out):
    whole = pl.BlockSpec(memory_space=pltpu.VMEM)
    far = pl.BlockSpec(memory_space=pltpu.HBM)
    moved = sum(a.size * a.dtype.itemsize for a in arrays) + sum(
        o.size * o.dtype.itemsize for o in out_shape
    )
    return pl.pallas_call(
        body,
        out_shape=[pltpu.HBM(o.shape, o.dtype) if i in far_out else o for i, o in enumerate(out_shape)],
        in_specs=[pl.BlockSpec(memory_space=pltpu.SMEM)] * len(scalars)
        + [far if i in far_in else whole for i in range(len(arrays))],
        out_specs=[far if i in far_out else whole for i in range(len(out_shape))],
        scratch_shapes=scratch,
        compiler_params=pltpu.CompilerParams(vmem_limit_bytes=limit_mb << 20),
        cost_estimate=pl.CostEstimate(flops=flops * COST_SCALE, transcendentals=0, bytes_accessed=moved),
    )(
        *scalars,
        *[
            pltpu.with_memory_space_constraint(a, pltpu.HBM) if i in far_in else a
            for i, a in enumerate(arrays)
        ],
    )


def sem(n):
    return pltpu.SemaphoreType.DMA((n,))


def vm(*shape, dtype=BF):
    return pltpu.VMEM(shape, dtype)


def copies(done, *pairs):
    made = [pltpu.make_async_copy(src, dst, done.at[i]) for i, (src, dst) in enumerate(pairs)]
    for c in made:
        c.start()
    return made


def block_start(meta, p, rows):
    return pl.multiple_of(lax.bitwise_xor(meta[0], jnp.int32(p)) * rows, rows)


def chip_slot(meta, p):
    return lax.bitwise_xor(meta[0] >> 1, jnp.int32(p >> 1))


def norm_rows(x):
    mean = jnp.mean(x, axis=-1, keepdims=True)
    centred = x - mean
    var = jnp.mean(centred * centred, axis=-1, keepdims=True)
    inv = lax.rsqrt(var + EPS)
    return centred * inv, inv


def phi_parts(u):
    cdf = 0.5 * (1.0 + lax.erf(u * 0.7071067811865476))
    return cdf, jnp.exp(u * u * -0.5) * 0.3989422804014327


def pad_range(clips, length):
    k0 = clips * 100 // 64 * 64
    step = 112 if (length - k0) % 112 == 0 else 64
    return k0, step, (length - k0) // step


def clip_start(first, length):
    return pl.multiple_of(jnp.minimum(first // 16 * 16, length - WINDOW), 16)


def stage_a(seq, heads, length, rows, meta, lens, *refs):
    x_refs, (g1, b1, w_h, bias, wo_h), refs = refs[:4], refs[4:9], refs[9:]
    normed_h, qkv_h, att_h, keep_o, send_o, x_s, w, wo, normed_o, qkv_o, att_o, in_sem, out_sem = refs
    clips = lens.shape[1]
    get = copies(
        in_sem,
        (x_refs[0].at[seq], x_s.at[0]),
        (w_h, w),
        *[(x_refs[p].at[seq], x_s.at[p]) for p in range(1, 4)],
        (wo_h, wo),
    )
    get[1].wait()
    for p in range(4):
        r0 = block_start(meta, p, rows)
        get[p + (p > 0)].wait()
        xhat, _ = norm_rows(x_s[p].astype(F32))
        nb = (xhat * g1[...] + b1[...]).astype(BF)
        normed_o[pl.ds(r0, rows), :] = nb
        qkv_o[pl.ds(r0, rows), :] = (dot_nt(nb, w[...]) + bias[...]).astype(BF)

    put = copies(out_sem, (normed_o, normed_h), (qkv_o, qkv_h))

    def attend(q0, q_rows, k0, k_rows, first, last):
        key_at = lax.broadcasted_iota(jnp.int32, (1, k_rows), 1) + k0
        allowed = (key_at >= first) & (key_at < last)
        row_at = lax.broadcasted_iota(jnp.int32, (q_rows, 1), 0) + q0
        scores, outs = [], []
        for h in range(heads):
            col = h * 3 * HEAD_DIM
            q = qkv_o[pl.ds(q0, q_rows), col : col + HEAD_DIM] * BF(SCALE)
            k = qkv_o[pl.ds(k0, k_rows), col + HEAD_DIM : col + 2 * HEAD_DIM]
            scores.append(dot_nt(q, k))
        for h in range(heads):
            v = qkv_o[pl.ds(k0, k_rows), (h * 3 + 2) * HEAD_DIM : (h * 3 + 3) * HEAD_DIM]
            s = jnp.where(allowed, scores[h], MASKED)
            e = jnp.exp(s - jnp.max(s, axis=1, keepdims=True))
            probs = (e * (1.0 / jnp.sum(e, axis=1, keepdims=True))).astype(BF)
            outs.append(dot_nn(probs, v).astype(BF))
        new = jnp.concatenate(outs, axis=1)
        old = att_o[pl.ds(q0, q_rows), :]
        att_o[pl.ds(q0, q_rows), :] = jnp.where(row_at >= first, new, old)

    def one_clip(c, first):
        last = first + lens[seq, c]
        w0 = clip_start(first, length)
        attend(w0, WINDOW, w0, WINDOW, first, last)
        return last

    first = lax.fori_loop(0, clips, one_clip, jnp.int32(0), unroll=3)
    k0, step, tiles = pad_range(clips, length)

    def pad_tile(i, carry):
        attend(pl.multiple_of(k0 + i * step, 16), step, k0, length - k0, first, length)
        return carry

    lax.fori_loop((first - k0) // step, tiles, pad_tile, jnp.int32(0))

    att_put = pltpu.make_async_copy(att_o, att_h, out_sem.at[2])
    att_put.start()
    get[5].wait()
    for p in range(4):
        r0 = block_start(meta, p, rows)
        part = dot_nn(att_o[pl.ds(r0, rows), :], wo[...]).astype(BF)
        (keep_o, send_o)[p & 1][chip_slot(meta, p)] = part
    for c in [*put, att_put]:
        c.wait()


def stage_b(seq, first_seq, last_seq, rows, blocks, meta, *refs):
    xs, ms, cots, refs = refs[:4], refs[4:6], refs[6:10], refs[10:]
    ob, g2, b2, wu_h, hb, wd_h = refs[:6]
    refs = refs[6:]
    if not first_seq:
        old_up, old_down, old_vec = refs[:3]
        refs = refs[3:]
    keep_fh, send_fh, keep_n, send_n, xhat_h, inv_h = refs[:6]
    refs = refs[6:]
    if last_seq:
        grads_o, vec_o = refs[:2]
        refs = refs[2:]
    else:
        up_o, down_o, vec_o = refs[:3]
        refs = refs[3:]
    n2_s, act_s, ug_s, cot_s, x_s, wu, wd, keep_f, send_f, xhat_o, inv_o, in_sem, out_sem = refs
    pieces = []
    for p in range(4):
        here = pl.ds(p * rows, rows)
        pieces += [(xs[p].at[seq], x_s.at[p]), (cots[p].at[seq], cot_s.at[here, :])]
        if p == 0:
            pieces += [(wu_h, wu), (wd_h, wd)]
    get = copies(in_sem, *pieces)
    get[2].wait()
    get[3].wait()
    d = wu.shape[0]
    up_sum = jnp.zeros((1, wu.shape[1]), F32)
    down_sum = jnp.zeros((1, d), F32)
    for p in range(4):
        slot = chip_slot(meta, p)
        here = slice(p * rows, p * rows + rows)
        for c in get[2 * p + 2 * (p > 0) : 2 * p + 2 * (p > 0) + 2]:
            c.wait()
        mid = x_s[p].astype(F32) + ms[p & 1][slot].astype(F32) + ob[...]
        xhat, inv = norm_rows(mid)
        xhat_o[here, :] = xhat.astype(BF)
        inv_o[here, :] = inv
        n2 = (xhat * g2[...] + b2[...]).astype(BF)
        n2_s[here, :] = n2
        u = dot_nn(n2, wu[...]) + hb[...]
        cdf, pdf = phi_parts(u)
        act = (u * cdf).astype(BF)
        act_s[here, :] = act
        (keep_f, send_f)[p & 1][slot] = dot_nn(act, wd[...]).astype(BF)
        cot = cot_s[here, :]
        down_sum = down_sum + jnp.sum(cot.astype(F32), axis=0, keepdims=True)
        ug = (dot_nt(cot, wd[...]) * (cdf + u * pdf)).astype(BF)
        ug_s[here, :] = ug
        up_sum = up_sum + jnp.sum(ug.astype(F32), axis=0, keepdims=True)
        (keep_n, send_n)[p & 1][slot] = dot_nt(ug, wu[...]).astype(BF)
    put = copies(
        out_sem, (keep_f, keep_fh), (send_f, send_fh), (xhat_o, xhat_h), (inv_o, inv_h)
    )
    grad_up = dot_tn(n2_s[...], ug_s[...])
    grad_down = dot_tn(act_s[...], cot_s[...])
    if not first_seq:
        grad_up = grad_up + old_up[...]
        grad_down = grad_down + old_down[...]
        up_sum = up_sum + old_vec[V_UP : V_UP + 1, :]
        down_sum = down_sum + old_vec[V_DOWN : V_DOWN + 1, :]
    vec_o[V_UP : V_UP + 1, :] = up_sum
    vec_o[V_DOWN : V_DOWN + 1, :] = down_sum
    if not last_seq:
        up_o[...] = grad_up
        down_o[...] = grad_down
    else:
        each = d // blocks
        for j in range(blocks):
            at = lax.bitwise_xor(meta[1], jnp.int32(j))
            grads_o[at, :each, :] = grad_up[j * each : j * each + each].astype(BF)
            grads_o[at, each:, :] = grad_down[j * each : j * each + each].astype(BF)
    for c in put:
        c.wait()


def stage_c(seq, heads, length, rows, meta, lens, *refs):
    ns, cots, refs = refs[:2], refs[2:6], refs[6:]
    xhat_h, inv_h, g2, wo_h, qkv_h, mg_h, ag_s, dq_s, vec_o = refs[:9]
    da_s, kv_acc, q_acc, cot_s, xhat_i, inv_i, wo, qkv, mg_o, in_sem, out_sem = refs[9:]
    pieces = []
    for p in range(4):
        here = pl.ds(p * rows, rows)
        pieces += [(cots[p].at[seq], cot_s.at[p])]
        pieces += [(ref.at[here, :], dst.at[here, :]) for ref, dst in ((xhat_h, xhat_i), (inv_h, inv_i))]
        if p == 0:
            pieces += [(wo_h, wo)]
    get = copies(in_sem, *pieces, (qkv_h, qkv))
    get[3].wait()
    clips = lens.shape[1]
    d = g2.shape[1]
    sums = {k: jnp.zeros((1, d), F32) for k in (V_GAIN2, V_SHIFT2, V_OUT)}
    for p in range(4):
        slot = chip_slot(meta, p)
        here = slice(p * rows, p * rows + rows)
        r0 = block_start(meta, p, rows)
        for c in [get[:3], get[4:13], [], []][p]:
            c.wait()
        n = ns[p & 1][slot].astype(F32)
        xhat = xhat_i[here, :].astype(F32)
        e = n * g2[...]
        mean_e = jnp.mean(e, axis=-1, keepdims=True)
        mean_ex = jnp.mean(e * xhat, axis=-1, keepdims=True)
        mg = cot_s[p].astype(F32) + inv_i[here, :] * (e - mean_e - xhat * mean_ex)
        if p == 0:
            mg_o[...] = mg
        ag = mg.astype(BF)
        ag_s[pl.ds(r0, rows), :] = ag
        da_s[pl.ds(r0, rows), :] = dot_nt(ag, wo[...]).astype(BF)
        sums[V_GAIN2] += jnp.sum(n * xhat, axis=0, keepdims=True)
        sums[V_SHIFT2] += jnp.sum(n, axis=0, keepdims=True)
        sums[V_OUT] += jnp.sum(ag.astype(F32), axis=0, keepdims=True)

    put = pltpu.make_async_copy(mg_o, mg_h, out_sem.at[0])
    put.start()
    get[13].wait()

    def attend_back(q0, q_rows, k0, k_rows, first, last):
        q_at = lax.broadcasted_iota(jnp.int32, (k_rows, q_rows), 1) + q0
        k_at = lax.broadcasted_iota(jnp.int32, (k_rows, q_rows), 0) + k0
        allowed = (k_at >= first) & (k_at < last) & (q_at >= first) & (q_at < last)
        qs, ks, dos, scores, prob_grads, sms, dss = [], [], [], [], [], [], []
        for h in range(heads):
            col = h * 3 * HEAD_DIM
            qs.append(qkv[pl.ds(q0, q_rows), col : col + HEAD_DIM] * BF(SCALE))
            ks.append(qkv[pl.ds(k0, k_rows), col + HEAD_DIM : col + 2 * HEAD_DIM])
            v = qkv[pl.ds(k0, k_rows), col + 2 * HEAD_DIM : col + 3 * HEAD_DIM]
            dos.append(da_s[pl.ds(q0, q_rows), h * HEAD_DIM : h * HEAD_DIM + HEAD_DIM])
            scores.append(dot_nt(ks[h], qs[h]))
            prob_grads.append(dot_nt(v, dos[h]))
        for h in range(heads):
            s = jnp.where(allowed, scores[h], MASKED)
            e = jnp.exp(s - jnp.max(s, axis=0, keepdims=True))
            sm = jnp.where(allowed, e * (1.0 / jnp.sum(e, axis=0, keepdims=True)), 0.0)
            t = sm * prob_grads[h]
            dss.append((t - sm * jnp.sum(t, axis=0, keepdims=True)).astype(BF))
            sms.append(sm.astype(BF))
        dv = [dot_nn(sms[h], dos[h]) for h in range(heads)]
        dk = [dot_nn(dss[h], qs[h]) for h in range(heads)]
        dq = [dot_tn(dss[h], ks[h]) * SCALE for h in range(heads)]
        return dq, dk, dv

    def one_clip(c, first):
        last = first + lens[seq, c]
        w0 = clip_start(first, length)
        dq, dk, dv = attend_back(w0, WINDOW, w0, WINDOW, first, last)
        new = jnp.concatenate(
            [part[h].astype(BF) for h in range(heads) for part in (dq, dk, dv)], axis=1
        )
        row_at = lax.broadcasted_iota(jnp.int32, (WINDOW, 1), 0) + w0
        old = dq_s[pl.ds(w0, WINDOW), :]
        dq_s[pl.ds(w0, WINDOW), :] = jnp.where(row_at >= first, new, old)
        return last

    first = lax.fori_loop(0, clips, one_clip, jnp.int32(0), unroll=3)
    k0, step, tiles = pad_range(clips, length)
    k_rows = length - k0
    kv_acc[...] = jnp.zeros_like(kv_acc)

    def pad_tile(i, carry):
        at = pl.multiple_of(i * step, 16)
        dq, dk, dv = attend_back(k0 + at, step, k0, k_rows, first, length)
        for h in range(heads):
            kv_acc[2 * h] += dk[h]
            kv_acc[2 * h + 1] += dv[h]
            q_acc[h, pl.ds(at, step), :] = dq[h].astype(BF)
        return carry

    lax.fori_loop((first - k0) // step, tiles, pad_tile, jnp.int32(0))
    new = jnp.concatenate(
        [
            part.astype(BF)
            for h in range(heads)
            for part in (q_acc[h], kv_acc[2 * h], kv_acc[2 * h + 1])
        ],
        axis=1,
    )
    row_at = lax.broadcasted_iota(jnp.int32, (k_rows, 1), 0) + k0
    dq_s[k0:, :] = jnp.where(row_at >= first, new, dq_s[k0:, :])
    for k in sums:
        vec_o[k : k + 1, :] = sums[k]
    put.wait()


def stage_grads(first_seq, last_seq, rows, blocks, meta, *refs):
    ag_s, dq_s, vec_a, normed_h, att_h, w_h, g1, b1 = refs[:8]
    refs = refs[8:]
    if not first_seq:
        old_qkv, old_out, old_vec = refs[:3]
        refs = refs[3:]
    if last_seq:
        vec_b, refs = refs[0], refs[1:]
    keep_o, send_o = refs[:2]
    refs = refs[2:]
    if last_seq:
        grads_o, refs = refs[0], refs[1:]
    else:
        qkv_o, out_o, vec_o = refs[:3]
        refs = refs[3:]
    normed, att, w, in_sem = refs
    get = copies(in_sem, (w_h, w), (normed_h, normed), (att_h, att))
    d = g1.shape[1]
    sums = {k: vec_a[k : k + 1, :] for k in (V_GAIN2, V_SHIFT2, V_OUT)}
    sums[V_GAIN1] = jnp.zeros((1, d), F32)
    sums[V_SHIFT1] = jnp.zeros((1, d), F32)
    for c in get:
        c.wait()
    grad_out = dot_tn(att[...], ag_s[...])
    grad_qkv = dot_tn(dq_s[...], normed[...])
    qkv_sum = jnp.sum(dq_s[...].astype(F32), axis=0, keepdims=True)
    for p in range(4):
        r0 = block_start(meta, p, rows)
        ng = dot_nn(dq_s[pl.ds(r0, rows), :], w[...])
        sums[V_SHIFT1] += jnp.sum(ng, axis=0, keepdims=True)
        sums[V_GAIN1] += jnp.sum(ng * normed[pl.ds(r0, rows), :].astype(F32), axis=0, keepdims=True)
        (keep_o, send_o)[p & 1][chip_slot(meta, p)] = ng.astype(BF)
    sums[V_GAIN1] = (sums[V_GAIN1] - b1[...] * sums[V_SHIFT1]) / g1[...]
    sums[V_QKV] = jnp.concatenate([qkv_sum, jnp.zeros((1, d - qkv_sum.shape[1]), F32)], axis=1)
    if not first_seq:
        grad_qkv = grad_qkv + old_qkv[...]
        grad_out = grad_out + old_out[...]
        for k in sums:
            sums[k] += old_vec[k : k + 1, :]
    if not last_seq:
        qkv_o[...] = grad_qkv
        out_o[...] = grad_out
        for k in sums:
            vec_o[k : k + 1, :] = sums[k]
        return
    for k in (V_UP, V_DOWN):
        sums[k] = vec_b[k : k + 1, :]
    each = d // blocks
    wide = grad_qkv.shape[0]
    for j in range(blocks):
        at = lax.bitwise_xor(meta[1], jnp.int32(j))
        r = j * each
        part = grad_qkv[r : r + each] if r < wide else grad_out[r - wide : r - wide + each]
        grads_o[at, :each, :] = part.astype(BF)
        grads_o[at, each:, :] = jnp.broadcast_to(sums[j], (VEC_ROWS, d)).astype(BF)


def run_a(seq, heads, length, rows, d, meta, lens, xs, g1, b1, w, bias, wo):
    wide, attn = 3 * heads * HEAD_DIM, heads * HEAD_DIM
    sd = jax.ShapeDtypeStruct
    return call(
        functools.partial(stage_a, seq, heads, length, rows),
        [sd((length, d), BF), sd((length, wide), BF), sd((length, attn), BF)]
        + [sd((2, rows, d), BF)] * 2,
        [meta, lens],
        [*xs, g1, b1, w, bias, wo],
        [vm(4, rows, d), vm(wide, d), vm(attn, d), vm(length, d), vm(length, wide)]
        + [vm(length, attn), sem(6), sem(3)],
        LIMIT_A,
        2 * length * d * (wide + attn) * 2,
        (0, 1, 2, 3, 6, 8),
        (0, 1, 2),
    )


def run_b(seq, first_seq, last_seq, rows, d, hidden, blocks, meta, xs, ms, cots, ob, g2, b2, wu, hb, wd, carry):
    sd = jax.ShapeDtypeStruct
    length = 4 * rows
    each = d // blocks
    return call(
        functools.partial(stage_b, seq, first_seq, last_seq, rows, blocks),
        [sd((2, rows, d), BF)] * 4
        + [sd((length, d), BF), sd((length, 1), F32)]
        + (
            [sd((blocks, 2 * each, d), BF)]
            if last_seq
            else [sd((d, hidden), F32), sd((hidden, d), F32)]
        )
        + [sd((8, d), F32)],
        [meta],
        [*xs, *ms, *cots, ob, g2, b2, wu, hb, wd, *carry],
        [pltpu.VMEM((length, d), BF), pltpu.VMEM((length, hidden), BF)]
        + [pltpu.VMEM((length, hidden), BF), pltpu.VMEM((length, d), BF)]
        + [vm(4, rows, d), vm(d, hidden), vm(hidden, d), vm(2, rows, d), vm(2, rows, d)]
        + [vm(length, d), vm(length, 1, dtype=F32), sem(10), sem(4)],
        LIMIT_B,
        12 * length * d * hidden,
        (0, 1, 2, 3, 6, 7, 8, 9, 13, 15),
        (0, 1, 4, 5),
    )


def run_c(seq, heads, length, rows, d, clips, meta, lens, arrays):
    sd = jax.ShapeDtypeStruct
    wide, attn = 3 * heads * HEAD_DIM, heads * HEAD_DIM
    k_rows = length - pad_range(clips, length)[0]
    return call(
        functools.partial(stage_c, seq, heads, length, rows),
        [sd((rows, d), F32), sd((length, d), BF), sd((length, wide), BF), sd((8, d), F32)],
        [meta, lens],
        arrays,
        [vm(length, attn), vm(2 * heads, k_rows, HEAD_DIM, dtype=F32), vm(heads, k_rows, HEAD_DIM)]
        + [vm(4, rows, d), vm(length, d), vm(length, 1, dtype=F32), vm(attn, d)]
        + [vm(length, wide), vm(rows, d, dtype=F32), sem(14), sem(1)],
        LIMIT_C,
        4 * length * d * attn * 2,
        (2, 3, 4, 5, 6, 7, 9, 10),
        (0,),
    )


def run_grads(first_seq, last_seq, rows, blocks, wide, meta, arrays):
    sd = jax.ShapeDtypeStruct
    length, d = arrays[0].shape
    attn = d - wide
    each = d // blocks
    return call(
        functools.partial(stage_grads, first_seq, last_seq, rows, blocks),
        [sd((2, rows, d), BF), sd((2, rows, d), BF)]
        + (
            [sd((blocks, each + VEC_ROWS, d), BF)]
            if last_seq
            else [sd((wide, d), F32), sd((attn, d), F32), sd((8, d), F32)]
        ),
        [meta],
        arrays,
        [vm(length, d), vm(length, attn), vm(wide, d), sem(3)],
        LIMIT_A,
        4 * length * d * d,
        (3, 4, 5),
        (),
    )


def stage_d(seq, meta, x, mg, keep, got, far, g1, out):
    xhat, inv = norm_rows(x[seq].astype(F32))
    slot = meta[0] >> 1
    n = keep[slot].astype(F32) + got[slot].astype(F32) + far[...].astype(F32)
    e = n * g1[...]
    mean_e = jnp.mean(e, axis=-1, keepdims=True)
    mean_ex = jnp.mean(e * xhat, axis=-1, keepdims=True)
    out[...] = (mg[...] + inv * (e - mean_e - xhat * mean_ex)).astype(BF)


def unpack_ff(each, d, near, far, meta, up_o, down_o):
    for j in range(8):
        at = lax.bitwise_xor(meta[1], jnp.int32(j))
        rows = slice(j * each, j * each + each)

        @pl.when(at < 4)
        def _():
            block = near[jnp.minimum(at, 3)].astype(F32)
            up_o[rows, :] = block[:each]
            down_o[rows, :] = block[each:]

        @pl.when(at >= 4)
        def _():
            block = far[jnp.maximum(at - 4, 0)].astype(F32)
            up_o[rows, :] = block[:each]
            down_o[rows, :] = block[each:]


def unpack_attn(each, wide, near, far, meta, qkv_o, out_o, vec_o):
    for j in range(8):
        at = lax.bitwise_xor(meta[1], jnp.int32(j))
        r = j * each

        def put(block):
            if r < wide:
                qkv_o[r : r + each, :] = block[:each]
            else:
                out_o[r - wide : r - wide + each, :] = block[:each]
            vec_o[j : j + 1, :] = block[each : each + 1, :]

        @pl.when(at < 4)
        def _():
            put(near[jnp.minimum(at, 3)].astype(F32))

        @pl.when(at >= 4)
        def _():
            put(far[jnp.maximum(at - 4, 0)].astype(F32))


def on_device(
    tokens,
    clip_lengths,
    cotangent,
    query_key_value_weight,
    qv_bias,
    output_weight,
    out_bias,
    gain1,
    shift1,
    gain2,
    shift2,
    up_weight,
    hidden_bias,
    down_weight,
    down_bias,
):
    n_dp = lax.axis_size("dp")
    n_tensor = lax.axis_size("tensor")
    seqs, rows, d = tokens.shape
    length = rows * n_tensor
    heads = output_weight.shape[0] // HEAD_DIM
    wide = 3 * HEAD_DIM * heads
    hidden = up_weight.shape[1]
    blocks = 8
    each = d // blocks

    def core_swap(v):
        return lax.ppermute(v, "tensor", [(t, t ^ 1) for t in range(n_tensor)])

    def chip_swap(v):
        return lax.ppermute(v, "tensor", [(t, t ^ 2) for t in range(n_tensor)])

    t = lax.axis_index("tensor")
    dp_at = lax.axis_index("dp")
    orders = ((0, 1, 2), (1, 0, 2))
    if n_dp == 8:

        def place(order):
            return sum(((dp_at >> order[k]) & 1) << (2 - k) for k in range(3))

        label = jnp.where(t % 2 == 0, place(orders[0]), place(orders[1]))
    else:
        label = jnp.zeros_like(dp_at)
    meta = jnp.stack([t, label]).astype(jnp.int32)

    def add(a, b):
        return (a.astype(F32) + b.astype(F32)).astype(BF)

    def after(value, *others):
        return lax.optimization_barrier((value, others))[0]

    def step_perm(k):
        pairs = []
        for dev in range(n_dp):
            for s in range(n_tensor):
                other = dev ^ (1 << orders[s % 2][k])
                pairs.append((dev * n_tensor + s, other * n_tensor + s))
        return pairs

    def reduce_get(held, k):
        return lax.ppermute(held[held.shape[0] // 2 :], ("dp", "tensor"), step_perm(k))

    def gather_step(held, k):
        return lax.ppermute(held, ("dp", "tensor"), step_perm(k))

    def after(value, *others):
        return lax.optimization_barrier((value, others))[0]

    def step_perm(k):
        pairs = []
        for dev in range(n_dp):
            for s in range(n_tensor):
                other = dev ^ (1 << orders[s % 2][k])
                pairs.append((dev * n_tensor + s, other * n_tensor + s))
        return pairs

    def reduce_get(held, k):
        return lax.ppermute(held[held.shape[0] // 2 :], ("dp", "tensor"), step_perm(k))

    def reduce_step(held, k):
        return add(held[: held.shape[0] // 2], reduce_get(held, k))

    def gather_step(held, k):
        return lax.ppermute(held, ("dp", "tensor"), step_perm(k))

    def gather_all(held):
        for k in (2, 1):
            held = jnp.concatenate([held, gather_step(held, k)], axis=0)
        return held, gather_step(held, 0)

    def after(value, *others):
        return lax.optimization_barrier((value, others))[0]

    def step_perm(k):
        pairs = []
        for dev in range(n_dp):
            for s in range(n_tensor):
                other = dev ^ (1 << orders[s % 2][k])
                pairs.append((dev * n_tensor + s, other * n_tensor + s))
        return pairs

    def all_reduce(buf):
        if n_dp != 8:
            full = lax.psum(buf, "dp")
            return full[:4], full[4:]
        held = buf
        for k in range(3):
            half = held.shape[0] // 2
            got = lax.ppermute(held[half:], ("dp", "tensor"), step_perm(k))
            held = add(held[:half], got)
        for k in (2, 1):
            got = lax.ppermute(held, ("dp", "tensor"), step_perm(k))
            held = jnp.concatenate([held, got], axis=0)
        return held, lax.ppermute(held, ("dp", "tensor"), step_perm(0))

    def row(v):
        return v.reshape(1, -1)

    pairs = qv_bias.reshape(heads, 2, HEAD_DIM)
    bias = row(jnp.stack([pairs[:, 0], jnp.zeros_like(pairs[:, 0]), pairs[:, 1]], axis=1))
    g1, b1, g2, b2 = row(gain1), row(shift1), row(gain2), row(shift2)
    ob, hb = row(out_bias), row(hidden_bias)
    chip_at = t >> 1

    w_t = query_key_value_weight.T

    def spread(v, *first):
        near = core_swap(v)
        across = after(chip_swap(v), *first)
        return [v, near, across, core_swap(across)]

    def chip_sum(keep, send):
        return add(keep, core_swap(send))

    def all_rows(chip, far):
        own = add(chip, far)
        return [own, core_swap(own)]

    def peer_rows(keep, got):
        return add(keep[1 - chip_at], got[1 - chip_at])

    xs = spread(tokens, g1, b1, g2, b2, ob, hb, bias, meta)
    cot_near = core_swap(cotangent)
    beside = chip_swap(cotangent)

    kept, chips, fars = [], [], []
    for s in range(seqs):
        outs = run_a(
            s, heads, length, rows, d, meta, clip_lengths, after(xs, *chips[-1:]), g1, b1,
            w_t, bias, output_weight,
        )
        kept.append(outs[:3])
        if s == 0:
            beside = after(beside, outs[3])
            cots = [cotangent, cot_near, beside, core_swap(beside)]
        chips.append(chip_sum(outs[3], after(outs[4], beside)))
        beside = chip_swap(chips[s])
        fars.append(beside)

    mids, stats, ff_keep, ff_send, n_chips, n_fars = [], [], [], [], [], []
    carry = []
    for s in range(seqs):
        mids.append(all_rows(chips[s], fars[s]))
        outs = run_b(
            s, s == 0, s == seqs - 1, rows, d, hidden, blocks, meta, xs,
            after(mids[s], *(chips[-1:] + n_chips[-1:])), cots,
            ob, g2, b2, up_weight, hb, down_weight, carry,
        )
        n_chips.append(chip_sum(outs[2], after(outs[3], beside)))
        beside = chip_swap(n_chips[s])
        n_fars.append(beside)
        ff_keep.append(outs[0])
        ff_send.append(outs[1])
        stats.append(outs[4:6])
        carry = outs[6:]
    ff_grads, vec_b = carry

    moves = [("halve", 0), ("halve", 1), ("halve", 2), ("double", 2), ("double", 1)]

    def send_move(held):
        kind, k = moves[0]
        return reduce_get(held, k) if kind == "halve" else gather_step(held, k)

    def take_move(held, part):
        if moves.pop(0)[0] == "halve":
            return add(held[: held.shape[0] // 2], part)
        return jnp.concatenate([held, part], axis=0)

    by_hand = n_dp == 8 and seqs == 2
    backs, peers, far_rows = [], [], []
    carry = []
    held = ff_grads
    for s in range(seqs):
        last = s == seqs - 1
        far_now = after(n_fars[s], *[b[1] for b in backs[-1:]])
        n_now = after(all_rows(n_chips[s], far_now), *n_chips[-1:], held)
        mg, ag, dq, vec_a = run_c(
            s, heads, length, rows, d, clip_lengths.shape[1], meta, clip_lengths,
            [*n_now, *cots, *stats[s], g2, output_weight, kept[s][1]],
        )
        if by_hand:
            held = take_move(held, after(send_move(held), dq))
            dq = after(dq, held)
        outs = run_grads(
            s == 0, last, rows, blocks, wide, meta,
            [ag, dq, vec_a, kept[s][0], kept[s][2], w_t, g1, b1, *carry] + ([vec_b] if last else []),
        )
        keep, send = outs[:2]
        carry = outs[2:]
        waits = [] if last else [beside]
        if by_hand and last:
            part = send_move(held)
        elif by_hand:
            held = take_move(held, after(send_move(held), send))
        got = core_swap(after(send, *waits))
        peers.append(peer_rows(keep, got))
        beside = chip_swap(peers[s])
        far_rows.append(beside)
        backs.append((mg, keep, got))
    at_grads = carry[0]
    ff_got = [core_swap(after(send, vec_a)) for send in ff_send]
    ff_peers = [peer_rows(keep, got) for keep, got in zip(ff_keep, ff_got)]
    ff_far_rows = [chip_swap(v) for v in ff_peers]
    whole = pl.BlockSpec(memory_space=pltpu.VMEM)

    def input_rows(s):
        return pl.pallas_call(
            functools.partial(stage_d, s),
            out_shape=jax.ShapeDtypeStruct((rows, d), BF),
            in_specs=[pl.BlockSpec(memory_space=pltpu.SMEM)] + [whole] * 6,
            out_specs=whole,
            compiler_params=pltpu.CompilerParams(vmem_limit_bytes=16 << 20),
        )(meta, tokens, *backs[s], far_rows[s], g1)

    def output_rows(s):
        ff = ff_keep[s][chip_at].astype(F32) + ff_got[s][chip_at].astype(F32)
        middle = tokens[s].astype(F32) + mids[s][0][chip_at].astype(F32) + out_bias
        return (middle + (ff + ff_far_rows[s].astype(F32) + down_bias)).astype(BF)

    input_grad = jnp.stack([input_rows(s) for s in range(seqs)])
    block_out = jnp.stack([output_rows(s) for s in range(seqs)])
    if by_hand:
        at_held = add(at_grads[:4], after(reduce_get(at_grads, 0), *ff_peers))
        held = take_move(held, after(part, at_held))
        part = send_move(held)
        at_held = add(at_held[:2], reduce_get(at_held, 1))
        at_held = add(at_held[:1], reduce_get(at_held, 2))
        ff_near = take_move(held, after(part, at_held, input_grad))
        ff_far = gather_step(ff_near, 0)
        at_held = jnp.concatenate([at_held, gather_step(at_held, 2)], axis=0)
        part = after(gather_step(at_held, 1), block_out)
        at_near = jnp.concatenate([at_held, part], axis=0)
        at_far = gather_step(at_near, 0)
    else:
        ff_sum, at_sum = lax.psum((ff_grads, at_grads), "dp")
        ff_near, ff_far, at_near, at_far = ff_sum[:4], ff_sum[4:], at_sum[:4], at_sum[4:]

    def unpack(body, near, far, out_shape):
        whole = pl.BlockSpec(memory_space=pltpu.VMEM)
        return pl.pallas_call(
            body,
            out_shape=out_shape,
            in_specs=[whole, whole, pl.BlockSpec(memory_space=pltpu.SMEM)],
            out_specs=[whole] * len(out_shape),
            compiler_params=pltpu.CompilerParams(vmem_limit_bytes=24 << 20),
        )(near, far, meta)

    grad_up, grad_down = unpack(
        functools.partial(unpack_ff, each, d),
        ff_near,
        ff_far,
        [jax.ShapeDtypeStruct((d, hidden), F32), jax.ShapeDtypeStruct((hidden, d), F32)],
    )
    at_far = after(at_far, block_out, input_grad, grad_up, grad_down)

    def vec_row(j):
        at = label ^ j
        return jnp.where(at < 4, at_near[at & 3, each], at_far[at & 3, each]).astype(F32)

    norm1 = jnp.stack([vec_row(V_GAIN1), vec_row(V_SHIFT1)])
    across = lax.ppermute(norm1, "tensor", [(t, t ^ 3) for t in range(n_tensor)])
    near = core_swap(norm1)
    at_near = after(at_near, near)
    norm1 = (norm1 + near) + (chip_swap(norm1) + across)
    grad_qkv, grad_out, vec = unpack(
        functools.partial(unpack_attn, each, wide),
        at_near,
        at_far,
        [
            jax.ShapeDtypeStruct((wide, d), F32),
            jax.ShapeDtypeStruct((d - wide, d), F32),
            jax.ShapeDtypeStruct((8, d), F32),
        ],
    )
    qkv_sum = vec[V_QKV, :wide].reshape(heads, 3, HEAD_DIM)
    return (
        block_out,
        input_grad,
        grad_qkv.T,
        qkv_sum[:, ::2].reshape(-1),
        grad_out,
        vec[V_OUT],
        norm1[0],
        norm1[1],
        vec[V_GAIN2],
        vec[V_SHIFT2],
        grad_up,
        vec[V_UP],
        grad_down,
        vec[V_DOWN],
    )


def solution(mesh):
    placed = (
        P("dp", "tensor", None),
        P("dp", None),
        P("dp", "tensor", None),
        P(None, "tensor"),
        P("tensor"),
        P("tensor", None),
        P(),
        P(),
        P(),
        P(),
        P(),
        P(None, "tensor"),
        P("tensor"),
        P("tensor", None),
        P(),
    )
    return jax.shard_map(
        on_device,
        mesh=mesh,
        in_specs=placed,
        out_specs=(
            P("dp", "tensor", None),
            P("dp", "tensor", None),
            P(None, "tensor"),
            P("tensor"),
            P("tensor", None),
            P(),
            P(),
            P(),
            P(),
            P(),
            P(None, "tensor"),
            P("tensor"),
            P("tensor", None),
            P(),
        ),
        check_vma=False,
    )
```
